32 devices in a mesh: fsdp: 8 (over z, core), mp: 4 (over y, x).
Axes of the slice: x: 2, y: 2, z: 4, core: 2. Of those that a mesh axis runs over, the one named last changes fastest.
Arguments:
- inputs: bfloat16 [2, 16384, 1024], P(None, ('fsdp', 'mp')), may hold values from -6 to 6
- lengths: int32 [2, 32], P(None, 'fsdp'), may hold values from 128 to 512, as said below
- qkv_weight: bfloat16 [1024, 3072], P('fsdp', 'mp'), may hold values from -0.1875 to 0.1875
- qv_bias: bfloat16 [2048], P(('mp', 'fsdp')), may hold values from -3 to 3
- out_weight: bfloat16 [1024, 1024], P('mp', 'fsdp'), may hold values from -1.5 to 1.5
- out_bias: bfloat16 [1024], P('fsdp'), may hold values from -3 to 3
- norm1_gain: bfloat16 [1024], P('fsdp'), may hold values from 0.099609375 to 1.8984375
- norm1_bias: bfloat16 [1024], P('fsdp'), may hold values from -3 to 3
- up_weight: bfloat16 [1024, 4096], P('fsdp', 'mp'), may hold values from -0.1875 to 0.1875
- up_bias: bfloat16 [4096], P('fsdp'), may hold values from -3 to 3
- down_weight: bfloat16 [4096, 1024], P('mp', 'fsdp'), may hold values from -0.09375 to 0.09375
- down_bias: bfloat16 [1024], P('fsdp'), may hold values from -3 to 3
- norm2_gain: bfloat16 [1024], P('fsdp'), may hold values from 0.099609375 to 1.8984375
- norm2_bias: bfloat16 [1024], P('fsdp'), may hold values from -3 to 3
- cotangent: bfloat16 [2, 16384, 1024], P(None, ('fsdp', 'mp')), may hold values from -6 to 6
Outputs:
- layer_output: bfloat16 [2, 16384, 1024], P(None, ('fsdp', 'mp'))
- input_grad: float32 [2, 16384, 1024], P(None, ('fsdp', 'mp'))
- qkv_weight_grad: float32 [1024, 3072], P('fsdp', 'mp')
- qv_bias_grad: float32 [2048], P(('mp', 'fsdp'))
- out_weight_grad: float32 [1024, 1024], P('mp', 'fsdp')
- out_bias_grad: float32 [1024], P('fsdp')
- norm1_gain_grad: float32 [1024], P('fsdp')
- norm1_bias_grad: float32 [1024], P('fsdp')
- up_weight_grad: float32 [1024, 4096], P('fsdp', 'mp')
- up_bias_grad: float32 [4096], P('fsdp')
- down_weight_grad: float32 [4096, 1024], P('mp', 'fsdp')
- down_bias_grad: float32 [1024], P('fsdp')
- norm2_gain_grad: float32 [1024], P('fsdp')
- norm2_bias_grad: float32 [1024], P('fsdp')
The draws below stay inside these ranges and needn't reach their ends.
Inputs may be any that keep to these rules, and one draw needn't show every extreme that they name: `lengths`: in every micro-batch one sequence has exactly 512 live tokens and another exactly 128.
All inputs are finite; a program needn't handle non-finite values.
Results may differ from the reference program's by a relative error of at most 0.022.
Values may be sent and summed in bfloat16 or wider, within the bound.
A program may use at most 448 MiB of HBM per device.

```python
import math
import jax
import jax.numpy as jnp
from jax import lax

D = 1024
HEADS = 16
DH = 64
FF = 4096
L = 512
MBS = 2
SEQ_ALL = 32
TOK_MB = 16384
MIN_LEN = 128


def draw_lengths(key, part):
    first_key, second_key, third_key = jax.random.split(key, 3)
    values = jax.random.randint(first_key, (MBS, SEQ_ALL), MIN_LEN, L + 1)
    top_at = jax.random.randint(second_key, (MBS, 1), 0, SEQ_ALL)
    low_at = (top_at + 1 + jax.random.randint(third_key, (MBS, 1), 0, SEQ_ALL - 1)) % SEQ_ALL
    column = jnp.arange(SEQ_ALL)[None, :]
    values = jnp.where(column == top_at, L, values)
    values = jnp.where(column == low_at, MIN_LEN, values)
    return values.astype(jnp.int32)


def shard_levels(rng, extent, pieces, least, largest):
    level = 1.0
    for position, blocks in pieces:
        heights = jax.random.uniform(jax.random.fold_in(jax.random.fold_in(rng, 6), position), (blocks,), jnp.float32, least / len(pieces), largest / len(pieces))
        level = level * jnp.repeat(jnp.exp(heights), extent[position] // blocks).reshape((-1,) + (1,) * (len(extent) - 1 - position))
    return level


def noise(stream_key, shape, scale, bound, shards=(), kind=jnp.bfloat16):
    drawn = scale * jax.random.normal(stream_key, shape, jnp.float32)
    if shards:
        drawn = drawn * shard_levels(stream_key, shape, shards, -0.22, 0.18)
    return jnp.clip(drawn, -bound, bound).astype(kind)


def setup_inputs(seed: int = 0) -> dict:
    keys = jax.random.split(jax.random.key(seed), 16)
    return {
        "inputs": noise(keys[0], (MBS, TOK_MB, D), 1.0, 6.0, ((1, 32),)),
        "lengths": draw_lengths(jax.random.fold_in(keys[15], 71), 0),
        "qkv_weight": noise(keys[2], (D, 3 * D), D ** -0.5, 0.1875, ((0, 8), (1, 4))),
        "qv_bias": noise(keys[3], (2 * D,), 0.5, 3.0, ((0, 32),)),
        "out_weight": noise(keys[4], (D, D), (D // 64) ** -0.5, 1.5, ((0, 4), (1, 8))),
        "out_bias": noise(keys[5], (D,), 0.5, 3.0, ((0, 8),)),
        "norm1_gain": jnp.clip(1.0 + 0.18 * jax.random.normal(keys[6], (D,), jnp.float32), 0.099609375, 1.8984375).astype(jnp.bfloat16),
        "norm1_bias": noise(keys[7], (D,), 0.5, 3.0, ((0, 8),)),
        "up_weight": noise(keys[8], (D, FF), D ** -0.5, 0.1875, ((0, 8), (1, 4))),
        "up_bias": noise(keys[9], (FF,), 0.5, 3.0, ((0, 8),)),
        "down_weight": noise(keys[10], (FF, D), FF ** -0.5, 0.09375, ((0, 4), (1, 8))),
        "down_bias": noise(keys[11], (D,), 0.5, 3.0, ((0, 8),)),
        "norm2_gain": jnp.clip(1.0 + 0.18 * jax.random.normal(keys[12], (D,), jnp.float32), 0.099609375, 1.8984375).astype(jnp.bfloat16),
        "norm2_bias": noise(keys[13], (D,), 0.5, 3.0, ((0, 8),)),
        "cotangent": noise(keys[14], (MBS, TOK_MB, D), 1.0, 6.0, ((1, 32),)),
    }


PRECISE = lax.Precision.HIGHEST
EPSILON = 1e-06

@jax.custom_vjp
def low(v):
    return lax.optimization_barrier(v.astype(jnp.bfloat16)).astype(jnp.float32)

@jax.custom_vjp
def low_back(v):
    return v

def low_keep(v):
    return (low(v), None)

def low_pass(kept, grad):
    return (grad,)

def back_keep(v):
    return (v, None)

def back_low(kept, grad):
    return (low(grad),)
low.defvjp(low_keep, low_pass)
low_back.defvjp(back_keep, back_low)

def normalize(values, scale_vec, shift_vec):
    row_mean = lax.optimization_barrier(jnp.mean(values, axis=-1, keepdims=True))
    centered = values - row_mean
    spread = lax.optimization_barrier(jnp.mean(centered * centered, axis=-1, keepdims=True))
    return centered * lax.rsqrt(spread + EPSILON) * scale_vec + shift_vec

def gelu_exact(values):
    return jax.nn.gelu(values, approximate=False)

def block_forward(params, packed):
    tokens, seq_lens = packed
    qkv_weight, qv_bias, out_weight, out_bias, norm1_gain, norm1_bias, up_weight, up_bias, down_weight, down_bias, norm2_gain, norm2_bias = params
    seq_count = tokens.shape[0]
    project = jnp.einsum('bld,dc->blc', tokens, qkv_weight, precision=PRECISE)
    project = project.reshape(seq_count, L, HEADS, 3, DH)
    paired = qv_bias.reshape(HEADS, 2, DH)
    bias_full = jnp.stack([paired[:, 0], jnp.zeros_like(paired[:, 0]), paired[:, 1]], axis=1)
    project = low_back(low(project + bias_full))
    queries = project[:, :, :, 0]
    keysets = project[:, :, :, 1]
    values = project[:, :, :, 2]
    scores = jnp.einsum('bqhe,bkhe->bhqk', queries, keysets, precision=PRECISE) * DH ** (-0.5)
    scores = low_back(scores)
    live_mask = jnp.arange(L)[None, None, None, :] < seq_lens[:, None, None, None]
    scores = jnp.where(live_mask, scores, -1000000000.0)
    attn_probs = jax.nn.softmax(scores, axis=-1)
    mixed_heads = jnp.einsum('bhqk,bkhe->bqhe', low(attn_probs), values, precision=PRECISE)
    mixed_heads = low_back(low(mixed_heads.reshape(seq_count, L, D)))
    attended = low_back(jnp.einsum('bld,dc->blc', mixed_heads, out_weight, precision=PRECISE))
    hidden = normalize(attended + out_bias + tokens, norm1_gain, norm1_bias)
    inner_sum = jnp.einsum('bld,df->blf', low(hidden), up_weight, precision=PRECISE) + up_bias
    inner_sum = low_back(inner_sum)
    branch = jnp.einsum('blf,fd->bld', low(gelu_exact(inner_sum)), down_weight, precision=PRECISE)
    branch = low_back(branch)
    return normalize(branch + down_bias + hidden, norm2_gain, norm2_bias)

def reference(inputs, lengths, qkv_weight, qv_bias, out_weight, out_bias, norm1_gain, norm1_bias, up_weight, up_bias, down_weight, down_bias, norm2_gain, norm2_bias, cotangent):
    params = tuple((array_in.astype(jnp.float32) for array_in in (qkv_weight, qv_bias, out_weight, out_bias, norm1_gain, norm1_bias, up_weight, up_bias, down_weight, down_bias, norm2_gain, norm2_bias)))
    seq_total = MBS * SEQ_ALL
    group_size = math.gcd(seq_total, 8)
    group_count = seq_total // group_size
    tokens = inputs.astype(jnp.float32).reshape(group_count, group_size, L, D)
    seq_lens = lengths.astype(jnp.int32).reshape(group_count, group_size)

    def whole_layer(token_blocks, weights):
        step_fn = jax.checkpoint(lambda packed: block_forward(weights, packed))
        return lax.map(step_fn, (token_blocks, seq_lens))
    result, pull_back = jax.vjp(whole_layer, tokens, params)
    live_rows = (jnp.arange(L)[None, None, :] < seq_lens[:, :, None]).astype(jnp.float32)
    seed_grad = cotangent.astype(jnp.float32).reshape(group_count, group_size, L, D) * live_rows[..., None]
    token_grad, weight_grads = pull_back(seed_grad)
    whole_shape = (MBS, TOK_MB, D)
    return (result.reshape(whole_shape).astype(jnp.bfloat16), token_grad.reshape(whole_shape), weight_grads[0], weight_grads[1], weight_grads[2], weight_grads[3], weight_grads[4], weight_grads[5], weight_grads[6], weight_grads[7], weight_grads[8], weight_grads[9], weight_grads[10], weight_grads[11])
```

```python
from functools import partial

import jax
import jax.numpy as jnp
from jax import lax
from jax.experimental import pallas as pl
from jax.experimental.pallas import tpu as pltpu
from jax.sharding import PartitionSpec as P

D = 1024
DH = 64
FF = 4096
L = 512
MBS = 2


EPSILON = 1e-06
CONTRACT_ROWS = (((0,), (0,)), ((), ()))
CONTRACT_COLS = (((1,), (1,)), ((), ()))


def normalize(values, scale_vec, shift_vec):
    row_mean = jnp.mean(values, axis=-1, keepdims=True)
    centered = values - row_mean
    spread = jnp.mean(centered * centered, axis=-1, keepdims=True)
    return centered * lax.rsqrt(spread + EPSILON) * scale_vec + shift_vec


def gelu_exact(values):
    return jax.nn.gelu(values, approximate=False)


def collect_forward(shards):
    return (
        lax.all_gather(shards[0], "fsdp", axis=0, tiled=True),
        lax.all_gather(shards[1], "fsdp", axis=0, tiled=True),
        lax.all_gather(shards[2], "fsdp", axis=1, tiled=True),
        lax.all_gather(shards[3], "fsdp", axis=0, tiled=True),
        lax.all_gather(shards[4], "fsdp", axis=0, tiled=True),
        lax.all_gather(shards[5], "fsdp", axis=0, tiled=True),
        lax.all_gather(shards[6], "fsdp", axis=0, tiled=True),
        lax.all_gather(shards[7], "fsdp", axis=0, tiled=True),
        lax.all_gather(shards[8], "fsdp", axis=1, tiled=True),
        lax.all_gather(shards[9], "fsdp", axis=0, tiled=True),
        lax.all_gather(shards[10], "fsdp", axis=0, tiled=True),
        lax.all_gather(shards[11], "fsdp", axis=0, tiled=True),
    )


def collect_backward(shards):
    return (
        lax.all_gather(shards[0], "fsdp", axis=0, tiled=True),
        lax.all_gather(shards[2], "fsdp", axis=1, tiled=True),
        lax.all_gather(shards[4], "fsdp", axis=0, tiled=True),
        lax.all_gather(shards[6], "fsdp", axis=0, tiled=True),
        lax.all_gather(shards[8], "fsdp", axis=1, tiled=True),
        lax.all_gather(shards[10], "fsdp", axis=0, tiled=True),
    )


def attend_forward(packed, scale_value):
    queries, keysets, values, seq_len = packed
    scores = (
        jnp.einsum("qhe,khe->hqk", queries, keysets, preferred_element_type=jnp.float32)
        * scale_value
    )
    live_mask = jnp.arange(scores.shape[-1])[None, None, :] < seq_len
    scores = jnp.where(live_mask, scores, -1000000000.0)
    row_max = jnp.max(scores, axis=-1, keepdims=True)
    exp_scores = jnp.exp(scores - row_max)
    denom_sum = jnp.sum(exp_scores, axis=-1, keepdims=True)
    attn_probs = (exp_scores / denom_sum).astype(jnp.bfloat16)
    mixed_heads = jnp.einsum("hqk,khe->qhe", attn_probs, values, preferred_element_type=jnp.float32)
    return (mixed_heads.astype(jnp.bfloat16), (row_max + jnp.log(denom_sum))[:, :, 0])


def attend_backward(packed, scale_value):
    queries, keysets, values, seq_len, log_sums, d_mixed = packed
    scores = (
        jnp.einsum("qhe,khe->hqk", queries, keysets, preferred_element_type=jnp.float32)
        * scale_value
    )
    live_mask = jnp.arange(scores.shape[-1])[None, None, :] < seq_len
    attn_probs = jnp.where(live_mask, jnp.exp(scores - log_sums[:, :, None]), 0.0)
    low_probs = attn_probs.astype(jnp.bfloat16)
    d_value = jnp.einsum("hqk,qhe->khe", low_probs, d_mixed, preferred_element_type=jnp.float32)
    d_probs = jnp.einsum("qhe,khe->hqk", d_mixed, values, preferred_element_type=jnp.float32)
    row_delta = jnp.sum(attn_probs * d_probs, axis=-1, keepdims=True)
    d_scores = (attn_probs * (d_probs - row_delta)).astype(jnp.bfloat16)
    d_query = (
        jnp.einsum("hqk,khe->qhe", d_scores, keysets, preferred_element_type=jnp.float32)
        * scale_value
    )
    d_key = (
        jnp.einsum("hqk,qhe->khe", d_scores, queries, preferred_element_type=jnp.float32)
        * scale_value
    )
    return jnp.stack([d_query, d_key, d_value], axis=2).astype(jnp.bfloat16)


def generic_body(
    inputs,
    lengths,
    qkv_weight,
    qv_bias,
    out_weight,
    out_bias,
    norm1_gain,
    norm1_bias,
    up_weight,
    up_bias,
    down_weight,
    down_bias,
    norm2_gain,
    norm2_bias,
    cotangent,
):
    shards = (
        qkv_weight,
        qv_bias,
        out_weight,
        out_bias,
        norm1_gain,
        norm1_bias,
        up_weight,
        up_bias,
        down_weight,
        down_bias,
        norm2_gain,
        norm2_bias,
    )
    row_count = inputs.shape[1]
    mp_count = lax.axis_size("mp")
    mp_index = lax.axis_index("mp")
    up_cols = up_weight.shape[1]
    scale_value = DH ** (-0.5)
    group_rows = row_count * mp_count
    head_count = qkv_weight.shape[1] // (3 * DH)
    row_ids = mp_index * row_count + jnp.arange(row_count)
    seq_count = group_rows // L
    head_width = head_count * DH
    seq_ids = row_ids // L
    positions = row_ids % L
    seq_match = seq_ids[:, None] == jnp.arange(seq_count)[None, :]
    grad_qkv = jnp.zeros((D, 3 * head_width), jnp.float32)
    grad_qvb = jnp.zeros((2 * head_width,), jnp.float32)
    grad_out = jnp.zeros((head_width, D), jnp.float32)
    grad_up = jnp.zeros((D, up_cols), jnp.float32)
    grad_down = jnp.zeros((up_cols, D), jnp.float32)
    grad_upb = jnp.zeros((FF,), jnp.float32)
    grad_outb = jnp.zeros((D,), jnp.float32)
    grad_gain1 = jnp.zeros((D,), jnp.float32)
    grad_shift1 = jnp.zeros((D,), jnp.float32)
    grad_downb = jnp.zeros((D,), jnp.float32)
    grad_gain2 = jnp.zeros((D,), jnp.float32)
    grad_shift2 = jnp.zeros((D,), jnp.float32)
    layer_rows = []
    input_rows = []
    for micro_idx in range(MBS):
        fwd_set = collect_forward(shards)
        qkv_full, qvb_full, out_full, outb_full = (fwd_set[0], fwd_set[1], fwd_set[2], fwd_set[3])
        gain_one = fwd_set[4].astype(jnp.float32)
        shift_one = fwd_set[5].astype(jnp.float32)
        up_full, upb_full, down_full = (fwd_set[6], fwd_set[7].astype(jnp.float32), fwd_set[8])
        downb_full = fwd_set[9].astype(jnp.float32)
        gain_two = fwd_set[10].astype(jnp.float32)
        shift_two = fwd_set[11].astype(jnp.float32)
        tokens = inputs[micro_idx]
        upb_used = lax.dynamic_slice_in_dim(upb_full, mp_index * up_cols, up_cols, 0)
        gathered = lax.all_gather(tokens, "mp", axis=0, tiled=True)
        seq_lens = lengths[micro_idx]
        pair_bias = qvb_full.astype(jnp.float32).reshape(head_count, 2, DH)
        bias_full = jnp.stack(
            [pair_bias[:, 0], jnp.zeros_like(pair_bias[:, 0]), pair_bias[:, 1]], axis=1
        )
        project = jnp.dot(
            gathered, qkv_full, preferred_element_type=jnp.float32
        ) + bias_full.reshape(3 * head_width)
        project = project.astype(jnp.bfloat16).reshape(seq_count, L, head_count, 3, DH)
        queries = project[:, :, :, 0]
        keysets = project[:, :, :, 1]
        values = project[:, :, :, 2]
        mixed_heads, log_sums = lax.map(
            partial(attend_forward, scale_value=scale_value), (queries, keysets, values, seq_lens)
        )
        mixed_flat = mixed_heads.reshape(group_rows, head_width)
        attn_own = lax.psum_scatter(
            jnp.dot(mixed_flat, out_full, preferred_element_type=jnp.float32).astype(jnp.bfloat16),
            "mp",
            scatter_dimension=0,
            tiled=True,
        ).astype(jnp.float32)
        pre_norm1 = attn_own + outb_full.astype(jnp.float32) + tokens.astype(jnp.float32)
        hidden = normalize(pre_norm1, gain_one, shift_one)
        low_hidden = hidden.astype(jnp.bfloat16)
        ffn_rows = lax.all_gather(low_hidden, "mp", axis=0, tiled=True)
        inner_sum = jnp.dot(ffn_rows, up_full, preferred_element_type=jnp.float32) + upb_used
        activated = gelu_exact(inner_sum).astype(jnp.bfloat16)
        branch = lax.psum_scatter(
            jnp.dot(activated, down_full, preferred_element_type=jnp.float32).astype(jnp.bfloat16),
            "mp",
            scatter_dimension=0,
            tiled=True,
        ).astype(jnp.float32)
        pre_norm2 = branch + downb_full + hidden
        layer_rows.append(normalize(pre_norm2, gain_two, shift_two).astype(jnp.bfloat16))
        bwd_set = collect_backward(shards)
        qkv_back, out_back = (bwd_set[0], bwd_set[1])
        gain_one_back = bwd_set[2].astype(jnp.float32)
        up_back, down_back = (bwd_set[3], bwd_set[4])
        gain_two_back = bwd_set[5].astype(jnp.float32)
        row_len = jnp.sum(jnp.where(seq_match, seq_lens[None, :], 0), axis=1)
        live_rows = (positions < row_len).astype(jnp.float32)
        grad_rows = cotangent[micro_idx].astype(jnp.float32) * live_rows[:, None]
        _, pull_two = jax.vjp(normalize, pre_norm2, gain_two_back, shift_two)
        d_pre2, d_gain2, d_shift2 = pull_two(grad_rows)
        grad_gain2 = grad_gain2 + d_gain2
        grad_shift2 = grad_shift2 + d_shift2
        grad_downb = grad_downb + jnp.sum(d_pre2, axis=0)
        d_branch = d_pre2.astype(jnp.bfloat16)
        d_rows = lax.all_gather(d_branch, "mp", axis=0, tiled=True)
        d_act = lax.dot_general(
            d_rows, down_back, CONTRACT_COLS, preferred_element_type=jnp.float32
        )
        grad_down = grad_down + lax.dot_general(
            activated, d_rows, CONTRACT_ROWS, preferred_element_type=jnp.float32
        )
        _, pull_gelu = jax.vjp(gelu_exact, inner_sum)
        d_inner = pull_gelu(d_act)[0].astype(jnp.bfloat16)
        bias_term = jnp.sum(d_inner.astype(jnp.float32), axis=0)
        grad_up = grad_up + lax.dot_general(
            ffn_rows, d_inner, CONTRACT_ROWS, preferred_element_type=jnp.float32
        )
        grad_upb = grad_upb + lax.dynamic_update_slice_in_dim(
            jnp.zeros((FF,), jnp.float32), bias_term, mp_index * up_cols, 0
        )
        d_hidden_part = lax.psum_scatter(
            lax.dot_general(
                d_inner, up_back, CONTRACT_COLS, preferred_element_type=jnp.float32
            ).astype(jnp.bfloat16),
            "mp",
            scatter_dimension=0,
            tiled=True,
        ).astype(jnp.float32)
        d_hidden = d_pre2 + d_hidden_part
        _, pull_one = jax.vjp(normalize, pre_norm1, gain_one_back, shift_one)
        d_pre1, d_gain1, d_shift1 = pull_one(d_hidden)
        grad_gain1 = grad_gain1 + d_gain1
        grad_shift1 = grad_shift1 + d_shift1
        grad_outb = grad_outb + jnp.sum(d_pre1, axis=0)
        d_attended = d_pre1.astype(jnp.bfloat16)
        d_attn_rows = lax.all_gather(d_attended, "mp", axis=0, tiled=True)
        d_mixed = lax.dot_general(
            d_attn_rows, out_back, CONTRACT_COLS, preferred_element_type=jnp.float32
        )
        d_mixed = d_mixed.astype(jnp.bfloat16)
        grad_out = grad_out + lax.dot_general(
            mixed_flat, d_attn_rows, CONTRACT_ROWS, preferred_element_type=jnp.float32
        )
        d_project = lax.map(
            partial(attend_backward, scale_value=scale_value),
            (
                queries,
                keysets,
                values,
                seq_lens,
                log_sums,
                d_mixed.reshape(seq_count, L, head_count, DH),
            ),
        )
        d_flat = d_project.reshape(group_rows, 3 * head_width)
        grad_qkv = grad_qkv + lax.dot_general(
            gathered, d_flat, CONTRACT_ROWS, preferred_element_type=jnp.float32
        )
        bias_parts = jnp.sum(d_flat.astype(jnp.float32), axis=0).reshape(head_count, 3, DH)
        grad_qvb = grad_qvb + jnp.stack([bias_parts[:, 0], bias_parts[:, 2]], axis=1).reshape(
            2 * head_width
        )
        input_rows.append(
            d_pre1
            + lax.psum_scatter(
                lax.dot_general(
                    d_flat, qkv_back, CONTRACT_COLS, preferred_element_type=jnp.float32
                ).astype(jnp.bfloat16),
                "mp",
                scatter_dimension=0,
                tiled=True,
            ).astype(jnp.float32)
        )
    summed = (
        lax.psum_scatter(
            grad_qkv.astype(jnp.bfloat16), "fsdp", scatter_dimension=0, tiled=True
        ).astype(jnp.float32),
        lax.psum_scatter(
            grad_qvb.astype(jnp.bfloat16), "fsdp", scatter_dimension=0, tiled=True
        ).astype(jnp.float32),
        lax.psum_scatter(
            grad_out.astype(jnp.bfloat16), "fsdp", scatter_dimension=1, tiled=True
        ).astype(jnp.float32),
        lax.psum_scatter(
            grad_outb.astype(jnp.bfloat16), "fsdp", scatter_dimension=0, tiled=True
        ).astype(jnp.float32),
        lax.psum_scatter(
            grad_gain1.astype(jnp.bfloat16), "fsdp", scatter_dimension=0, tiled=True
        ).astype(jnp.float32),
        lax.psum_scatter(
            grad_shift1.astype(jnp.bfloat16), "fsdp", scatter_dimension=0, tiled=True
        ).astype(jnp.float32),
        lax.psum_scatter(
            grad_up.astype(jnp.bfloat16), "fsdp", scatter_dimension=0, tiled=True
        ).astype(jnp.float32),
        lax.psum_scatter(
            grad_upb.astype(jnp.bfloat16), "fsdp", scatter_dimension=0, tiled=True
        ).astype(jnp.float32),
        lax.psum_scatter(
            grad_down.astype(jnp.bfloat16), "fsdp", scatter_dimension=1, tiled=True
        ).astype(jnp.float32),
        lax.psum_scatter(
            grad_downb.astype(jnp.bfloat16), "fsdp", scatter_dimension=0, tiled=True
        ).astype(jnp.float32),
        lax.psum_scatter(
            grad_gain2.astype(jnp.bfloat16), "fsdp", scatter_dimension=0, tiled=True
        ).astype(jnp.float32),
        lax.psum_scatter(
            grad_shift2.astype(jnp.bfloat16), "fsdp", scatter_dimension=0, tiled=True
        ).astype(jnp.float32),
    )
    vectors = lax.psum(
        (summed[3], summed[4], summed[5], summed[7], summed[9], summed[10], summed[11]), "mp"
    )
    return (
        jnp.stack(layer_rows),
        jnp.stack(input_rows),
        summed[0],
        summed[1],
        summed[2],
        vectors[0],
        vectors[1],
        vectors[2],
        summed[6],
        vectors[3],
        summed[8],
        vectors[4],
        vectors[5],
        vectors[6],
    )


MESH_ID = pl.DeviceIdType.MESH
F32 = jnp.float32
BF16 = jnp.bfloat16
PLANES = 4
SIDE = 128
HALF = 512
KINDS = ("rows", "cols", "rows", "cols")
FIRST = (1, 2)
SECOND = (2, 1)


def place():
    f = lax.axis_index("fsdp")
    return f // 2, f % 2, lax.axis_index("mp")


def span(ref, kind, start, size):
    start = pl.multiple_of(start, SIDE)
    if kind == "rows":
        return ref.at[pl.ds(start, size), :]
    return ref.at[:, pl.ds(start, size)]


def remote(src, dst, send, recv, f, m):
    return pltpu.make_async_remote_copy(
        src_ref=src, dst_ref=dst, send_sem=send, recv_sem=recv, device_id=(f, m), device_id_type=MESH_ID
    )


def greet_all():
    z, c, m = place()
    me = (z * 2 + c) * 4 + m
    barrier = pltpu.get_barrier_semaphore()

    def hello(d, carry):
        other = (me + d) % 32
        pl.semaphore_signal(barrier, inc=1, device_id=(other // 4, other % 4), device_id_type=MESH_ID)
        return carry

    lax.fori_loop(1, 32, hello, 0)
    pl.semaphore_wait(barrier, 31)


class Spread:
    def __init__(self, shards, wholes, sems):
        self.shards, self.wholes = shards, wholes
        self.zs, self.zr, self.xs, self.xr, self.ys, self.yr, self.cs, self.cr, self.own = sems
        self.z, self.c, self.m = place()

    def core_span(self, t, k, m, c):
        return span(self.wholes[t].at[k, m], KINDS[t], c * HALF, HALF)

    def z_copy(self, t, k, d):
        z = (self.z + d) % PLANES
        dst = span(self.wholes[t].at[k, self.m], KINDS[t], self.c * HALF + self.z * SIDE, SIDE)
        return remote(
            self.shards[t][k], dst, self.zs.at[t, k, d - 1], self.zr.at[t, k, d - 1], z * 2 + self.c, self.m
        )

    def own_copy(self, t, k):
        dst = span(self.wholes[t].at[k, self.m], KINDS[t], self.c * HALF + self.z * SIDE, SIDE)
        return pltpu.make_async_copy(self.shards[t][k], dst, self.own.at[t, k])

    def x_copy(self, t, k):
        blk = self.core_span(t, k, self.m, self.c)
        return remote(blk, blk, self.xs.at[t, k], self.xr.at[t, k], self.z * 2 + self.c, self.m ^ FIRST[k])

    def y_copy(self, t, k, i):
        blk = self.core_span(t, k, self.m ^ (FIRST[k] if i else 0), self.c)
        return remote(blk, blk, self.ys.at[t, k, i], self.yr.at[t, k, i], self.z * 2 + self.c, self.m ^ SECOND[k])

    def c_copy(self, t, k, i):
        blk = self.core_span(t, k, self.m ^ i, self.c)
        return remote(blk, blk, self.cs.at[t, k, i], self.cr.at[t, k, i], self.z * 2 + 1 - self.c, self.m)

    def start(self, t):
        for k in range(2):
            for d in range(1, PLANES):
                self.z_copy(t, k, d).start()
            self.own_copy(t, k).start()

    def stage(self, t, n):
        for k in range(2):
            if n == 0:
                self.own_copy(t, k).wait()
                for d in range(1, PLANES):
                    self.z_copy(t, k, d).wait_recv()
                self.x_copy(t, k).start()
                self.y_copy(t, k, 0).start()
                self.c_copy(t, k, 0).start()
            elif n == 1:
                self.x_copy(t, k).wait_recv()
                self.y_copy(t, k, 1).start()
                self.c_copy(t, k, FIRST[k]).start()
            elif n == 2:
                self.y_copy(t, k, 0).wait_recv()
                self.c_copy(t, k, SECOND[k]).start()
                self.y_copy(t, k, 1).wait_recv()
                self.c_copy(t, k, 3).start()
            else:
                for i in range(4):
                    self.c_copy(t, k, i).wait_recv()

    def drain(self, t):
        for k in range(2):
            for d in range(1, PLANES):
                self.z_copy(t, k, d).wait_send()
            self.x_copy(t, k).wait_send()
            self.y_copy(t, k, 0).wait_send()
            self.y_copy(t, k, 1).wait_send()
            for i in range(4):
                self.c_copy(t, k, i).wait_send()


def spread_sems():
    dma = pltpu.SemaphoreType.DMA
    return [
        dma((4, 2, 3)), dma((4, 2, 3)), dma((4, 2)), dma((4, 2)), dma((4, 2, 2)), dma((4, 2, 2)),
        dma((4, 2, 4)), dma((4, 2, 4)), dma((4, 2)),
    ]


def swap_vectors(src, dst, send, recv, chunked):
    z, c, m = place()
    f = z * 2 + c
    me = f * 4 + m

    def copy(d):
        other = (me + d) % 32
        fo, mo = other // 4, other % 4
        piece = src.at[mo * 8 + fo] if chunked else src
        return remote(piece, dst.at[m * 8 + f], send.at[d], recv.at[d], fo, mo)

    return copy


def run_31(fn):
    def step(d, carry):
        fn(d)
        return carry

    lax.fori_loop(1, 32, step, 0)


WHOLE = ((2, 4, 1024, 384), (2, 4, 128, 1024), (2, 4, 1024, 512), (2, 4, 512, 1024))


def add_into(dst, src, step=64):
    rows = dst.shape[0]
    step = min(step, rows)

    def body(i, carry):
        r = pl.ds(pl.multiple_of(i * step, step), step)
        dst[r, :] = (dst[r, :].astype(F32) + src[r, :].astype(F32)).astype(BF16)
        return carry

    lax.fori_loop(0, rows // step, body, 0)


class Fold:
    def __init__(self, grads, outs, rc, rx, ry, rz, sems):
        self.grads, self.outs, self.rc, self.rx, self.ry, self.rz = grads, outs, rc, rx, ry, rz
        self.cs, self.cr, self.xs, self.xr, self.ys, self.yr, self.zs, self.zr = sems
        self.z, self.c, self.m = place()

    def c_copy(self, t, k, i):
        m = self.m ^ i
        src = span(self.grads[t].at[k, m], KINDS[t], (1 - self.c) * HALF, HALF)
        return remote(
            src, self.rc[t].at[k, m], self.cs.at[t, k, i], self.cr.at[t, k, i], self.z * 2 + 1 - self.c, self.m
        )

    def x_copy(self, t, k, i):
        m = self.m ^ FIRST[k] ^ (SECOND[k] if i else 0)
        return remote(
            self.rc[t].at[k, m], self.rx[t].at[k, i], self.xs.at[t, k, i], self.xr.at[t, k, i],
            self.z * 2 + self.c, self.m ^ FIRST[k],
        )

    def y_copy(self, t, k):
        m = self.m ^ SECOND[k]
        return remote(
            self.rc[t].at[k, m], self.ry[t].at[k], self.ys.at[t, k], self.yr.at[t, k], self.z * 2 + self.c, m
        )

    def z_copy(self, t, k, d):
        z = (self.z + d) % PLANES
        src = span(self.rc[t].at[k, self.m], KINDS[t], z * SIDE, SIDE)
        return remote(
            src, self.rz[t].at[k, d - 1], self.zs.at[t, k, d - 1], self.zr.at[t, k, d - 1], z * 2 + self.c, self.m
        )

    def stage(self, t, n):
        for k in range(2):
            rc = self.rc[t].at[k]
            if n == 0:
                for i in (3, FIRST[k], SECOND[k], 0):
                    self.c_copy(t, k, i).start()
            elif n == 1:
                for i in (3, FIRST[k], SECOND[k], 0):
                    self.c_copy(t, k, i).wait_recv()
                    m = self.m ^ i
                    add_into(rc.at[m], span(self.grads[t].at[k, m], KINDS[t], self.c * HALF, HALF))
                    if i == 3:
                        self.x_copy(t, k, 1).start()
                    elif i == FIRST[k]:
                        self.x_copy(t, k, 0).start()
            elif n == 2:
                self.x_copy(t, k, 1).wait_recv()
                add_into(rc.at[self.m ^ SECOND[k]], self.rx[t].at[k, 1])
                self.y_copy(t, k).start()
                self.x_copy(t, k, 0).wait_recv()
                add_into(rc.at[self.m], self.rx[t].at[k, 0])
            elif n == 3:
                self.y_copy(t, k).wait_recv()
                add_into(rc.at[self.m], self.ry[t].at[k])
                for d in range(1, PLANES):
                    self.z_copy(t, k, d).start()
            else:
                own = span(rc.at[self.m], KINDS[t], self.z * SIDE, SIDE)
                for d in range(1, PLANES):
                    self.z_copy(t, k, d).wait_recv()
                rz, out = self.rz[t].at[k], self.outs[t].at[k]

                def body(i, carry, own=own, rz=rz, out=out):
                    r = pl.ds(pl.multiple_of(i * 64, 64), 64)
                    total = own[r, :].astype(F32) + rz[0, r, :].astype(F32)
                    out[r, :] = total + rz[1, r, :].astype(F32) + rz[2, r, :].astype(F32)
                    return carry

                lax.fori_loop(0, own.shape[0] // 64, body, 0)

    def drain(self, t):
        for k in range(2):
            for i in range(4):
                self.c_copy(t, k, i).wait_send()
            self.x_copy(t, k, 0).wait_send()
            self.x_copy(t, k, 1).wait_send()
            self.y_copy(t, k).wait_send()
            for d in range(1, PLANES):
                self.z_copy(t, k, d).wait_send()


def fold_shapes():
    halves, blocks = [], []
    for (_, _, r, c), kind in zip(WHOLE, KINDS):
        halves.append((HALF, c) if kind == "rows" else (r, HALF))
        blocks.append((SIDE, c) if kind == "rows" else (r, SIDE))
    return halves, blocks


def fold_scratch():
    dma = pltpu.SemaphoreType.DMA
    halves, blocks = fold_shapes()
    return (
        [pltpu.VMEM((2, 4) + h, BF16) for h in halves]
        + [pltpu.VMEM((2, 2) + h, BF16) for h in halves]
        + [pltpu.VMEM((2,) + h, BF16) for h in halves]
        + [pltpu.VMEM((2, 3) + b, BF16) for b in blocks],
        [dma((4, 2, 4)), dma((4, 2, 4)), dma((4, 2, 2)), dma((4, 2, 2)), dma((4, 2)), dma((4, 2)),
         dma((4, 2, 3)), dma((4, 2, 3))],
    )


def fold_kernel(gq, go, gu, gd, gv, oq, oo, ou, od, ov, *rest):
    bufs, sems, rv = rest[:16], rest[16:24], rest[24]
    greet_all()
    z, c, m = place()
    vcopy = swap_vectors(gv, rv, rest[25], rest[26], True)
    run_31(lambda d: vcopy(d).start())
    me = m * 8 + z * 2 + c
    rv[me] = gv[me]
    fold = Fold((gq, go, gu, gd), (oq, oo, ou, od), bufs[0:4], bufs[4:8], bufs[8:12], bufs[12:16], sems)
    order = (3, 2, 1, 0)
    for i in range(8):
        for n in range(5):
            if 0 <= i - n < 4:
                fold.stage(order[i - n], n)
    run_31(lambda d: vcopy(d).wait())

    def body(i, acc):
        return acc + rv[i]

    ov[...] = lax.fori_loop(0, 32, body, jnp.zeros((16, 128), F32))
    for t in range(4):
        fold.drain(t)


def fold_gradients(grads, vectors):
    vm = pl.BlockSpec(memory_space=pltpu.VMEM)
    bufs, sems = fold_scratch()
    _, blocks = fold_shapes()
    return pl.pallas_call(
        fold_kernel,
        out_shape=[jax.ShapeDtypeStruct((2,) + b, F32) for b in blocks] + [jax.ShapeDtypeStruct((16, 128), F32)],
        in_specs=[vm] * 5,
        out_specs=[vm] * 5,
        scratch_shapes=bufs + sems + [
            pltpu.VMEM((32, 16, 128), F32), pltpu.SemaphoreType.DMA((32,)), pltpu.SemaphoreType.DMA((32,))
        ],
        compiler_params=pltpu.CompilerParams(collective_id=1, has_side_effects=True, vmem_limit_bytes=62 << 20),
    )(*grads, vectors)


def to_perm(v):
    return v.reshape(v.shape[:-1] + (4, 2, 128)).swapaxes(-3, -2).reshape(v.shape)


def from_perm(v):
    return v.reshape(v.shape[:-1] + (2, 4, 128)).swapaxes(-3, -2).reshape(v.shape)


LOG2E = 1.4426950408889634
ERFC = (
    0.19566775565881125, 0.2262050475851227, 0.020554232590134225, 0.6380773756660296, -0.6389923965501372,
    0.7525645406195645, -0.19407655893061698,
)
NT = (((1,), (1,)), ((), ()))
TN = (((0,), (0,)), ((), ()))


def mm(a, b):
    return jnp.dot(a, b, preferred_element_type=F32)


def mm_nt(a, b):
    return lax.dot_general(a, b, NT, preferred_element_type=F32)


def mm_tn(a, b):
    return lax.dot_general(a, b, TN, preferred_element_type=F32)


def aligned(start, size):
    return pl.ds(pl.multiple_of(start, size), size)


def gelu_pair(u):
    x = jnp.abs(u) * 0.7071067811865476
    e = jnp.exp(x * x * -1.0)
    t = 1.0 / (1.0 + 0.35 * x)
    p = ERFC[6]
    for coef in ERFC[5::-1]:
        p = p * t + coef
    tail = 0.5 * (p * t) * e
    phi = jnp.where(u >= 0.0, 1.0 - tail, tail)
    return u * phi, phi + u * e * 0.3989422804014327


def column_copies(hbm, vmem, sems, store):
    copies = []
    for s in range(2):
        for p in range(8):
            f = (p % 4) * 2 + p // 4
            outside = hbm.at[s, :, pl.ds(f * SIDE, SIDE)]
            inside = vmem.at[pl.ds(s * L, L), pl.ds(p * SIDE, SIDE)]
            pair = (inside, outside) if store else (outside, inside)
            copies.append(pltpu.make_async_copy(pair[0], pair[1], sems.at[s, p]))
    return copies


def lane_half(value, e):
    lane = lax.broadcasted_iota(jnp.int32, (1, value.shape[1]), 1)
    return jnp.where((lane < 64) if e == 0 else (lane >= 64), value, jnp.zeros_like(value))


def row_mean(v):
    return jnp.sum(v, axis=1, keepdims=True) * (1.0 / D)


def forward_kernel(
    lens, x_hbm, cot_hbm, sqr, sor, sur, sdr, ob, g1, b1, db, g2, b2, ub, qb,
    y_hbm, wq_hbm, wo_hbm, wu_hbm, wd_hbm, qkv_hbm, p_hbm, mixed_hbm, lowh_hbm, n1_hbm, rs_hbm, act_hbm, gp_hbm,
    dpre_hbm, vec_out, gain_out,
    wq, wo, wu, wd, vec, x, sqp, sv, qst, pst, mixed, hid, lowh, act, gst, cot, yst, nst, rst, dst, dv, ubs, qvb,
    *sems,
):
    (vs, vr, xsem, csem, ysem, wsem, qsem, psem, msem, gsem, nsem, dsem, asem) = sems[9:]
    z, c, m = place()
    greet_all()
    shards = (
        [sqp.at[k] for k in range(2)],
        [sor.at[pl.ds(k * 128, 128), :] for k in range(2)],
        [sur.at[:, pl.ds(k * HALF, HALF)] for k in range(2)],
        [sdr.at[pl.ds(k * HALF, HALF), :] for k in range(2)],
    )
    for e in range(6):
        pair = e // 3
        part = e % 3
        a = sqr[:, (pair * 2) * 192 + part * 64:(pair * 2) * 192 + part * 64 + 64].astype(F32)
        b = sqr[:, (pair * 2 + 1) * 192 + part * 64:(pair * 2 + 1) * 192 + part * 64 + 64].astype(F32)
        sqp[pair, :, part * 128:part * 128 + 128] = jnp.concatenate([a, b], axis=1).astype(BF16)
    q1 = qb[...].astype(F32)
    zero = jnp.zeros((1, 128), F32)
    sv[...] = jnp.concatenate(
        [r[...].astype(F32) for r in (ob, g1, b1, db, g2, b2)] + [zero, zero, ub[...].astype(F32)]
        + [jnp.concatenate([q1, q1], axis=1), zero, zero, zero], axis=0
    ).astype(BF16)
    spread = Spread(shards, (wq, wo, wu, wd), sems[:9])
    spread.start(0)
    vcopy = swap_vectors(sv, vec, vs, vr, False)
    run_31(lambda d: vcopy(d).start())
    vec[m * 8 + z * 2 + c] = sv[...]
    for t in range(1, 4):
        spread.start(t)
    x_copies = column_copies(x_hbm, x, xsem, False)
    c_copies = column_copies(cot_hbm, cot, csem, False)
    for cp in x_copies + c_copies:
        cp.start()
    run_31(lambda d: vcopy(d).wait())
    for p in range(8):
        dv[:, p * SIDE:(p + 1) * SIDE] = vec[m * 8 + (p % 4) * 2 + p // 4].astype(F32)[0:8]
    for j in range(8):
        k, mm_ = j // 4, j % 4
        t = vec[m * 8 + mm_ * 2 + k].astype(F32)
        ubs[j] = jnp.concatenate([t[8:9], t[9:10], t[10:11], t[11:12]], axis=1)
        rows = [vec[mm_ * 8 + 4 * k + i].astype(F32)[12:13] for i in range(4)]
        lane = lax.broadcasted_iota(jnp.int32, (1, 128), 1)
        qvb[j] = jnp.concatenate(
            [jnp.where(lane < 64, rows[0], rows[2]), zero, jnp.where(lane < 64, rows[1], rows[3])], axis=1
        )
    for cp in x_copies + c_copies:
        cp.wait()
    wholes = ((wq, wq_hbm), (wo, wo_hbm), (wu, wu_hbm), (wd, wd_hbm))
    w_copies = [pltpu.make_async_copy(a, b, wsem.at[i]) for i, (a, b) in enumerate(wholes)]
    spread.stage(0, 0)
    spread.stage(0, 1)
    spread.stage(1, 0)
    spread.stage(0, 2)
    spread.stage(1, 1)
    spread.stage(0, 3)
    w_copies[0].start()
    spread.stage(2, 0)

    def q_copy(it):
        j, s = it // 2, it % 2
        return pltpu.make_async_copy(qst.at[s], qkv_hbm.at[j, aligned(s * L, L), :], qsem.at[s])

    def p_copy(it):
        j, s = it // 2, it % 2
        return pltpu.make_async_copy(pst.at[s], p_hbm.at[j, s], psem.at[s])

    def attend(it, carry):
        j, s = it // 2, it % 2
        rows = aligned(s * L, L)

        @pl.when(it >= 2)
        def _():
            q_copy(it - 2).wait()
            p_copy(it - 2).wait()

        qst[s] = (mm(x[rows, :], wq[j // 4, j % 4]) + qvb[j]).astype(BF16)
        q_copy(it).start()
        keys, values = qst[s, :, 128:256], qst[s, :, 256:384]
        length = lens[s, m]
        lane = lax.broadcasted_iota(jnp.int32, (1, L), 1)
        bias = jnp.where(lane < length, 0.0, -1e30)
        out = [None, None]
        for e in range(2):
            k_e, v_e = lane_half(keys, e), lane_half(values, e)
            for h in range(2):
                half = slice(h * 256, h * 256 + 256)
                scores = mm_nt(qst[s, half, 0:128], k_e) + bias
                top = jnp.max(scores, axis=1, keepdims=True)
                ex = jnp.exp2((scores - top) * (LOG2E * DH ** (-0.5)))
                probs = (ex * (1.0 / jnp.sum(ex, axis=1, keepdims=True))).astype(BF16)
                pst[s, e, half, :] = probs
                part = mm(probs, v_e)
                out[h] = part if out[h] is None else out[h] + part
        p_copy(it).start()
        mixed[rows, aligned(j * 128, 128)] = jnp.concatenate(out, axis=0).astype(BF16)

        @pl.when(it == 3)
        def _():
            spread.stage(1, 2)

        @pl.when(it == 6)
        def _():
            spread.stage(1, 3)
            w_copies[1].start()

        @pl.when(it == 9)
        def _():
            spread.stage(2, 1)

        @pl.when(it == 12)
        def _():
            spread.stage(3, 0)

        return carry

    lax.fori_loop(0, 16, attend, 0)
    for it in (14, 15):
        q_copy(it).wait()
        p_copy(it).wait()
    m_copy = pltpu.make_async_copy(mixed, mixed_hbm, msem.at[0])
    m_copy.start()

    def n_copy(i):
        return pltpu.make_async_copy(nst.at[i % 2], n1_hbm.at[aligned(i * 256, 256), :], nsem.at[i % 2])

    def r_copy(i):
        return pltpu.make_async_copy(rst.at[i % 2], rs_hbm.at[aligned(i * 256, 256), :], nsem.at[2 + i % 2])

    def first_norm(i, carry):
        rows = aligned(i * 256, 256)

        @pl.when(i >= 2)
        def _():
            n_copy(i - 2).wait()
            r_copy(i - 2).wait()

        pre = mm(mixed[rows, :], wo[...].reshape(D, D)) + dv[0:1] + x[rows, :].astype(F32)
        cen = pre - row_mean(pre)
        inv = lax.rsqrt(row_mean(cen * cen) + EPSILON)
        n = cen * inv
        nst[i % 2] = n
        rst[i % 2] = jnp.broadcast_to(inv, (256, 128))
        n_copy(i).start()
        r_copy(i).start()
        h = n * dv[1:2] + dv[2:3]
        hid[rows, :] = h
        lowh[rows, :] = h.astype(BF16)
        return carry

    lax.fori_loop(0, 4, first_norm, 0)
    spread.stage(2, 2)
    for i in (2, 3):
        n_copy(i).wait()
        r_copy(i).wait()
    h_copy = pltpu.make_async_copy(lowh, lowh_hbm, msem.at[1])
    h_copy.start()
    spread.stage(2, 3)
    w_copies[2].start()
    spread.stage(3, 1)

    def g_copy(it):
        j, r = it // 2, it % 2
        return pltpu.make_async_copy(gst.at[r], gp_hbm.at[j, aligned(r * L, L), :], gsem.at[r])

    def a_copy(it):
        j, r = it // 2, it % 2
        src = act.at[aligned(r * L, L), aligned(j * HALF, HALF)]
        return pltpu.make_async_copy(src, act_hbm.at[j, aligned(r * L, L), :], asem.at[it])

    def up(it, carry):
        j, r = it // 2, it % 2
        rows = aligned(r * L, L)

        @pl.when(it >= 2)
        def _():
            g_copy(it - 2).wait()

        w = wu[j // 4, j % 4]
        for h in range(2):
            sub = pl.ds(pl.multiple_of(r * L + h * 256, 256), 256)
            a, g = gelu_pair(mm(lowh[sub, :], w) + ubs[j])
            act[sub, aligned(j * HALF, HALF)] = a.astype(BF16)
            gst[r, h * 256:h * 256 + 256, :] = g.astype(BF16)
        g_copy(it).start()
        a_copy(it).start()

        @pl.when(it == 12)
        def _():
            spread.stage(3, 2)

        return carry

    lax.fori_loop(0, 16, up, 0)
    spread.stage(3, 3)
    w_copies[3].start()
    gain_out[...] = jnp.zeros((8, D), F32)

    def d_copy(i):
        return pltpu.make_async_copy(dst.at[i % 2], dpre_hbm.at[aligned(i * 256, 256), :], dsem.at[i % 2])

    def down(i, carry):
        rows = aligned(i * 256, 256)

        @pl.when(i >= 2)
        def _():
            d_copy(i - 2).wait()

        pre = mm(act[rows, :], wd[...].reshape(FF, D)) + dv[3:4] + hid[rows, :]
        cen = pre - row_mean(pre)
        inv = lax.rsqrt(row_mean(cen * cen) + EPSILON)
        n = cen * inv
        yst[rows, :] = (n * dv[4:5] + dv[5:6]).astype(BF16)
        pos = (i % 2) * 256 + lax.broadcasted_iota(jnp.int32, (256, 1), 0)
        grad = jnp.where(pos < lens[i // 2, m], cot[rows, :].astype(F32), 0.0)
        g = grad * dv[4:5]
        back = inv * (g - row_mean(g) - n * row_mean(g * n))
        dst[i % 2] = back
        d_copy(i).start()
        gain_out[3:4, :] += jnp.sum(back, axis=0, keepdims=True)
        gain_out[4:5, :] += jnp.sum(grad * n, axis=0, keepdims=True)
        gain_out[5:6, :] += jnp.sum(grad, axis=0, keepdims=True)
        return carry

    lax.fori_loop(0, 4, down, 0)
    y_copies = column_copies(y_hbm, yst, ysem, True)
    for cp in y_copies:
        cp.start()
    vec_out[...] = dv[...]
    for i in (2, 3):
        d_copy(i).wait()
    for it in (14, 15):
        g_copy(it).wait()

    def a_wait(it, carry):
        a_copy(it).wait()
        return carry

    lax.fori_loop(0, 16, a_wait, 0)
    m_copy.wait()
    h_copy.wait()
    for cp in y_copies + w_copies:
        cp.wait()
    for t in range(4):
        spread.drain(t)


SAVED = (
    ((8, 1024, 384), BF16), ((8, 2, 2, L, L), BF16), ((1024, D), BF16), ((1024, D), BF16), ((1024, D), F32),
    ((1024, 128), F32), ((8, 1024, HALF), BF16), ((8, 1024, HALF), BF16), ((1024, D), F32),
)


def forward(lengths, inputs, cotangent, weights, vectors):
    vm = pl.BlockSpec(memory_space=pltpu.VMEM)
    anywhere = pl.BlockSpec(memory_space=pl.ANY)
    shape = jax.ShapeDtypeStruct
    dma = pltpu.SemaphoreType.DMA
    v = pltpu.VMEM
    scratch = [v(s, BF16) for s in WHOLE] + [
        v((32, 16, 128), BF16), v((1024, D), BF16), v((2, 128, 384), BF16), v((16, 128), BF16), v((2, L, 384), BF16),
        v((2, 2, L, L), BF16), v((1024, D), BF16), v((1024, D), F32), v((1024, D), BF16), v((1024, FF), BF16),
        v((2, L, HALF), BF16), v((1024, D), BF16), v((1024, D), BF16), v((2, 256, D), F32), v((2, 256, 128), F32),
        v((2, 256, D), F32), v((8, D), F32), v((8, 1, HALF), F32), v((8, 1, 384), F32),
    ] + spread_sems() + [
        dma((32,)), dma((32,)), dma((2, 8)), dma((2, 8)), dma((2, 8)), dma((4,)), dma((2,)), dma((2,)), dma((2,)),
        dma((2,)), dma((4,)), dma((2,)), dma((16,)),
    ]
    return pl.pallas_call(
        forward_kernel,
        out_shape=[shape((2, L, D), BF16)] + [shape(s, BF16) for s in WHOLE] + [shape(s, d) for s, d in SAVED]
        + [shape((8, D), F32), shape((8, D), F32)],
        in_specs=[pl.BlockSpec(memory_space=pltpu.SMEM), anywhere, anywhere] + [vm] * 12,
        out_specs=[anywhere] * 14 + [vm, vm],
        scratch_shapes=scratch,
        compiler_params=pltpu.CompilerParams(collective_id=0, has_side_effects=True, vmem_limit_bytes=67000000),
    )(lengths, inputs, cotangent, *weights, *vectors)

def fast_body(
    inputs, lengths, qkv_weight, qv_bias, out_weight, out_bias, norm1_gain, norm1_bias, up_weight, up_bias,
    down_weight, down_bias, norm2_gain, norm2_bias, cotangent,
):
    rows = 2 * L
    row = lambda v: v.reshape(1, 128)
    y, wq, wo, wu, wd, qkv, low_probs, mixed, low_hidden, n1, rs1, act, slope, d_pre2, dv, gains = forward(
        lengths, inputs, cotangent, (qkv_weight, out_weight, up_weight, down_weight),
        (row(out_bias), row(norm1_gain), row(norm1_bias), row(down_bias), row(norm2_gain), row(norm2_bias),
         up_bias.reshape(4, 128), qv_bias.reshape(1, 64)),
    )
    wq, wo, wu, wd = (w.reshape((8,) + w.shape[2:]) for w in (wq, wo, wu, wd))
    x = to_perm(inputs.reshape(rows, D))
    scale = DH ** (-0.5)
    heads = qkv.reshape(8, 2, L, 3, 2, 64)
    q, k, v = heads[:, :, :, 0], heads[:, :, :, 1], heads[:, :, :, 2]
    probs = low_probs.astype(F32)
    d_branch = d_pre2.astype(BF16)
    d_act = jnp.einsum("rd,jcd->jrc", d_branch, wd, preferred_element_type=F32)
    g_down = jnp.einsum("jrc,rd->jcd", act, d_branch, preferred_element_type=F32).astype(BF16)
    d_inner = (d_act * slope.astype(F32)).astype(BF16)
    g_up = jnp.einsum("rd,jrc->jdc", low_hidden, d_inner, preferred_element_type=F32).astype(BF16)
    d_hidden = d_pre2 + jnp.einsum("jrc,jdc->rd", d_inner, wu, preferred_element_type=F32)
    gn = d_hidden * dv[1]
    d_pre1 = rs1[:, :1] * (
        gn - jnp.mean(gn, axis=1, keepdims=True) - n1 * jnp.mean(gn * n1, axis=1, keepdims=True)
    )
    d_gain1, d_shift1 = jnp.sum(d_hidden * n1, 0), jnp.sum(d_hidden, 0)
    d_attended = d_pre1.astype(BF16)
    d_mixed = lax.dot_general(d_attended, wo.reshape(D, D), CONTRACT_COLS, preferred_element_type=F32).astype(BF16)
    g_out = lax.dot_general(mixed, d_attended, CONTRACT_ROWS, preferred_element_type=F32).astype(BF16)
    d_heads = d_mixed.reshape(2, L, 8, 2, 64)
    d_value = jnp.einsum("jshqk,sqjhe->jskhe", low_probs, d_heads, preferred_element_type=F32)
    d_probs = jnp.einsum("sqjhe,jskhe->jshqk", d_heads, v, preferred_element_type=F32)
    delta = jnp.sum(probs * d_probs, axis=-1, keepdims=True)
    d_scores = (probs * (d_probs - delta)).astype(BF16)
    d_query = jnp.einsum("jshqk,jskhe->jsqhe", d_scores, k, preferred_element_type=F32) * scale
    d_key = jnp.einsum("jshqk,jsqhe->jskhe", d_scores, q, preferred_element_type=F32) * scale
    d_proj = jnp.stack([d_query, d_key, d_value], axis=3).astype(BF16).reshape(8, rows, 384)
    g_qkv = jnp.einsum("rd,jrc->jdc", x, d_proj, preferred_element_type=F32).astype(BF16)
    input_grad = d_pre1 + jnp.einsum("jrc,jdc->rd", d_proj, wq, preferred_element_type=F32)

    wide = [from_perm(g).reshape(8, 128) for g in (jnp.sum(d_pre1, 0), d_gain1, d_shift1, gains[3], gains[4], gains[5])]
    up_sum = jnp.sum(d_inner.astype(F32), axis=1).reshape(2, 4, 512).swapaxes(0, 1).reshape(8, 4, 128)
    common = jnp.concatenate([jnp.stack(wide, axis=1), jnp.zeros((8, 2, 128), F32), up_sum], axis=1)
    qv_sum = jnp.sum(d_proj.astype(F32), axis=1).reshape(2, 4, 3, 2, 64).transpose(1, 0, 3, 2, 4)
    qv_sum = jnp.stack([qv_sum[:, :, :, 0], qv_sum[:, :, :, 2]], axis=3).reshape(4, 8, 1, 64)
    qv_sum = jnp.pad(qv_sum, ((0, 0), (0, 0), (0, 3), (0, 64)))
    vec_grad = jnp.concatenate([jnp.broadcast_to(common[None], (4, 8, 12, 128)), qv_sum], axis=2)
    grads = (g_qkv.reshape(WHOLE[0]), g_out.reshape(WHOLE[1]), g_up.reshape(WHOLE[2]), g_down.reshape(WHOLE[3]))
    oq, oo, ou, od, ov = fold_gradients(grads, vec_grad.reshape(32, 16, 128))
    return (
        y,
        from_perm(input_grad).reshape(inputs.shape),
        oq.reshape(2, 128, 3, 2, 64).transpose(1, 0, 3, 2, 4).reshape(128, 768),
        ov[12, :64],
        oo.reshape(256, 128),
        ov[0],
        ov[1],
        ov[2],
        ou.transpose(1, 0, 2).reshape(128, 1024),
        ov[8:12].reshape(512),
        od.reshape(1024, 128),
        ov[3],
        ov[4],
        ov[5],
    )


def solution(mesh):
    placed = (
        P(None, ("fsdp", "mp"), None),
        P(None, "fsdp"),
        P("fsdp", "mp"),
        P(("mp", "fsdp")),
        P("mp", "fsdp"),
        P("fsdp"),
        P("fsdp"),
        P("fsdp"),
        P("fsdp", "mp"),
        P("fsdp"),
        P("mp", "fsdp"),
        P("fsdp"),
        P("fsdp"),
        P("fsdp"),
        P(None, ("fsdp", "mp"), None),
    )
    blocks_fit = mesh.shape["fsdp"] == 8 and mesh.shape["mp"] == 4
    return jax.shard_map(
        fast_body if blocks_fit else generic_body,
        mesh=mesh,
        in_specs=placed,
        out_specs=(
            P(None, ("fsdp", "mp"), None),
            P(None, ("fsdp", "mp"), None),
            P("fsdp", "mp"),
            P(("mp", "fsdp")),
            P("mp", "fsdp"),
            P("fsdp"),
            P("fsdp"),
            P("fsdp"),
            P("fsdp", "mp"),
            P("fsdp"),
            P("mp", "fsdp"),
            P("fsdp"),
            P("fsdp"),
            P("fsdp"),
        ),
        check_vma=False,
    )
```

```python
from functools import partial

import jax
import jax.numpy as jnp
from jax import lax
from jax.experimental import pallas as pl
from jax.experimental.pallas import tpu as pltpu
from jax.sharding import PartitionSpec as P

D = 1024
DH = 64
FF = 4096
L = 512
MBS = 2


EPSILON = 1e-06
CONTRACT_ROWS = (((0,), (0,)), ((), ()))
CONTRACT_COLS = (((1,), (1,)), ((), ()))


def normalize(values, scale_vec, shift_vec):
    row_mean = jnp.mean(values, axis=-1, keepdims=True)
    centered = values - row_mean
    spread = jnp.mean(centered * centered, axis=-1, keepdims=True)
    return centered * lax.rsqrt(spread + EPSILON) * scale_vec + shift_vec


def gelu_exact(values):
    return jax.nn.gelu(values, approximate=False)


def collect_forward(shards):
    return (
        lax.all_gather(shards[0], "fsdp", axis=0, tiled=True),
        lax.all_gather(shards[1], "fsdp", axis=0, tiled=True),
        lax.all_gather(shards[2], "fsdp", axis=1, tiled=True),
        lax.all_gather(shards[3], "fsdp", axis=0, tiled=True),
        lax.all_gather(shards[4], "fsdp", axis=0, tiled=True),
        lax.all_gather(shards[5], "fsdp", axis=0, tiled=True),
        lax.all_gather(shards[6], "fsdp", axis=0, tiled=True),
        lax.all_gather(shards[7], "fsdp", axis=0, tiled=True),
        lax.all_gather(shards[8], "fsdp", axis=1, tiled=True),
        lax.all_gather(shards[9], "fsdp", axis=0, tiled=True),
        lax.all_gather(shards[10], "fsdp", axis=0, tiled=True),
        lax.all_gather(shards[11], "fsdp", axis=0, tiled=True),
    )


def collect_backward(shards):
    return (
        lax.all_gather(shards[0], "fsdp", axis=0, tiled=True),
        lax.all_gather(shards[2], "fsdp", axis=1, tiled=True),
        lax.all_gather(shards[4], "fsdp", axis=0, tiled=True),
        lax.all_gather(shards[6], "fsdp", axis=0, tiled=True),
        lax.all_gather(shards[8], "fsdp", axis=1, tiled=True),
        lax.all_gather(shards[10], "fsdp", axis=0, tiled=True),
    )


def attend_forward(packed, scale_value):
    queries, keysets, values, seq_len = packed
    scores = (
        jnp.einsum("qhe,khe->hqk", queries, keysets, preferred_element_type=jnp.float32)
        * scale_value
    )
    live_mask = jnp.arange(scores.shape[-1])[None, None, :] < seq_len
    scores = jnp.where(live_mask, scores, -1000000000.0)
    row_max = jnp.max(scores, axis=-1, keepdims=True)
    exp_scores = jnp.exp(scores - row_max)
    denom_sum = jnp.sum(exp_scores, axis=-1, keepdims=True)
    attn_probs = (exp_scores / denom_sum).astype(jnp.bfloat16)
    mixed_heads = jnp.einsum("hqk,khe->qhe", attn_probs, values, preferred_element_type=jnp.float32)
    return (mixed_heads.astype(jnp.bfloat16), (row_max + jnp.log(denom_sum))[:, :, 0])


def attend_backward(packed, scale_value):
    queries, keysets, values, seq_len, log_sums, d_mixed = packed
    scores = (
        jnp.einsum("qhe,khe->hqk", queries, keysets, preferred_element_type=jnp.float32)
        * scale_value
    )
    live_mask = jnp.arange(scores.shape[-1])[None, None, :] < seq_len
    attn_probs = jnp.where(live_mask, jnp.exp(scores - log_sums[:, :, None]), 0.0)
    low_probs = attn_probs.astype(jnp.bfloat16)
    d_value = jnp.einsum("hqk,qhe->khe", low_probs, d_mixed, preferred_element_type=jnp.float32)
    d_probs = jnp.einsum("qhe,khe->hqk", d_mixed, values, preferred_element_type=jnp.float32)
    row_delta = jnp.sum(attn_probs * d_probs, axis=-1, keepdims=True)
    d_scores = (attn_probs * (d_probs - row_delta)).astype(jnp.bfloat16)
    d_query = (
        jnp.einsum("hqk,khe->qhe", d_scores, keysets, preferred_element_type=jnp.float32)
        * scale_value
    )
    d_key = (
        jnp.einsum("hqk,qhe->khe", d_scores, queries, preferred_element_type=jnp.float32)
        * scale_value
    )
    return jnp.stack([d_query, d_key, d_value], axis=2).astype(jnp.bfloat16)


def generic_body(
    inputs,
    lengths,
    qkv_weight,
    qv_bias,
    out_weight,
    out_bias,
    norm1_gain,
    norm1_bias,
    up_weight,
    up_bias,
    down_weight,
    down_bias,
    norm2_gain,
    norm2_bias,
    cotangent,
):
    shards = (
        qkv_weight,
        qv_bias,
        out_weight,
        out_bias,
        norm1_gain,
        norm1_bias,
        up_weight,
        up_bias,
        down_weight,
        down_bias,
        norm2_gain,
        norm2_bias,
    )
    row_count = inputs.shape[1]
    mp_count = lax.axis_size("mp")
    mp_index = lax.axis_index("mp")
    up_cols = up_weight.shape[1]
    scale_value = DH ** (-0.5)
    group_rows = row_count * mp_count
    head_count = qkv_weight.shape[1] // (3 * DH)
    row_ids = mp_index * row_count + jnp.arange(row_count)
    seq_count = group_rows // L
    head_width = head_count * DH
    seq_ids = row_ids // L
    positions = row_ids % L
    seq_match = seq_ids[:, None] == jnp.arange(seq_count)[None, :]
    grad_qkv = jnp.zeros((D, 3 * head_width), jnp.float32)
    grad_qvb = jnp.zeros((2 * head_width,), jnp.float32)
    grad_out = jnp.zeros((head_width, D), jnp.float32)
    grad_up = jnp.zeros((D, up_cols), jnp.float32)
    grad_down = jnp.zeros((up_cols, D), jnp.float32)
    grad_upb = jnp.zeros((FF,), jnp.float32)
    grad_outb = jnp.zeros((D,), jnp.float32)
    grad_gain1 = jnp.zeros((D,), jnp.float32)
    grad_shift1 = jnp.zeros((D,), jnp.float32)
    grad_downb = jnp.zeros((D,), jnp.float32)
    grad_gain2 = jnp.zeros((D,), jnp.float32)
    grad_shift2 = jnp.zeros((D,), jnp.float32)
    layer_rows = []
    input_rows = []
    for micro_idx in range(MBS):
        fwd_set = collect_forward(shards)
        qkv_full, qvb_full, out_full, outb_full = (fwd_set[0], fwd_set[1], fwd_set[2], fwd_set[3])
        gain_one = fwd_set[4].astype(jnp.float32)
        shift_one = fwd_set[5].astype(jnp.float32)
        up_full, upb_full, down_full = (fwd_set[6], fwd_set[7].astype(jnp.float32), fwd_set[8])
        downb_full = fwd_set[9].astype(jnp.float32)
        gain_two = fwd_set[10].astype(jnp.float32)
        shift_two = fwd_set[11].astype(jnp.float32)
        tokens = inputs[micro_idx]
        upb_used = lax.dynamic_slice_in_dim(upb_full, mp_index * up_cols, up_cols, 0)
        gathered = lax.all_gather(tokens, "mp", axis=0, tiled=True)
        seq_lens = lengths[micro_idx]
        pair_bias = qvb_full.astype(jnp.float32).reshape(head_count, 2, DH)
        bias_full = jnp.stack(
            [pair_bias[:, 0], jnp.zeros_like(pair_bias[:, 0]), pair_bias[:, 1]], axis=1
        )
        project = jnp.dot(
            gathered, qkv_full, preferred_element_type=jnp.float32
        ) + bias_full.reshape(3 * head_width)
        project = project.astype(jnp.bfloat16).reshape(seq_count, L, head_count, 3, DH)
        queries = project[:, :, :, 0]
        keysets = project[:, :, :, 1]
        values = project[:, :, :, 2]
        mixed_heads, log_sums = lax.map(
            partial(attend_forward, scale_value=scale_value), (queries, keysets, values, seq_lens)
        )
        mixed_flat = mixed_heads.reshape(group_rows, head_width)
        attn_own = lax.psum_scatter(
            jnp.dot(mixed_flat, out_full, preferred_element_type=jnp.float32).astype(jnp.bfloat16),
            "mp",
            scatter_dimension=0,
            tiled=True,
        ).astype(jnp.float32)
        pre_norm1 = attn_own + outb_full.astype(jnp.float32) + tokens.astype(jnp.float32)
        hidden = normalize(pre_norm1, gain_one, shift_one)
        low_hidden = hidden.astype(jnp.bfloat16)
        ffn_rows = lax.all_gather(low_hidden, "mp", axis=0, tiled=True)
        inner_sum = jnp.dot(ffn_rows, up_full, preferred_element_type=jnp.float32) + upb_used
        activated = gelu_exact(inner_sum).astype(jnp.bfloat16)
        branch = lax.psum_scatter(
            jnp.dot(activated, down_full, preferred_element_type=jnp.float32).astype(jnp.bfloat16),
            "mp",
            scatter_dimension=0,
            tiled=True,
        ).astype(jnp.float32)
        pre_norm2 = branch + downb_full + hidden
        layer_rows.append(normalize(pre_norm2, gain_two, shift_two).astype(jnp.bfloat16))
        bwd_set = collect_backward(shards)
        qkv_back, out_back = (bwd_set[0], bwd_set[1])
        gain_one_back = bwd_set[2].astype(jnp.float32)
        up_back, down_back = (bwd_set[3], bwd_set[4])
        gain_two_back = bwd_set[5].astype(jnp.float32)
        row_len = jnp.sum(jnp.where(seq_match, seq_lens[None, :], 0), axis=1)
        live_rows = (positions < row_len).astype(jnp.float32)
        grad_rows = cotangent[micro_idx].astype(jnp.float32) * live_rows[:, None]
        _, pull_two = jax.vjp(normalize, pre_norm2, gain_two_back, shift_two)
        d_pre2, d_gain2, d_shift2 = pull_two(grad_rows)
        grad_gain2 = grad_gain2 + d_gain2
        grad_shift2 = grad_shift2 + d_shift2
        grad_downb = grad_downb + jnp.sum(d_pre2, axis=0)
        d_branch = d_pre2.astype(jnp.bfloat16)
        d_rows = lax.all_gather(d_branch, "mp", axis=0, tiled=True)
        d_act = lax.dot_general(
            d_rows, down_back, CONTRACT_COLS, preferred_element_type=jnp.float32
        )
        grad_down = grad_down + lax.dot_general(
            activated, d_rows, CONTRACT_ROWS, preferred_element_type=jnp.float32
        )
        _, pull_gelu = jax.vjp(gelu_exact, inner_sum)
        d_inner = pull_gelu(d_act)[0].astype(jnp.bfloat16)
        bias_term = jnp.sum(d_inner.astype(jnp.float32), axis=0)
        grad_up = grad_up + lax.dot_general(
            ffn_rows, d_inner, CONTRACT_ROWS, preferred_element_type=jnp.float32
        )
        grad_upb = grad_upb + lax.dynamic_update_slice_in_dim(
            jnp.zeros((FF,), jnp.float32), bias_term, mp_index * up_cols, 0
        )
        d_hidden_part = lax.psum_scatter(
            lax.dot_general(
                d_inner, up_back, CONTRACT_COLS, preferred_element_type=jnp.float32
            ).astype(jnp.bfloat16),
            "mp",
            scatter_dimension=0,
            tiled=True,
        ).astype(jnp.float32)
        d_hidden = d_pre2 + d_hidden_part
        _, pull_one = jax.vjp(normalize, pre_norm1, gain_one_back, shift_one)
        d_pre1, d_gain1, d_shift1 = pull_one(d_hidden)
        grad_gain1 = grad_gain1 + d_gain1
        grad_shift1 = grad_shift1 + d_shift1
        grad_outb = grad_outb + jnp.sum(d_pre1, axis=0)
        d_attended = d_pre1.astype(jnp.bfloat16)
        d_attn_rows = lax.all_gather(d_attended, "mp", axis=0, tiled=True)
        d_mixed = lax.dot_general(
            d_attn_rows, out_back, CONTRACT_COLS, preferred_element_type=jnp.float32
        )
        d_mixed = d_mixed.astype(jnp.bfloat16)
        grad_out = grad_out + lax.dot_general(
            mixed_flat, d_attn_rows, CONTRACT_ROWS, preferred_element_type=jnp.float32
        )
        d_project = lax.map(
            partial(attend_backward, scale_value=scale_value),
            (
                queries,
                keysets,
                values,
                seq_lens,
                log_sums,
                d_mixed.reshape(seq_count, L, head_count, DH),
            ),
        )
        d_flat = d_project.reshape(group_rows, 3 * head_width)
        grad_qkv = grad_qkv + lax.dot_general(
            gathered, d_flat, CONTRACT_ROWS, preferred_element_type=jnp.float32
        )
        bias_parts = jnp.sum(d_flat.astype(jnp.float32), axis=0).reshape(head_count, 3, DH)
        grad_qvb = grad_qvb + jnp.stack([bias_parts[:, 0], bias_parts[:, 2]], axis=1).reshape(
            2 * head_width
        )
        input_rows.append(
            d_pre1
            + lax.psum_scatter(
                lax.dot_general(
                    d_flat, qkv_back, CONTRACT_COLS, preferred_element_type=jnp.float32
                ).astype(jnp.bfloat16),
                "mp",
                scatter_dimension=0,
                tiled=True,
            ).astype(jnp.float32)
        )
    summed = (
        lax.psum_scatter(
            grad_qkv.astype(jnp.bfloat16), "fsdp", scatter_dimension=0, tiled=True
        ).astype(jnp.float32),
        lax.psum_scatter(
            grad_qvb.astype(jnp.bfloat16), "fsdp", scatter_dimension=0, tiled=True
        ).astype(jnp.float32),
        lax.psum_scatter(
            grad_out.astype(jnp.bfloat16), "fsdp", scatter_dimension=1, tiled=True
        ).astype(jnp.float32),
        lax.psum_scatter(
            grad_outb.astype(jnp.bfloat16), "fsdp", scatter_dimension=0, tiled=True
        ).astype(jnp.float32),
        lax.psum_scatter(
            grad_gain1.astype(jnp.bfloat16), "fsdp", scatter_dimension=0, tiled=True
        ).astype(jnp.float32),
        lax.psum_scatter(
            grad_shift1.astype(jnp.bfloat16), "fsdp", scatter_dimension=0, tiled=True
        ).astype(jnp.float32),
        lax.psum_scatter(
            grad_up.astype(jnp.bfloat16), "fsdp", scatter_dimension=0, tiled=True
        ).astype(jnp.float32),
        lax.psum_scatter(
            grad_upb.astype(jnp.bfloat16), "fsdp", scatter_dimension=0, tiled=True
        ).astype(jnp.float32),
        lax.psum_scatter(
            grad_down.astype(jnp.bfloat16), "fsdp", scatter_dimension=1, tiled=True
        ).astype(jnp.float32),
        lax.psum_scatter(
            grad_downb.astype(jnp.bfloat16), "fsdp", scatter_dimension=0, tiled=True
        ).astype(jnp.float32),
        lax.psum_scatter(
            grad_gain2.astype(jnp.bfloat16), "fsdp", scatter_dimension=0, tiled=True
        ).astype(jnp.float32),
        lax.psum_scatter(
            grad_shift2.astype(jnp.bfloat16), "fsdp", scatter_dimension=0, tiled=True
        ).astype(jnp.float32),
    )
    vectors = lax.psum(
        (summed[3], summed[4], summed[5], summed[7], summed[9], summed[10], summed[11]), "mp"
    )
    return (
        jnp.stack(layer_rows),
        jnp.stack(input_rows),
        summed[0],
        summed[1],
        summed[2],
        vectors[0],
        vectors[1],
        vectors[2],
        summed[6],
        vectors[3],
        summed[8],
        vectors[4],
        vectors[5],
        vectors[6],
    )


MESH_ID = pl.DeviceIdType.MESH
F32 = jnp.float32
BF16 = jnp.bfloat16
PLANES = 4
SIDE = 128
HALF = 512
KINDS = ("rows", "cols", "rows", "cols")
FIRST = (1, 2)
SECOND = (2, 1)


def place():
    f = lax.axis_index("fsdp")
    return f // 2, f % 2, lax.axis_index("mp")


def span(ref, kind, start, size):
    start = pl.multiple_of(start, SIDE)
    if kind == "rows":
        return ref.at[pl.ds(start, size), :]
    return ref.at[:, pl.ds(start, size)]


def remote(src, dst, send, recv, f, m):
    return pltpu.make_async_remote_copy(
        src_ref=src, dst_ref=dst, send_sem=send, recv_sem=recv, device_id=(f, m), device_id_type=MESH_ID
    )


def greet_all():
    z, c, m = place()
    me = (z * 2 + c) * 4 + m
    barrier = pltpu.get_barrier_semaphore()

    def hello(d, carry):
        other = (me + d) % 32
        pl.semaphore_signal(barrier, inc=1, device_id=(other // 4, other % 4), device_id_type=MESH_ID)
        return carry

    lax.fori_loop(1, 32, hello, 0)
    pl.semaphore_wait(barrier, 31)


class Spread:
    def __init__(self, shards, wholes, sems):
        self.shards, self.wholes = shards, wholes
        self.zs, self.zr, self.xs, self.xr, self.ys, self.yr, self.cs, self.cr, self.own = sems
        self.z, self.c, self.m = place()

    def core_span(self, t, k, m, c):
        return span(self.wholes[t].at[k, m], KINDS[t], c * HALF, HALF)

    def z_copy(self, t, k, d):
        z = (self.z + d) % PLANES
        dst = span(self.wholes[t].at[k, self.m], KINDS[t], self.c * HALF + self.z * SIDE, SIDE)
        return remote(
            self.shards[t][k], dst, self.zs.at[t, k, d - 1], self.zr.at[t, k, d - 1], z * 2 + self.c, self.m
        )

    def own_copy(self, t, k):
        dst = span(self.wholes[t].at[k, self.m], KINDS[t], self.c * HALF + self.z * SIDE, SIDE)
        return pltpu.make_async_copy(self.shards[t][k], dst, self.own.at[t, k])

    def x_copy(self, t, k):
        blk = self.core_span(t, k, self.m, self.c)
        return remote(blk, blk, self.xs.at[t, k], self.xr.at[t, k], self.z * 2 + self.c, self.m ^ FIRST[k])

    def y_copy(self, t, k, i):
        blk = self.core_span(t, k, self.m ^ (FIRST[k] if i else 0), self.c)
        return remote(blk, blk, self.ys.at[t, k, i], self.yr.at[t, k, i], self.z * 2 + self.c, self.m ^ SECOND[k])

    def c_copy(self, t, k, i):
        blk = self.core_span(t, k, self.m ^ i, self.c)
        return remote(blk, blk, self.cs.at[t, k, i], self.cr.at[t, k, i], self.z * 2 + 1 - self.c, self.m)

    def start(self, t):
        for k in range(2):
            for d in range(1, PLANES):
                self.z_copy(t, k, d).start()
            self.own_copy(t, k).start()

    def stage(self, t, n):
        for k in range(2):
            if n == 0:
                self.own_copy(t, k).wait()
                for d in range(1, PLANES):
                    self.z_copy(t, k, d).wait_recv()
                self.x_copy(t, k).start()
                self.y_copy(t, k, 0).start()
                self.c_copy(t, k, 0).start()
            elif n == 1:
                self.x_copy(t, k).wait_recv()
                self.y_copy(t, k, 1).start()
                self.c_copy(t, k, FIRST[k]).start()
            elif n == 2:
                self.y_copy(t, k, 0).wait_recv()
                self.c_copy(t, k, SECOND[k]).start()
                self.y_copy(t, k, 1).wait_recv()
                self.c_copy(t, k, 3).start()
            else:
                for i in range(4):
                    self.c_copy(t, k, i).wait_recv()

    def drain(self, t):
        for k in range(2):
            for d in range(1, PLANES):
                self.z_copy(t, k, d).wait_send()
            self.x_copy(t, k).wait_send()
            self.y_copy(t, k, 0).wait_send()
            self.y_copy(t, k, 1).wait_send()
            for i in range(4):
                self.c_copy(t, k, i).wait_send()


def spread_sems():
    dma = pltpu.SemaphoreType.DMA
    return [
        dma((4, 2, 3)), dma((4, 2, 3)), dma((4, 2)), dma((4, 2)), dma((4, 2, 2)), dma((4, 2, 2)),
        dma((4, 2, 4)), dma((4, 2, 4)), dma((4, 2)),
    ]


def swap_vectors(src, dst, send, recv, chunked):
    z, c, m = place()
    f = z * 2 + c
    me = f * 4 + m

    def copy(d):
        other = (me + d) % 32
        fo, mo = other // 4, other % 4
        piece = src.at[mo * 8 + fo] if chunked else src
        return remote(piece, dst.at[m * 8 + f], send.at[d], recv.at[d], fo, mo)

    return copy


def run_31(fn):
    def step(d, carry):
        fn(d)
        return carry

    lax.fori_loop(1, 32, step, 0)


WHOLE = ((2, 4, 1024, 384), (2, 4, 128, 1024), (2, 4, 1024, 512), (2, 4, 512, 1024))


def add_into(dst, src, step=64):
    rows = dst.shape[0]
    step = min(step, rows)

    def body(i, carry):
        r = pl.ds(pl.multiple_of(i * step, step), step)
        dst[r, :] = (dst[r, :].astype(F32) + src[r, :].astype(F32)).astype(BF16)
        return carry

    lax.fori_loop(0, rows // step, body, 0)


def fold_shapes():
    halves, blocks = [], []
    for (_, _, r, c), kind in zip(WHOLE, KINDS):
        halves.append((HALF, c) if kind == "rows" else (r, HALF))
        blocks.append((SIDE, c) if kind == "rows" else (r, SIDE))
    return halves, blocks


def fold_scratch():
    dma = pltpu.SemaphoreType.DMA
    halves, blocks = fold_shapes()
    return (
        [pltpu.VMEM((2, 4) + h, BF16) for h in halves]
        + [pltpu.VMEM((2, 2) + h, BF16) for h in halves]
        + [pltpu.VMEM((2,) + h, BF16) for h in halves]
        + [pltpu.VMEM((2, 3) + b, BF16) for b in blocks],
        [dma((4, 2, 4)), dma((4, 2, 4)), dma((4, 2, 2)), dma((4, 2, 2)), dma((4, 2)), dma((4, 2)),
         dma((4, 2, 3)), dma((4, 2, 3))],
    )


LOG2E = 1.4426950408889634
ERFC = (
    0.19566775565881125, 0.2262050475851227, 0.020554232590134225, 0.6380773756660296, -0.6389923965501372,
    0.7525645406195645, -0.19407655893061698,
)
NT = (((1,), (1,)), ((), ()))
TN = (((0,), (0,)), ((), ()))


def mm(a, b):
    return jnp.dot(a, b, preferred_element_type=F32)


def mm_nt(a, b):
    return lax.dot_general(a, b, NT, preferred_element_type=F32)


def mm_tn(a, b):
    return lax.dot_general(a, b, TN, preferred_element_type=F32)


def aligned(start, size):
    return pl.ds(pl.multiple_of(start, size), size)


def gelu_pair(u):
    x = jnp.abs(u) * 0.7071067811865476
    e = jnp.exp(x * x * -1.0)
    t = 1.0 / (1.0 + 0.35 * x)
    p = ERFC[6]
    for coef in ERFC[5::-1]:
        p = p * t + coef
    tail = 0.5 * (p * t) * e
    phi = jnp.where(u >= 0.0, 1.0 - tail, tail)
    return u * phi, phi + u * e * 0.3989422804014327


def column_copies(hbm, vmem, sems, store):
    copies = []
    for s in range(2):
        for p in range(8):
            f = (p % 4) * 2 + p // 4
            outside = hbm.at[s, :, pl.ds(f * SIDE, SIDE)]
            inside = vmem.at[pl.ds(s * L, L), pl.ds(p * SIDE, SIDE)]
            pair = (inside, outside) if store else (outside, inside)
            copies.append(pltpu.make_async_copy(pair[0], pair[1], sems.at[s, p]))
    return copies


def lane_half(value, e):
    lane = lax.broadcasted_iota(jnp.int32, (1, value.shape[1]), 1)
    return jnp.where((lane < 64) if e == 0 else (lane >= 64), value, jnp.zeros_like(value))


def row_mean(v):
    return jnp.sum(v, axis=1, keepdims=True) * (1.0 / D)


def forward_kernel(
    lens, x_hbm, cot_hbm, sqr, sor, sur, sdr, ob, g1, b1, db, g2, b2, ub, qb,
    y_hbm, wq_hbm, wo_hbm, wu_hbm, wd_hbm, qkv_hbm, p_hbm, mixed_hbm, lowh_hbm, n1_hbm, rs_hbm, act_hbm, gp_hbm,
    dpre_hbm, vec_out, gain_out,
    wq, wo, wu, wd, vec, x, sqp, sv, qst, pst, mixed, hid, lowh, act, gst, cot, yst, nst, rst, dst, dv, ubs, qvb,
    *sems,
):
    (vs, vr, xsem, csem, ysem, wsem, qsem, psem, msem, gsem, nsem, dsem, asem) = sems[9:]
    z, c, m = place()
    greet_all()
    shards = (
        [sqp.at[k] for k in range(2)],
        [sor.at[pl.ds(k * 128, 128), :] for k in range(2)],
        [sur.at[:, pl.ds(k * HALF, HALF)] for k in range(2)],
        [sdr.at[pl.ds(k * HALF, HALF), :] for k in range(2)],
    )
    for e in range(6):
        pair = e // 3
        part = e % 3
        a = sqr[:, (pair * 2) * 192 + part * 64:(pair * 2) * 192 + part * 64 + 64].astype(F32)
        b = sqr[:, (pair * 2 + 1) * 192 + part * 64:(pair * 2 + 1) * 192 + part * 64 + 64].astype(F32)
        sqp[pair, :, part * 128:part * 128 + 128] = jnp.concatenate([a, b], axis=1).astype(BF16)
    q1 = qb[...].astype(F32)
    zero = jnp.zeros((1, 128), F32)
    sv[...] = jnp.concatenate(
        [r[...].astype(F32) for r in (ob, g1, b1, db, g2, b2)] + [zero, zero, ub[...].astype(F32)]
        + [jnp.concatenate([q1, q1], axis=1), zero, zero, zero], axis=0
    ).astype(BF16)
    spread = Spread(shards, (wq, wo, wu, wd), sems[:9])
    spread.start(0)
    vcopy = swap_vectors(sv, vec, vs, vr, False)
    run_31(lambda d: vcopy(d).start())
    vec[m * 8 + z * 2 + c] = sv[...]
    for t in range(1, 4):
        spread.start(t)
    x_copies = column_copies(x_hbm, x, xsem, False)
    c_copies = column_copies(cot_hbm, cot, csem, False)
    for cp in x_copies + c_copies:
        cp.start()
    run_31(lambda d: vcopy(d).wait())
    for p in range(8):
        dv[:, p * SIDE:(p + 1) * SIDE] = vec[m * 8 + (p % 4) * 2 + p // 4].astype(F32)[0:8]
    for j in range(8):
        k, mm_ = j // 4, j % 4
        t = vec[m * 8 + mm_ * 2 + k].astype(F32)
        ubs[j] = jnp.concatenate([t[8:9], t[9:10], t[10:11], t[11:12]], axis=1)
        rows = [vec[mm_ * 8 + 4 * k + i].astype(F32)[12:13] for i in range(4)]
        lane = lax.broadcasted_iota(jnp.int32, (1, 128), 1)
        qvb[j] = jnp.concatenate(
            [jnp.where(lane < 64, rows[0], rows[2]), zero, jnp.where(lane < 64, rows[1], rows[3])], axis=1
        )
    for cp in x_copies + c_copies:
        cp.wait()
    wholes = ((wq, wq_hbm), (wo, wo_hbm), (wu, wu_hbm), (wd, wd_hbm))
    w_copies = [pltpu.make_async_copy(a, b, wsem.at[i]) for i, (a, b) in enumerate(wholes)]
    spread.stage(0, 0)
    spread.stage(0, 1)
    spread.stage(1, 0)
    spread.stage(0, 2)
    spread.stage(1, 1)
    spread.stage(0, 3)
    w_copies[0].start()
    spread.stage(2, 0)

    def q_copy(it):
        j, s = it // 2, it % 2
        return pltpu.make_async_copy(qst.at[s], qkv_hbm.at[j, aligned(s * L, L), :], qsem.at[s])

    def p_copy(it):
        j, s = it // 2, it % 2
        return pltpu.make_async_copy(pst.at[s], p_hbm.at[j, s], psem.at[s])

    def attend(it, carry):
        j, s = it // 2, it % 2
        rows = aligned(s * L, L)

        @pl.when(it >= 2)
        def _():
            q_copy(it - 2).wait()
            p_copy(it - 2).wait()

        qst[s] = (mm(x[rows, :], wq[j // 4, j % 4]) + qvb[j]).astype(BF16)
        q_copy(it).start()
        keys, values = qst[s, :, 128:256], qst[s, :, 256:384]
        length = lens[s, m]
        lane = lax.broadcasted_iota(jnp.int32, (1, L), 1)
        bias = jnp.where(lane < length, 0.0, -1e30)
        out = [None, None]
        for e in range(2):
            k_e, v_e = lane_half(keys, e), lane_half(values, e)
            for h in range(2):
                half = slice(h * 256, h * 256 + 256)
                scores = mm_nt(qst[s, half, 0:128], k_e) + bias
                top = jnp.max(scores, axis=1, keepdims=True)
                ex = jnp.exp2((scores - top) * (LOG2E * DH ** (-0.5)))
                probs = (ex * (1.0 / jnp.sum(ex, axis=1, keepdims=True))).astype(BF16)
                pst[s, e, half, :] = probs
                part = mm(probs, v_e)
                out[h] = part if out[h] is None else out[h] + part
        p_copy(it).start()
        mixed[rows, aligned(j * 128, 128)] = jnp.concatenate(out, axis=0).astype(BF16)

        @pl.when(it == 3)
        def _():
            spread.stage(1, 2)

        @pl.when(it == 6)
        def _():
            spread.stage(1, 3)
            w_copies[1].start()

        @pl.when(it == 9)
        def _():
            spread.stage(2, 1)

        @pl.when(it == 12)
        def _():
            spread.stage(3, 0)

        return carry

    lax.fori_loop(0, 16, attend, 0)
    for it in (14, 15):
        q_copy(it).wait()
        p_copy(it).wait()
    m_copy = pltpu.make_async_copy(mixed, mixed_hbm, msem.at[0])
    m_copy.start()

    def n_copy(i):
        return pltpu.make_async_copy(nst.at[i % 2], n1_hbm.at[aligned(i * 256, 256), :], nsem.at[i % 2])

    def r_copy(i):
        return pltpu.make_async_copy(rst.at[i % 2], rs_hbm.at[aligned(i * 256, 256), :], nsem.at[2 + i % 2])

    def first_norm(i, carry):
        rows = aligned(i * 256, 256)

        @pl.when(i >= 2)
        def _():
            n_copy(i - 2).wait()
            r_copy(i - 2).wait()

        pre = mm(mixed[rows, :], wo[...].reshape(D, D)) + dv[0:1] + x[rows, :].astype(F32)
        cen = pre - row_mean(pre)
        inv = lax.rsqrt(row_mean(cen * cen) + EPSILON)
        n = cen * inv
        nst[i % 2] = n
        rst[i % 2] = jnp.broadcast_to(inv, (256, 128))
        n_copy(i).start()
        r_copy(i).start()
        h = n * dv[1:2] + dv[2:3]
        hid[rows, :] = h
        lowh[rows, :] = h.astype(BF16)
        return carry

    lax.fori_loop(0, 4, first_norm, 0)
    spread.stage(2, 2)
    for i in (2, 3):
        n_copy(i).wait()
        r_copy(i).wait()
    h_copy = pltpu.make_async_copy(lowh, lowh_hbm, msem.at[1])
    h_copy.start()
    spread.stage(2, 3)
    w_copies[2].start()
    spread.stage(3, 1)

    def g_copy(it):
        j, r = it // 2, it % 2
        return pltpu.make_async_copy(gst.at[r], gp_hbm.at[j, aligned(r * L, L), :], gsem.at[r])

    def a_copy(it):
        j, r = it // 2, it % 2
        src = act.at[aligned(r * L, L), aligned(j * HALF, HALF)]
        return pltpu.make_async_copy(src, act_hbm.at[j, aligned(r * L, L), :], asem.at[it])

    def up(it, carry):
        j, r = it // 2, it % 2
        rows = aligned(r * L, L)

        @pl.when(it >= 2)
        def _():
            g_copy(it - 2).wait()

        w = wu[j // 4, j % 4]
        for h in range(2):
            sub = pl.ds(pl.multiple_of(r * L + h * 256, 256), 256)
            a, g = gelu_pair(mm(lowh[sub, :], w) + ubs[j])
            act[sub, aligned(j * HALF, HALF)] = a.astype(BF16)
            gst[r, h * 256:h * 256 + 256, :] = g.astype(BF16)
        g_copy(it).start()
        a_copy(it).start()

        @pl.when(it == 12)
        def _():
            spread.stage(3, 2)

        return carry

    lax.fori_loop(0, 16, up, 0)
    spread.stage(3, 3)
    w_copies[3].start()
    gain_out[...] = jnp.zeros((8, D), F32)

    def d_copy(i):
        return pltpu.make_async_copy(dst.at[i % 2], dpre_hbm.at[aligned(i * 256, 256), :], dsem.at[i % 2])

    def down(i, carry):
        rows = aligned(i * 256, 256)

        @pl.when(i >= 2)
        def _():
            d_copy(i - 2).wait()

        pre = mm(act[rows, :], wd[...].reshape(FF, D)) + dv[3:4] + hid[rows, :]
        cen = pre - row_mean(pre)
        inv = lax.rsqrt(row_mean(cen * cen) + EPSILON)
        n = cen * inv
        yst[rows, :] = (n * dv[4:5] + dv[5:6]).astype(BF16)
        pos = (i % 2) * 256 + lax.broadcasted_iota(jnp.int32, (256, 1), 0)
        grad = jnp.where(pos < lens[i // 2, m], cot[rows, :].astype(F32), 0.0)
        g = grad * dv[4:5]
        back = inv * (g - row_mean(g) - n * row_mean(g * n))
        dst[i % 2] = back
        d_copy(i).start()
        gain_out[3:4, :] += jnp.sum(back, axis=0, keepdims=True)
        gain_out[4:5, :] += jnp.sum(grad * n, axis=0, keepdims=True)
        gain_out[5:6, :] += jnp.sum(grad, axis=0, keepdims=True)
        return carry

    lax.fori_loop(0, 4, down, 0)
    y_copies = column_copies(y_hbm, yst, ysem, True)
    for cp in y_copies:
        cp.start()
    vec_out[...] = dv[...]
    for i in (2, 3):
        d_copy(i).wait()
    for it in (14, 15):
        g_copy(it).wait()

    def a_wait(it, carry):
        a_copy(it).wait()
        return carry

    lax.fori_loop(0, 16, a_wait, 0)
    m_copy.wait()
    h_copy.wait()
    for cp in y_copies + w_copies:
        cp.wait()
    for t in range(4):
        spread.drain(t)


SAVED = (
    ((8, 1024, 384), BF16), ((8, 2, 2, L, L), BF16), ((1024, D), BF16), ((1024, D), BF16), ((1024, D), F32),
    ((1024, 128), F32), ((8, 1024, HALF), BF16), ((8, 1024, HALF), BF16), ((1024, D), F32),
)


def forward(lengths, inputs, cotangent, weights, vectors):
    vm = pl.BlockSpec(memory_space=pltpu.VMEM)
    anywhere = pl.BlockSpec(memory_space=pl.ANY)
    shape = jax.ShapeDtypeStruct
    dma = pltpu.SemaphoreType.DMA
    v = pltpu.VMEM
    scratch = [v(s, BF16) for s in WHOLE] + [
        v((32, 16, 128), BF16), v((1024, D), BF16), v((2, 128, 384), BF16), v((16, 128), BF16), v((2, L, 384), BF16),
        v((2, 2, L, L), BF16), v((1024, D), BF16), v((1024, D), F32), v((1024, D), BF16), v((1024, FF), BF16),
        v((2, L, HALF), BF16), v((1024, D), BF16), v((1024, D), BF16), v((2, 256, D), F32), v((2, 256, 128), F32),
        v((2, 256, D), F32), v((8, D), F32), v((8, 1, HALF), F32), v((8, 1, 384), F32),
    ] + spread_sems() + [
        dma((32,)), dma((32,)), dma((2, 8)), dma((2, 8)), dma((2, 8)), dma((4,)), dma((2,)), dma((2,)), dma((2,)),
        dma((2,)), dma((4,)), dma((2,)), dma((16,)),
    ]
    return pl.pallas_call(
        forward_kernel,
        out_shape=[shape((2, L, D), BF16)] + [shape(s, BF16) for s in WHOLE] + [shape(s, d) for s, d in SAVED]
        + [shape((8, D), F32), shape((8, D), F32)],
        in_specs=[pl.BlockSpec(memory_space=pltpu.SMEM), anywhere, anywhere] + [vm] * 12,
        out_specs=[anywhere] * 14 + [vm, vm],
        scratch_shapes=scratch,
        compiler_params=pltpu.CompilerParams(collective_id=0, has_side_effects=True, vmem_limit_bytes=67000000),
    )(lengths, inputs, cotangent, *weights, *vectors)

class Fold:
    def __init__(self, rc, rx, ry, rz, sems):
        self.rc, self.rx, self.ry, self.rz = rc, rx, ry, rz
        self.cs, self.cr, self.xs, self.xr, self.ys, self.yr, self.zs, self.zr = sems
        self.z, self.c, self.m = place()

    def c_copy(self, t, k, off, src):
        return remote(
            src, self.rc[t].at[k, self.m ^ off], self.cs.at[t, k, off], self.cr.at[t, k, off],
            self.z * 2 + 1 - self.c, self.m,
        )

    def x_copy(self, t, k, i):
        m = self.m ^ (3 if i else 1 + k)
        return remote(
            self.rc[t].at[k, m], self.rx[t].at[k, i], self.xs.at[t, k, i], self.xr.at[t, k, i],
            self.z * 2 + self.c, self.m ^ (1 + k),
        )

    def y_copy(self, t, k):
        m = self.m ^ (2 - k)
        return remote(
            self.rc[t].at[k, m], self.ry[t].at[k], self.ys.at[t, k], self.yr.at[t, k], self.z * 2 + self.c, m
        )

    def z_copy(self, t, k, d):
        z = (self.z + d) % PLANES
        src = span(self.rc[t].at[k, self.m], KINDS[t], z * SIDE, SIDE)
        return remote(
            src, self.rz[t].at[k, d - 1], self.zs.at[t, k, d - 1], self.zr.at[t, k, d - 1], z * 2 + self.c, self.m
        )

    def to_y(self, t, k):
        self.x_copy(t, k, 1).wait_recv()
        add_into(self.rc[t].at[k, self.m ^ (2 - k)], self.rx[t].at[k, 1])
        self.y_copy(t, k).start()

    def to_z(self, t, k):
        self.x_copy(t, k, 0).wait_recv()
        add_into(self.rc[t].at[k, self.m], self.rx[t].at[k, 0])
        self.y_copy(t, k).wait_recv()
        add_into(self.rc[t].at[k, self.m], self.ry[t].at[k])
        for d in range(1, PLANES):
            self.z_copy(t, k, d).start()

    def total(self, t, k):
        for d in range(1, PLANES):
            self.z_copy(t, k, d).wait_recv()
        own = span(self.rc[t].at[k, self.m], KINDS[t], self.z * SIDE, SIDE)[...].astype(F32)
        rz = self.rz[t]
        return own + rz[k, 0].astype(F32) + rz[k, 1].astype(F32) + rz[k, 2].astype(F32)

    def drain(self, t, k):
        self.x_copy(t, k, 0).wait_send()
        self.x_copy(t, k, 1).wait_send()
        self.y_copy(t, k).wait_send()
        for d in range(1, PLANES):
            self.z_copy(t, k, d).wait_send()


def backward_kernel(
    x_hbm, wq_hbm, wo_hbm, wu_hbm, wd_hbm, qkv_hbm, p_hbm, mixed_hbm, lowh_hbm, n1_hbm, rs_hbm, act_hbm, gp_hbm,
    dpre_hbm, dv, gains,
    ig_hbm, oq, oo, ou, od, ov,
    *rest,
):
    rc, rx, ry, rz = rest[0:4], rest[4:8], rest[8:12], rest[12:16]
    (dbr, dh, low, wdj, wuj, ag, din, gd, gu, mixed, dmix, qkvj, dproj, nst, rst, rv, gv, sums, ubg, qvg) = rest[16:36]
    fold = Fold(rc, rx, ry, rz, rest[36:44])
    vs, vr, lsem, psem, ssem, nsem, isem, xsem = rest[44:]
    z, c, m = place()
    other = 1 - c
    mine, theirs = aligned(c * HALF, HALF), aligned(other * HALF, HALF)

    def turn(idx):
        k, p = idx % 2, idx // 2
        off = jnp.where(p == 0, 3, jnp.where(p == 1, 1 + k, jnp.where(p == 2, 2 - k, 0)))
        return k, p, off

    def ffn_loads(idx):
        k, _, off = turn(idx)
        mo, slot = m ^ off, idx % 2
        j = k * 4 + mo
        pairs = (
            (wd_hbm.at[k, mo], wdj.at[slot]), (act_hbm.at[j], ag.at[slot, 0]), (gp_hbm.at[j], ag.at[slot, 1]),
            (wu_hbm.at[k, mo], wuj.at[slot]),
        )
        return [pltpu.make_async_copy(a, b, lsem.at[slot, i]) for i, (a, b) in enumerate(pairs)]

    dp_copy = pltpu.make_async_copy(dpre_hbm, dh, ssem.at[0])
    dp_copy.start()
    for cp in ffn_loads(0):
        cp.start()
    lh_copy = pltpu.make_async_copy(lowh_hbm, low, ssem.at[1])
    lh_copy.start()
    mx_copy = pltpu.make_async_copy(mixed_hbm, mixed, ssem.at[2])
    mx_copy.start()
    greet_all()
    sums[...] = gains[...]
    dp_copy.wait()

    def cast(i, carry):
        rows = aligned(i * 128, 128)
        dbr[rows, :] = dh[rows, :].astype(BF16)
        return carry

    lax.fori_loop(0, 8, cast, 0)
    lh_copy.wait()

    def ffn(idx, carry):
        k, p, off = turn(idx)
        mo, slot = m ^ off, idx % 2
        for cp in ffn_loads(idx):
            cp.wait()

        @pl.when(idx < 7)
        def _():
            for cp in ffn_loads(idx + 1):
                cp.start()

        @pl.when(idx >= 2)
        def _():
            pk, _, poff = turn(idx - 2)
            fold.c_copy(3, pk, poff, gd.at[slot]).wait_send()
            fold.c_copy(2, pk, poff, gu.at[slot]).wait_send()

        total = jnp.zeros((1, HALF), F32)
        for r in range(2):
            rows = slice(r * L, r * L + L)
            d = (mm_nt(dbr[rows, :], wdj[slot]) * ag[slot, 1, rows, :].astype(F32)).astype(BF16)
            din[rows, :] = d
            total = total + jnp.sum(d.astype(F32), axis=0, keepdims=True)
        ubg[k * 4 + mo] = total
        gd[slot] = mm_tn(ag[slot, 0], dbr[:, theirs]).astype(BF16)
        fold.c_copy(3, k, off, gd.at[slot]).start()
        gu[slot] = mm_tn(low[:, theirs], din[...]).astype(BF16)
        fold.c_copy(2, k, off, gu.at[slot]).start()
        for r in range(2):
            for h in range(2):
                rows, cols = slice(r * L, r * L + L), slice(h * HALF, h * HALF + HALF)
                dh[rows, cols] += mm_nt(din[rows, :], wuj[slot, cols, :])
        fold.c_copy(3, k, off, gd.at[slot]).wait_recv()
        rc[3][k, mo] = (mm_tn(ag[slot, 0], dbr[:, mine]) + rc[3][k, mo].astype(F32)).astype(BF16)
        fold.c_copy(2, k, off, gu.at[slot]).wait_recv()
        rc[2][k, mo] = (mm_tn(low[:, mine], din[...]) + rc[2][k, mo].astype(F32)).astype(BF16)

        @pl.when(p == 0)
        def _():
            fold.x_copy(3, k, 1).start()
            fold.x_copy(2, k, 1).start()

        @pl.when(p == 1)
        def _():
            fold.x_copy(3, k, 0).start()
            fold.x_copy(2, k, 0).start()

        @pl.when(p == 2)
        def _():
            fold.to_y(3, k)
            fold.to_y(2, k)

        return carry

    lax.fori_loop(0, 8, ffn, 0)
    for idx in (6, 7):
        pk, pslot = idx % 2, idx % 2
        fold.c_copy(3, pk, 0, gd.at[pslot]).wait_send()
        fold.c_copy(2, pk, 0, gu.at[pslot]).wait_send()

    def norm_loads(i):
        rows, slot = aligned(i * 256, 256), i % 2
        return (
            pltpu.make_async_copy(n1_hbm.at[rows, :], nst.at[slot], nsem.at[slot, 0]),
            pltpu.make_async_copy(rs_hbm.at[rows, :], rst.at[slot], nsem.at[slot, 1]),
        )

    for cp in norm_loads(0):
        cp.start()
    wo_copies = [
        pltpu.make_async_copy(
            wo_hbm.at[j // 4, j % 4], wdj.at[j // 4, pl.ds((j % 4) * 128, 128), :], lsem.at[j // 4, j % 4]
        )
        for j in range(8)
    ]
    for cp in wo_copies:
        cp.start()
    x_copies = column_copies(x_hbm, low, xsem, False)
    for cp in x_copies:
        cp.start()

    def attn_loads(idx):
        k, _, off = turn(idx)
        j, slot = k * 4 + (m ^ off), idx % 2
        copies = [pltpu.make_async_copy(qkv_hbm.at[j], qkvj.at[slot], psem.at[slot, 4])]
        for s in range(2):
            for e in range(2):
                copies.append(
                    pltpu.make_async_copy(
                        p_hbm.at[j, s, e], ag.at[slot, s, pl.ds(e * L, L), :], psem.at[slot, 2 * s + e]
                    )
                )
        return copies

    for cp in attn_loads(0):
        cp.start()

    def first_back(i, carry):
        rows, slot = aligned(i * 256, 256), i % 2

        @pl.when(i < 3)
        def _():
            for cp in norm_loads(i + 1):
                cp.start()

        for cp in norm_loads(i):
            cp.wait()
        grad, n = dh[rows, :], nst[slot]
        g = grad * dv[1:2]
        inv = rst[slot][:, 0:1]
        back = inv * (g - row_mean(g) - n * row_mean(g * n))
        dh[rows, :] = back
        dbr[rows, :] = back.astype(BF16)
        sums[0:1, :] += jnp.sum(back, axis=0, keepdims=True)
        sums[1:2, :] += jnp.sum(grad * n, axis=0, keepdims=True)
        sums[2:3, :] += jnp.sum(grad, axis=0, keepdims=True)
        return carry

    lax.fori_loop(0, 4, first_back, 0)
    mx_copy.wait()
    for h in range(2):
        rows = slice(h * L, h * L + L)
        wuj[0, rows, :] = mm_tn(mixed[:, rows], dbr[:, theirs]).astype(BF16)
    for k in range(2):
        for off in range(4):
            src = wuj.at[0, aligned((k * 4 + (m ^ off)) * 128, 128), :]
            fold.c_copy(1, k, off, src).start()
    for cp in wo_copies:
        cp.wait()
    for h in range(2):
        rows = slice(h * L, h * L + L)
        for q in range(2):
            dmix[rows, q * L:q * L + L] = mm_nt(dbr[rows, :], wdj[q]).astype(BF16)
    for h in range(2):
        rows = slice(h * L, h * L + L)
        wuj[1, rows, :] = mm_tn(mixed[:, rows], dbr[:, mine]).astype(BF16)
    for k in range(2):
        for off in (3, 1 + k, 2 - k, 0):
            src = wuj.at[0, aligned((k * 4 + (m ^ off)) * 128, 128), :]
            fold.c_copy(1, k, off, src).wait()
            add_into(rc[1].at[k, m ^ off], wuj.at[1, aligned((k * 4 + (m ^ off)) * 128, 128), :])
            if off == 3:
                fold.x_copy(1, k, 1).start()
            elif off == 1 + k:
                fold.x_copy(1, k, 0).start()
    for cp in x_copies:
        cp.wait()

    def piece(idx):
        return gu.at[idx % 2, :, pl.ds(0, 384)]

    def attend(idx, s):
        k, _, off = turn(idx)
        mo, slot = m ^ off, idx % 2
        j = k * 4 + mo
        rows = slice(s * L, s * L + L)
        dout = dmix[rows, aligned(j * 128, 128)]
        queries, keys, values = (qkvj[slot, rows, i * 128:i * 128 + 128] for i in range(3))
        dq = dk = dval = None
        for e in range(2):
            probs = ag[slot, s, e * L:e * L + L, :]
            p32 = probs.astype(F32)
            t = p32 * mm_nt(dout, lane_half(values, e))
            ds = (t - p32 * jnp.sum(t, axis=1, keepdims=True)).astype(BF16)
            parts = (mm(ds, lane_half(keys, e)), mm_tn(ds, lane_half(queries, e)), mm_tn(probs, lane_half(dout, e)))
            dq, dk, dval = parts if e == 0 else (dq + parts[0], dk + parts[1], dval + parts[2])
        scale = DH ** (-0.5)
        out = jnp.concatenate([dq * scale, dk * scale, dval], axis=1).astype(BF16)
        dproj[idx, rows, :] = out
        return jnp.sum(out.astype(F32), axis=0, keepdims=True)

    def settle(idx):
        k, p, off = turn(idx)
        mo = m ^ off
        fold.c_copy(0, k, off, piece(idx)).wait()
        rc[0][k, mo] = (mm_tn(low[:, mine], dproj[idx]) + rc[0][k, mo].astype(F32)).astype(BF16)

        @pl.when(p == 0)
        def _():
            fold.x_copy(0, k, 1).start()

        @pl.when(p == 1)
        def _():
            fold.x_copy(0, k, 0).start()

        @pl.when(p == 2)
        def _():
            fold.to_y(0, k)

    def heads(idx, carry):
        k, p, off = turn(idx)
        j = k * 4 + (m ^ off)
        for cp in attn_loads(idx):
            cp.wait()

        @pl.when(idx < 7)
        def _():
            for cp in attn_loads(idx + 1):
                cp.start()

        first = attend(idx, 0)

        @pl.when(idx >= 1)
        def _():
            settle(idx - 1)

        qvg[j] = first + attend(idx, 1)
        gu[idx % 2, :, 0:384] = mm_tn(low[:, theirs], dproj[idx]).astype(BF16)
        fold.c_copy(0, k, off, piece(idx)).start()

        @pl.when(idx == 2)
        def _():
            fold.to_z(3, 1)
            fold.to_z(2, 1)

        @pl.when(idx == 3)
        def _():
            fold.to_z(3, 0)
            fold.to_z(2, 0)

        @pl.when(idx == 4)
        def _():
            fold.to_y(1, 0)
            fold.to_y(1, 1)

        @pl.when(idx == 6)
        def _():
            fold.to_z(1, 0)
            fold.to_z(1, 1)

        return carry

    lax.fori_loop(0, 8, heads, 0)

    def wq_load(idx):
        k, _, off = turn(idx)
        return pltpu.make_async_copy(wq_hbm.at[k, m ^ off], qkvj.at[idx % 2], psem.at[idx % 2, 4])

    wq_load(0).start()
    wq_load(1).start()
    settle(7)
    for k in range(2):
        fold.to_z(0, k)
    for f in range(8):
        p = (f % 2) * 4 + f // 2
        wide = sums[:, p * SIDE:(p + 1) * SIDE]
        ub = ubg[(f % 2) * 4 + f // 2]
        pad = jnp.zeros((3, 128), F32)
        for mo in range(4):
            kk, e, part = f // 4, (f // 2) % 2, f % 2
            qv = qvg[kk * 4 + mo][:, part * 256 + e * 64:part * 256 + e * 64 + 64]
            gv[mo * 8 + f] = jnp.concatenate(
                [wide] + [ub[:, i * 128:i * 128 + 128] for i in range(4)] + [jnp.concatenate([qv, qv], axis=1), pad],
                axis=0,
            )
    vcopy = swap_vectors(gv, rv, vs, vr, True)
    run_31(lambda d: vcopy(d).start())
    me = m * 8 + z * 2 + c
    rv[me] = gv[me]

    def pull(idx, carry):
        slot = idx % 2
        wq_load(idx).wait()
        for r in range(2):
            for h in range(2):
                rows, cols = slice(r * L, r * L + L), slice(h * HALF, h * HALF + HALF)
                dh[rows, cols] += mm_nt(dproj[idx, rows, :], qkvj[slot, cols, :])

        @pl.when(idx < 6)
        def _():
            wq_load(idx + 2).start()

        return carry

    lax.fori_loop(0, 8, pull, 0)
    i_copies = column_copies(ig_hbm, dh, isem, True)
    for cp in i_copies:
        cp.start()
    run_31(lambda d: vcopy(d).wait())

    def gather_sum(i, acc):
        return acc + rv[i]

    ov[...] = lax.fori_loop(0, 32, gather_sum, jnp.zeros((16, 128), F32))
    for k in range(2):
        od[k * HALF:k * HALF + HALF, :] = fold.total(3, k)
        ou[:, k * HALF:k * HALF + HALF] = fold.total(2, k)
        oo[k * 128:k * 128 + 128, :] = fold.total(1, k)
        t = fold.total(0, k)
        parts = [t[:, i * 128 + e * 64:i * 128 + e * 64 + 64] for e in range(2) for i in range(3)]
        oq[:, k * 384:k * 384 + 384] = jnp.concatenate(parts, axis=1)
    for cp in i_copies:
        cp.wait()
    for t in range(4):
        for k in range(2):
            fold.drain(t, k)


def backward(inputs, weights, saved, dv, gains):
    vm = pl.BlockSpec(memory_space=pltpu.VMEM)
    anywhere = pl.BlockSpec(memory_space=pl.ANY)
    shape = jax.ShapeDtypeStruct
    dma = pltpu.SemaphoreType.DMA
    v = pltpu.VMEM
    bufs, sems = fold_scratch()
    scratch = bufs + [
        v((1024, D), BF16), v((1024, D), F32), v((1024, D), BF16), v((2, HALF, D), BF16), v((2, D, HALF), BF16),
        v((2, 2, 1024, HALF), BF16), v((1024, HALF), BF16), v((2, HALF, HALF), BF16), v((2, HALF, HALF), BF16),
        v((1024, D), BF16), v((1024, D), BF16), v((2, 1024, 384), BF16), v((8, 1024, 384), BF16),
        v((2, 256, D), F32), v((2, 256, 128), F32), v((32, 16, 128), F32), v((32, 16, 128), F32), v((8, D), F32),
        v((8, 1, HALF), F32), v((8, 1, 384), F32),
    ] + sems + [
        dma((32,)), dma((32,)), dma((2, 4)), dma((2, 5)), dma((3,)), dma((2, 2)), dma((2, 8)), dma((2, 8)),
    ]
    return pl.pallas_call(
        backward_kernel,
        out_shape=[
            shape((2, L, D), F32), shape((128, 768), F32), shape((256, 128), F32), shape((128, 1024), F32),
            shape((1024, 128), F32), shape((16, 128), F32),
        ],
        in_specs=[anywhere] * 14 + [vm, vm],
        out_specs=[anywhere] + [vm] * 5,
        scratch_shapes=scratch,
        compiler_params=pltpu.CompilerParams(collective_id=1, has_side_effects=True, vmem_limit_bytes=67000000),
    )(inputs, *weights, *saved, dv, gains)

def fast_body(
    inputs, lengths, qkv_weight, qv_bias, out_weight, out_bias, norm1_gain, norm1_bias, up_weight, up_bias,
    down_weight, down_bias, norm2_gain, norm2_bias, cotangent,
):
    row = lambda v: v.reshape(1, 128)
    results = forward(
        lengths, inputs, cotangent, (qkv_weight, out_weight, up_weight, down_weight),
        (row(out_bias), row(norm1_gain), row(norm1_bias), row(down_bias), row(norm2_gain), row(norm2_bias),
         up_bias.reshape(4, 128), qv_bias.reshape(1, 64)),
    )
    input_grad, oq, oo, ou, od, ov = backward(inputs, results[1:5], results[5:14], results[14], results[15])
    return (
        results[0],
        input_grad,
        oq,
        ov[12, :64],
        oo,
        ov[0],
        ov[1],
        ov[2],
        ou,
        ov[8:12].reshape(512),
        od,
        ov[3],
        ov[4],
        ov[5],
    )


def solution(mesh):
    placed = (
        P(None, ("fsdp", "mp"), None),
        P(None, "fsdp"),
        P("fsdp", "mp"),
        P(("mp", "fsdp")),
        P("mp", "fsdp"),
        P("fsdp"),
        P("fsdp"),
        P("fsdp"),
        P("fsdp", "mp"),
        P("fsdp"),
        P("mp", "fsdp"),
        P("fsdp"),
        P("fsdp"),
        P("fsdp"),
        P(None, ("fsdp", "mp"), None),
    )
    blocks_fit = mesh.shape["fsdp"] == 8 and mesh.shape["mp"] == 4
    return jax.shard_map(
        fast_body if blocks_fit else generic_body,
        mesh=mesh,
        in_specs=placed,
        out_specs=(
            P(None, ("fsdp", "mp"), None),
            P(None, ("fsdp", "mp"), None),
            P("fsdp", "mp"),
            P(("mp", "fsdp")),
            P("mp", "fsdp"),
            P("fsdp"),
            P("fsdp"),
            P("fsdp"),
            P("fsdp", "mp"),
            P("fsdp"),
            P("mp", "fsdp"),
            P("fsdp"),
            P("fsdp"),
            P("fsdp"),
        ),
        check_vma=False,
    )
```

```python
from functools import partial

import jax
import jax.numpy as jnp
from jax import lax
from jax.experimental import pallas as pl
from jax.experimental.pallas import tpu as pltpu
from jax.sharding import PartitionSpec as P

D = 1024
DH = 64
FF = 4096
L = 512
MBS = 2


EPSILON = 1e-06
CONTRACT_ROWS = (((0,), (0,)), ((), ()))
CONTRACT_COLS = (((1,), (1,)), ((), ()))


def normalize(values, scale_vec, shift_vec):
    row_mean = jnp.mean(values, axis=-1, keepdims=True)
    centered = values - row_mean
    spread = jnp.mean(centered * centered, axis=-1, keepdims=True)
    return centered * lax.rsqrt(spread + EPSILON) * scale_vec + shift_vec


def gelu_exact(values):
    return jax.nn.gelu(values, approximate=False)


def collect_forward(shards):
    return (
        lax.all_gather(shards[0], "fsdp", axis=0, tiled=True),
        lax.all_gather(shards[1], "fsdp", axis=0, tiled=True),
        lax.all_gather(shards[2], "fsdp", axis=1, tiled=True),
        lax.all_gather(shards[3], "fsdp", axis=0, tiled=True),
        lax.all_gather(shards[4], "fsdp", axis=0, tiled=True),
        lax.all_gather(shards[5], "fsdp", axis=0, tiled=True),
        lax.all_gather(shards[6], "fsdp", axis=0, tiled=True),
        lax.all_gather(shards[7], "fsdp", axis=0, tiled=True),
        lax.all_gather(shards[8], "fsdp", axis=1, tiled=True),
        lax.all_gather(shards[9], "fsdp", axis=0, tiled=True),
        lax.all_gather(shards[10], "fsdp", axis=0, tiled=True),
        lax.all_gather(shards[11], "fsdp", axis=0, tiled=True),
    )


def collect_backward(shards):
    return (
        lax.all_gather(shards[0], "fsdp", axis=0, tiled=True),
        lax.all_gather(shards[2], "fsdp", axis=1, tiled=True),
        lax.all_gather(shards[4], "fsdp", axis=0, tiled=True),
        lax.all_gather(shards[6], "fsdp", axis=0, tiled=True),
        lax.all_gather(shards[8], "fsdp", axis=1, tiled=True),
        lax.all_gather(shards[10], "fsdp", axis=0, tiled=True),
    )


def attend_forward(packed, scale_value):
    queries, keysets, values, seq_len = packed
    scores = (
        jnp.einsum("qhe,khe->hqk", queries, keysets, preferred_element_type=jnp.float32)
        * scale_value
    )
    live_mask = jnp.arange(scores.shape[-1])[None, None, :] < seq_len
    scores = jnp.where(live_mask, scores, -1000000000.0)
    row_max = jnp.max(scores, axis=-1, keepdims=True)
    exp_scores = jnp.exp(scores - row_max)
    denom_sum = jnp.sum(exp_scores, axis=-1, keepdims=True)
    attn_probs = (exp_scores / denom_sum).astype(jnp.bfloat16)
    mixed_heads = jnp.einsum("hqk,khe->qhe", attn_probs, values, preferred_element_type=jnp.float32)
    return (mixed_heads.astype(jnp.bfloat16), (row_max + jnp.log(denom_sum))[:, :, 0])


def attend_backward(packed, scale_value):
    queries, keysets, values, seq_len, log_sums, d_mixed = packed
    scores = (
        jnp.einsum("qhe,khe->hqk", queries, keysets, preferred_element_type=jnp.float32)
        * scale_value
    )
    live_mask = jnp.arange(scores.shape[-1])[None, None, :] < seq_len
    attn_probs = jnp.where(live_mask, jnp.exp(scores - log_sums[:, :, None]), 0.0)
    low_probs = attn_probs.astype(jnp.bfloat16)
    d_value = jnp.einsum("hqk,qhe->khe", low_probs, d_mixed, preferred_element_type=jnp.float32)
    d_probs = jnp.einsum("qhe,khe->hqk", d_mixed, values, preferred_element_type=jnp.float32)
    row_delta = jnp.sum(attn_probs * d_probs, axis=-1, keepdims=True)
    d_scores = (attn_probs * (d_probs - row_delta)).astype(jnp.bfloat16)
    d_query = (
        jnp.einsum("hqk,khe->qhe", d_scores, keysets, preferred_element_type=jnp.float32)
        * scale_value
    )
    d_key = (
        jnp.einsum("hqk,qhe->khe", d_scores, queries, preferred_element_type=jnp.float32)
        * scale_value
    )
    return jnp.stack([d_query, d_key, d_value], axis=2).astype(jnp.bfloat16)


def generic_body(
    inputs,
    lengths,
    qkv_weight,
    qv_bias,
    out_weight,
    out_bias,
    norm1_gain,
    norm1_bias,
    up_weight,
    up_bias,
    down_weight,
    down_bias,
    norm2_gain,
    norm2_bias,
    cotangent,
):
    shards = (
        qkv_weight,
        qv_bias,
        out_weight,
        out_bias,
        norm1_gain,
        norm1_bias,
        up_weight,
        up_bias,
        down_weight,
        down_bias,
        norm2_gain,
        norm2_bias,
    )
    row_count = inputs.shape[1]
    mp_count = lax.axis_size("mp")
    mp_index = lax.axis_index("mp")
    up_cols = up_weight.shape[1]
    scale_value = DH ** (-0.5)
    group_rows = row_count * mp_count
    head_count = qkv_weight.shape[1] // (3 * DH)
    row_ids = mp_index * row_count + jnp.arange(row_count)
    seq_count = group_rows // L
    head_width = head_count * DH
    seq_ids = row_ids // L
    positions = row_ids % L
    seq_match = seq_ids[:, None] == jnp.arange(seq_count)[None, :]
    grad_qkv = jnp.zeros((D, 3 * head_width), jnp.float32)
    grad_qvb = jnp.zeros((2 * head_width,), jnp.float32)
    grad_out = jnp.zeros((head_width, D), jnp.float32)
    grad_up = jnp.zeros((D, up_cols), jnp.float32)
    grad_down = jnp.zeros((up_cols, D), jnp.float32)
    grad_upb = jnp.zeros((FF,), jnp.float32)
    grad_outb = jnp.zeros((D,), jnp.float32)
    grad_gain1 = jnp.zeros((D,), jnp.float32)
    grad_shift1 = jnp.zeros((D,), jnp.float32)
    grad_downb = jnp.zeros((D,), jnp.float32)
    grad_gain2 = jnp.zeros((D,), jnp.float32)
    grad_shift2 = jnp.zeros((D,), jnp.float32)
    layer_rows = []
    input_rows = []
    for micro_idx in range(MBS):
        fwd_set = collect_forward(shards)
        qkv_full, qvb_full, out_full, outb_full = (fwd_set[0], fwd_set[1], fwd_set[2], fwd_set[3])
        gain_one = fwd_set[4].astype(jnp.float32)
        shift_one = fwd_set[5].astype(jnp.float32)
        up_full, upb_full, down_full = (fwd_set[6], fwd_set[7].astype(jnp.float32), fwd_set[8])
        downb_full = fwd_set[9].astype(jnp.float32)
        gain_two = fwd_set[10].astype(jnp.float32)
        shift_two = fwd_set[11].astype(jnp.float32)
        tokens = inputs[micro_idx]
        upb_used = lax.dynamic_slice_in_dim(upb_full, mp_index * up_cols, up_cols, 0)
        gathered = lax.all_gather(tokens, "mp", axis=0, tiled=True)
        seq_lens = lengths[micro_idx]
        pair_bias = qvb_full.astype(jnp.float32).reshape(head_count, 2, DH)
        bias_full = jnp.stack(
            [pair_bias[:, 0], jnp.zeros_like(pair_bias[:, 0]), pair_bias[:, 1]], axis=1
        )
        project = jnp.dot(
            gathered, qkv_full, preferred_element_type=jnp.float32
        ) + bias_full.reshape(3 * head_width)
        project = project.astype(jnp.bfloat16).reshape(seq_count, L, head_count, 3, DH)
        queries = project[:, :, :, 0]
        keysets = project[:, :, :, 1]
        values = project[:, :, :, 2]
        mixed_heads, log_sums = lax.map(
            partial(attend_forward, scale_value=scale_value), (queries, keysets, values, seq_lens)
        )
        mixed_flat = mixed_heads.reshape(group_rows, head_width)
        attn_own = lax.psum_scatter(
            jnp.dot(mixed_flat, out_full, preferred_element_type=jnp.float32).astype(jnp.bfloat16),
            "mp",
            scatter_dimension=0,
            tiled=True,
        ).astype(jnp.float32)
        pre_norm1 = attn_own + outb_full.astype(jnp.float32) + tokens.astype(jnp.float32)
        hidden = normalize(pre_norm1, gain_one, shift_one)
        low_hidden = hidden.astype(jnp.bfloat16)
        ffn_rows = lax.all_gather(low_hidden, "mp", axis=0, tiled=True)
        inner_sum = jnp.dot(ffn_rows, up_full, preferred_element_type=jnp.float32) + upb_used
        activated = gelu_exact(inner_sum).astype(jnp.bfloat16)
        branch = lax.psum_scatter(
            jnp.dot(activated, down_full, preferred_element_type=jnp.float32).astype(jnp.bfloat16),
            "mp",
            scatter_dimension=0,
            tiled=True,
        ).astype(jnp.float32)
        pre_norm2 = branch + downb_full + hidden
        layer_rows.append(normalize(pre_norm2, gain_two, shift_two).astype(jnp.bfloat16))
        bwd_set = collect_backward(shards)
        qkv_back, out_back = (bwd_set[0], bwd_set[1])
        gain_one_back = bwd_set[2].astype(jnp.float32)
        up_back, down_back = (bwd_set[3], bwd_set[4])
        gain_two_back = bwd_set[5].astype(jnp.float32)
        row_len = jnp.sum(jnp.where(seq_match, seq_lens[None, :], 0), axis=1)
        live_rows = (positions < row_len).astype(jnp.float32)
        grad_rows = cotangent[micro_idx].astype(jnp.float32) * live_rows[:, None]
        _, pull_two = jax.vjp(normalize, pre_norm2, gain_two_back, shift_two)
        d_pre2, d_gain2, d_shift2 = pull_two(grad_rows)
        grad_gain2 = grad_gain2 + d_gain2
        grad_shift2 = grad_shift2 + d_shift2
        grad_downb = grad_downb + jnp.sum(d_pre2, axis=0)
        d_branch = d_pre2.astype(jnp.bfloat16)
        d_rows = lax.all_gather(d_branch, "mp", axis=0, tiled=True)
        d_act = lax.dot_general(
            d_rows, down_back, CONTRACT_COLS, preferred_element_type=jnp.float32
        )
        grad_down = grad_down + lax.dot_general(
            activated, d_rows, CONTRACT_ROWS, preferred_element_type=jnp.float32
        )
        _, pull_gelu = jax.vjp(gelu_exact, inner_sum)
        d_inner = pull_gelu(d_act)[0].astype(jnp.bfloat16)
        bias_term = jnp.sum(d_inner.astype(jnp.float32), axis=0)
        grad_up = grad_up + lax.dot_general(
            ffn_rows, d_inner, CONTRACT_ROWS, preferred_element_type=jnp.float32
        )
        grad_upb = grad_upb + lax.dynamic_update_slice_in_dim(
            jnp.zeros((FF,), jnp.float32), bias_term, mp_index * up_cols, 0
        )
        d_hidden_part = lax.psum_scatter(
            lax.dot_general(
                d_inner, up_back, CONTRACT_COLS, preferred_element_type=jnp.float32
            ).astype(jnp.bfloat16),
            "mp",
            scatter_dimension=0,
            tiled=True,
        ).astype(jnp.float32)
        d_hidden = d_pre2 + d_hidden_part
        _, pull_one = jax.vjp(normalize, pre_norm1, gain_one_back, shift_one)
        d_pre1, d_gain1, d_shift1 = pull_one(d_hidden)
        grad_gain1 = grad_gain1 + d_gain1
        grad_shift1 = grad_shift1 + d_shift1
        grad_outb = grad_outb + jnp.sum(d_pre1, axis=0)
        d_attended = d_pre1.astype(jnp.bfloat16)
        d_attn_rows = lax.all_gather(d_attended, "mp", axis=0, tiled=True)
        d_mixed = lax.dot_general(
            d_attn_rows, out_back, CONTRACT_COLS, preferred_element_type=jnp.float32
        )
        d_mixed = d_mixed.astype(jnp.bfloat16)
        grad_out = grad_out + lax.dot_general(
            mixed_flat, d_attn_rows, CONTRACT_ROWS, preferred_element_type=jnp.float32
        )
        d_project = lax.map(
            partial(attend_backward, scale_value=scale_value),
            (
                queries,
                keysets,
                values,
                seq_lens,
                log_sums,
                d_mixed.reshape(seq_count, L, head_count, DH),
            ),
        )
        d_flat = d_project.reshape(group_rows, 3 * head_width)
        grad_qkv = grad_qkv + lax.dot_general(
            gathered, d_flat, CONTRACT_ROWS, preferred_element_type=jnp.float32
        )
        bias_parts = jnp.sum(d_flat.astype(jnp.float32), axis=0).reshape(head_count, 3, DH)
        grad_qvb = grad_qvb + jnp.stack([bias_parts[:, 0], bias_parts[:, 2]], axis=1).reshape(
            2 * head_width
        )
        input_rows.append(
            d_pre1
            + lax.psum_scatter(
                lax.dot_general(
                    d_flat, qkv_back, CONTRACT_COLS, preferred_element_type=jnp.float32
                ).astype(jnp.bfloat16),
                "mp",
                scatter_dimension=0,
                tiled=True,
            ).astype(jnp.float32)
        )
    summed = (
        lax.psum_scatter(
            grad_qkv.astype(jnp.bfloat16), "fsdp", scatter_dimension=0, tiled=True
        ).astype(jnp.float32),
        lax.psum_scatter(
            grad_qvb.astype(jnp.bfloat16), "fsdp", scatter_dimension=0, tiled=True
        ).astype(jnp.float32),
        lax.psum_scatter(
            grad_out.astype(jnp.bfloat16), "fsdp", scatter_dimension=1, tiled=True
        ).astype(jnp.float32),
        lax.psum_scatter(
            grad_outb.astype(jnp.bfloat16), "fsdp", scatter_dimension=0, tiled=True
        ).astype(jnp.float32),
        lax.psum_scatter(
            grad_gain1.astype(jnp.bfloat16), "fsdp", scatter_dimension=0, tiled=True
        ).astype(jnp.float32),
        lax.psum_scatter(
            grad_shift1.astype(jnp.bfloat16), "fsdp", scatter_dimension=0, tiled=True
        ).astype(jnp.float32),
        lax.psum_scatter(
            grad_up.astype(jnp.bfloat16), "fsdp", scatter_dimension=0, tiled=True
        ).astype(jnp.float32),
        lax.psum_scatter(
            grad_upb.astype(jnp.bfloat16), "fsdp", scatter_dimension=0, tiled=True
        ).astype(jnp.float32),
        lax.psum_scatter(
            grad_down.astype(jnp.bfloat16), "fsdp", scatter_dimension=1, tiled=True
        ).astype(jnp.float32),
        lax.psum_scatter(
            grad_downb.astype(jnp.bfloat16), "fsdp", scatter_dimension=0, tiled=True
        ).astype(jnp.float32),
        lax.psum_scatter(
            grad_gain2.astype(jnp.bfloat16), "fsdp", scatter_dimension=0, tiled=True
        ).astype(jnp.float32),
        lax.psum_scatter(
            grad_shift2.astype(jnp.bfloat16), "fsdp", scatter_dimension=0, tiled=True
        ).astype(jnp.float32),
    )
    vectors = lax.psum(
        (summed[3], summed[4], summed[5], summed[7], summed[9], summed[10], summed[11]), "mp"
    )
    return (
        jnp.stack(layer_rows),
        jnp.stack(input_rows),
        summed[0],
        summed[1],
        summed[2],
        vectors[0],
        vectors[1],
        vectors[2],
        summed[6],
        vectors[3],
        summed[8],
        vectors[4],
        vectors[5],
        vectors[6],
    )


MESH_ID = pl.DeviceIdType.MESH
F32 = jnp.float32
BF16 = jnp.bfloat16
PLANES = 4
SIDE = 128
HALF = 512
KINDS = ("rows", "cols", "rows", "cols")
FIRST = (1, 2)
SECOND = (2, 1)


def place():
    f = lax.axis_index("fsdp")
    return f // 2, f % 2, lax.axis_index("mp")


def span(ref, kind, start, size):
    start = pl.multiple_of(start, SIDE)
    if kind == "rows":
        return ref.at[pl.ds(start, size), :]
    return ref.at[:, pl.ds(start, size)]


def remote(src, dst, send, recv, f, m):
    return pltpu.make_async_remote_copy(
        src_ref=src, dst_ref=dst, send_sem=send, recv_sem=recv, device_id=(f, m), device_id_type=MESH_ID
    )


def greet_all(between=None):
    z, c, m = place()
    me = (z * 2 + c) * 4 + m
    barrier = pltpu.get_barrier_semaphore()

    def hello(d, carry):
        other = (me + d) % 32
        pl.semaphore_signal(barrier, inc=1, device_id=(other // 4, other % 4), device_id_type=MESH_ID)
        return carry

    lax.fori_loop(1, 32, hello, 0)
    if between is not None:
        between()
    pl.semaphore_wait(barrier, 31)


ROWS_A = 320
ROWS_B = 192


class Spread:
    def __init__(self, shards, wholes, sems):
        self.shards, self.wholes = shards, wholes
        self.zs, self.zr, self.xs, self.xr, self.ys, self.yr, self.cs, self.cr, self.own = sems
        self.z, self.c, self.m = place()
        self.f = self.z * 2 + self.c

    def window(self, t, k, m, start, size):
        start = pl.multiple_of(start, SIDE)
        if t == 3:
            return self.wholes[3].at[k, m, pl.ds(0, ROWS_A), pl.ds(start, size)]
        if t == 4:
            return self.wholes[3].at[k, m, pl.ds(ROWS_A, ROWS_B), pl.ds(start, size)]
        return span(self.wholes[t].at[k, m], KINDS[t], start, size)

    def block(self, t, k):
        return self.window(t, k, self.m, self.c * HALF + self.z * SIDE, SIDE)

    def z_copy(self, t, k, d):
        z = (self.z + d) % PLANES
        return remote(
            self.shards[t][k], self.block(t, k), self.zs.at[t, k, d - 1], self.zr.at[t, k, d - 1], z * 2 + self.c, self.m
        )

    def own_copy(self, t, k):
        return pltpu.make_async_copy(self.shards[t][k], self.block(t, k), self.own.at[t, k])

    def x_copy(self, t, k):
        blk = self.window(t, k, self.m, self.c * HALF, HALF)
        return remote(blk, blk, self.xs.at[t, k], self.xr.at[t, k], self.f, self.m ^ FIRST[k])

    def y_copy(self, t, k, i):
        blk = self.window(t, k, self.m ^ (FIRST[k] if i else 0), self.c * HALF, HALF)
        return remote(blk, blk, self.ys.at[t, k, i], self.yr.at[t, k, i], self.f, self.m ^ SECOND[k])

    def c_copy(self, t, k, off):
        blk = self.window(t, k, self.m ^ off, self.c * HALF, HALF)
        return remote(blk, blk, self.cs.at[t, k, off], self.cr.at[t, k, off], self.z * 2 + 1 - self.c, self.m)

    def start(self, t, k):
        for d in range(1, PLANES):
            self.z_copy(t, k, d).start()
        self.own_copy(t, k).start()

    def enter(self, t, k):
        self.own_copy(t, k).wait()
        for d in range(1, PLANES):
            self.z_copy(t, k, d).wait_recv()
        self.x_copy(t, k).start()
        self.c_copy(t, k, 0).start()

    def second(self, t, k):
        self.y_copy(t, k, 0).start()

    def relay(self, t, k):
        self.x_copy(t, k).wait_recv()
        self.y_copy(t, k, 1).start()
        self.c_copy(t, k, FIRST[k]).start()

    def cross(self, t, k, i):
        self.y_copy(t, k, i).wait_recv()
        self.c_copy(t, k, 3 if i else SECOND[k]).start()

    def late_x(self, k):
        blk = self.block(4, k)
        return remote(self.shards[4][k], blk, self.xs.at[4, k], self.xr.at[4, k], self.f, self.m ^ FIRST[k])

    def late_y(self, k, i):
        dst = self.window(4, k, self.m ^ (FIRST[k] if i else 0), self.c * HALF + self.z * SIDE, SIDE)
        src = dst if i else self.shards[4][k]
        return remote(src, dst, self.ys.at[4, k, i], self.yr.at[4, k, i], self.f, self.m ^ SECOND[k])

    def plane(self, k, start, size):
        return self.wholes[3].at[k, :, pl.ds(ROWS_A, ROWS_B), pl.ds(pl.multiple_of(start, SIDE), size)]

    def late_z(self, k, d):
        z = (self.z + d) % PLANES
        blk = self.plane(k, self.c * HALF + self.z * SIDE, SIDE)
        return remote(blk, blk, self.zs.at[4, k, d - 1], self.zr.at[4, k, d - 1], z * 2 + self.c, self.m)

    def late_c(self, k):
        blk = self.plane(k, self.c * HALF, HALF)
        return remote(blk, blk, self.cs.at[4, k, 0], self.cr.at[4, k, 0], self.z * 2 + 1 - self.c, self.m)

    def late_start(self):
        for k in range(2):
            self.late_x(k).start()
            self.late_y(k, 0).start()
            self.own_copy(4, k).start()

    def late_relay(self):
        for k in range(2):
            self.late_x(k).wait_recv()
            self.late_y(k, 1).start()

    def late_planes(self):
        for k in range(2):
            self.own_copy(4, k).wait()
            self.late_y(k, 0).wait_recv()
            self.late_y(k, 1).wait_recv()
            for d in range(1, PLANES):
                self.late_z(k, d).start()

    def late_cross(self):
        for k in range(2):
            for d in range(1, PLANES):
                self.late_z(k, d).wait_recv()
            self.late_c(k).start()

    def drain(self):
        for k in range(2):
            for t in range(4):
                for d in range(1, PLANES):
                    self.z_copy(t, k, d).wait_send()
                self.x_copy(t, k).wait_send()
                self.y_copy(t, k, 0).wait_send()
                self.y_copy(t, k, 1).wait_send()
                for off in range(4):
                    self.c_copy(t, k, off).wait_send()
            self.late_x(k).wait_send()
            self.late_y(k, 0).wait_send()
            self.late_y(k, 1).wait_send()
            for d in range(1, PLANES):
                self.late_z(k, d).wait_send()
            self.late_c(k).wait_send()


def spread_sems():
    dma = pltpu.SemaphoreType.DMA
    return [
        dma((5, 2, 3)), dma((5, 2, 3)), dma((5, 2)), dma((5, 2)), dma((5, 2, 2)), dma((5, 2, 2)),
        dma((5, 2, 4)), dma((5, 2, 4)), dma((5, 2)),
    ]


def swap_vectors(src, dst, send, recv, chunked):
    z, c, m = place()
    f = z * 2 + c
    me = f * 4 + m

    def copy(d):
        other = (me + d) % 32
        fo, mo = other // 4, other % 4
        piece = src.at[mo * 8 + fo] if chunked else src
        return remote(piece, dst.at[m * 8 + f], send.at[d], recv.at[d], fo, mo)

    return copy


def run_31(fn):
    def step(d, carry):
        fn(d)
        return carry

    lax.fori_loop(1, 32, step, 0)


WHOLE = ((2, 4, 1024, 384), (2, 4, 128, 1024), (2, 4, 1024, 512), (2, 4, 512, 1024))


def add_into(dst, src, step=64):
    rows = dst.shape[0]
    step = min(step, rows)

    def body(i, carry):
        r = pl.ds(pl.multiple_of(i * step, step), step)
        dst[r, :] = (dst[r, :].astype(F32) + src[r, :].astype(F32)).astype(BF16)
        return carry

    lax.fori_loop(0, rows // step, body, 0)


def fold_shapes():
    halves, blocks = [], []
    for (_, _, r, c), kind in zip(WHOLE, KINDS):
        halves.append((HALF, c) if kind == "rows" else (r, HALF))
        blocks.append((SIDE, c) if kind == "rows" else (r, SIDE))
    return halves, blocks


def fold_scratch():
    dma = pltpu.SemaphoreType.DMA
    halves, blocks = fold_shapes()
    return (
        [pltpu.VMEM((2, 4) + h, BF16) for h in halves]
        + [pltpu.VMEM((2, 2) + h, BF16) for h in halves]
        + [pltpu.VMEM((2,) + h, BF16) for h in halves]
        + [pltpu.VMEM((2, 3) + b, BF16) for b in blocks],
        [dma((4, 2, 4)), dma((4, 2, 4)), dma((4, 2, 2)), dma((4, 2, 2)), dma((4, 2)), dma((4, 2)),
         dma((4, 2, 3)), dma((4, 2, 3))],
    )


LOG2E = 1.4426950408889634
ERFC_P = 0.4
ERFC = (
    0.11596272084822187, 0.08090171204448858, 0.23416118618048126, -0.18548266222668147, 0.3545906580628177,
    -0.10013362874972173,
)
NT = (((1,), (1,)), ((), ()))
TN = (((0,), (0,)), ((), ()))


def mm(a, b):
    return jnp.dot(a, b, preferred_element_type=F32)


def mm_nt(a, b):
    return lax.dot_general(a, b, NT, preferred_element_type=F32)


def mm_tn(a, b):
    return lax.dot_general(a, b, TN, preferred_element_type=F32)


def aligned(start, size):
    return pl.ds(pl.multiple_of(start, size), size)


def gelu_pair(u):
    e = jnp.exp2(u * u * (-0.5 * LOG2E))
    d = 1.0 + (ERFC_P * 0.7071067811865476) * jnp.abs(u)
    t = pl.reciprocal(d, approx=True)
    t = t * (2.0 - d * t)
    p = ERFC[-1]
    for coef in ERFC[-2::-1]:
        p = p * t + coef
    tail = p * t * e
    phi = jnp.where(u >= 0.0, 1.0 - tail, tail)
    return u * phi, phi + u * (e * 0.3989422804014327)


def column_copies(hbm, vmem, sems, store):
    copies = []
    for s in range(2):
        for p in range(8):
            f = (p % 4) * 2 + p // 4
            outside = hbm.at[s, :, pl.ds(f * SIDE, SIDE)]
            inside = vmem.at[pl.ds(s * L, L), pl.ds(p * SIDE, SIDE)]
            pair = (inside, outside) if store else (outside, inside)
            copies.append(pltpu.make_async_copy(pair[0], pair[1], sems.at[s, p]))
    return copies


def lane_half(value, e):
    lane = lax.broadcasted_iota(jnp.int32, (1, value.shape[1]), 1)
    return jnp.where((lane < 64) if e == 0 else (lane >= 64), value, jnp.zeros_like(value))


def row_mean(v):
    return jnp.sum(v, axis=1, keepdims=True) * (1.0 / D)


def turn_out(m, idx):
    k, p = idx % 2, idx // 2
    off = jnp.where(p == 0, 0, jnp.where(p == 1, 1 + k, jnp.where(p == 2, 2 - k, 3)))
    return k, off, m ^ off


def forward_kernel(
    lens, x_hbm, cot_hbm, sqr, sor, sur, sdr, ob, g1, b1, db, g2, b2, ub, qb,
    y_hbm, wq_hbm, wo_hbm, wu_hbm, wd_hbm, qkv_hbm, p_hbm, mixed_hbm, lowh_hbm, n1_hbm, rs_hbm, act_hbm, gp_hbm,
    dpre_hbm, vec_out, gain_out,
    wq, wo, wu, wd, vec, x, sqp, sv, qst, pst, mixed, hid, lowh, act, gst, cot, yst, nst, rst, dst, dv, ubs, qvb, ust,
    *sems,
):
    (vs, vr, xsem, csem, ysem, wsem, qsem, psem, msem, gsem, nsem, dsem, asem) = sems[9:]
    z, c, m = place()
    zero = jnp.zeros((1, 128), F32)

    def prepare():
        for e in range(6):
            pair, part = e // 3, e % 3
            halves = [
                sqr[:, (pair * 2 + h) * 192 + part * 64:(pair * 2 + h) * 192 + part * 64 + 64].astype(F32)
                for h in range(2)
            ]
            sqp[pair, :, part * 128:part * 128 + 128] = jnp.concatenate(halves, axis=1).astype(BF16)
        q1 = qb[...].astype(F32)
        sv[...] = jnp.concatenate(
            [r[...].astype(F32) for r in (ob, g1, b1, db, g2, b2)] + [zero, zero, ub[...].astype(F32)]
            + [jnp.concatenate([q1, q1], axis=1), zero, zero, zero], axis=0
        ).astype(BF16)

    greet_all(prepare)
    shards = (
        [sqp.at[k] for k in range(2)],
        [sor.at[pl.ds(k * 128, 128), :] for k in range(2)],
        [sur.at[:, pl.ds(k * HALF, HALF)] for k in range(2)],
        [sdr.at[pl.ds(k * HALF, ROWS_A), :] for k in range(2)],
        [sdr.at[pl.ds(k * HALF + ROWS_A, ROWS_B), :] for k in range(2)],
    )
    spread = Spread(shards, (wq, wo, wu, wd), sems[:9])
    spread.start(0, 0)
    spread.late_start()
    vcopy = swap_vectors(sv, vec, vs, vr, False)
    run_31(lambda d: vcopy(d).start())
    vec[m * 8 + z * 2 + c] = sv[...]
    x_copies = column_copies(x_hbm, x, xsem, False)
    c_copies = column_copies(cot_hbm, cot, csem, False)
    for cp in x_copies:
        cp.start()
    spread.late_relay()
    spread.enter(0, 0)
    spread.second(0, 0)
    spread.start(0, 1)
    spread.start(1, 0)
    run_31(lambda d: vcopy(d).wait())
    for p in range(8):
        dv[:, p * SIDE:(p + 1) * SIDE] = vec[m * 8 + (p % 4) * 2 + p // 4].astype(F32)[0:8]
    lane = lax.broadcasted_iota(jnp.int32, (1, 128), 1)
    for j in range(8):
        k, mo = j // 4, j % 4
        t = vec[m * 8 + mo * 2 + k].astype(F32)
        ubs[j] = jnp.concatenate([t[8:9], t[9:10], t[10:11], t[11:12]], axis=1)
        rows = [vec[mo * 8 + 4 * k + i].astype(F32)[12:13] for i in range(4)]
        qvb[j] = jnp.concatenate(
            [jnp.where(lane < 64, rows[0], rows[2]), zero, jnp.where(lane < 64, rows[1], rows[3])], axis=1
        )
    for cp in x_copies:
        cp.wait()
    for cp in c_copies:
        cp.start()

    def w_copy(t, idx):
        k, _, mo = turn_out(m, idx)
        src, dst = ((wq, wq_hbm), (wo, wo_hbm), (wu, wu_hbm), (wd, wd_hbm))[t]
        return pltpu.make_async_copy(src.at[k, mo], dst.at[k, mo], wsem.at[t, idx])

    def q_copy(it):
        k, _, mo = turn_out(m, it // 2)
        s = it % 2
        return pltpu.make_async_copy(qst.at[s], qkv_hbm.at[k * 4 + mo, aligned(s * L, L), :], qsem.at[s])

    def p_copy(it):
        k, _, mo = turn_out(m, it // 2)
        s = it % 2
        return pltpu.make_async_copy(pst.at[s], p_hbm.at[k * 4 + mo, s], psem.at[s])

    def attend(it, carry):
        idx, s = it // 2, it % 2
        k, off, mo = turn_out(m, idx)
        j = k * 4 + mo
        rows = aligned(s * L, L)

        @pl.when(it == 2)
        def _():
            spread.enter(0, 1)
            spread.second(0, 1)
            spread.start(1, 1)
            spread.start(2, 0)
            spread.relay(0, 0)
            spread.cross(0, 0, 0)

        @pl.when(it == 4)
        def _():
            spread.enter(1, 0)
            spread.second(1, 0)

        @pl.when(it == 6)
        def _():
            spread.enter(1, 1)
            spread.second(1, 1)
            spread.relay(0, 1)
            spread.cross(0, 1, 0)
            spread.start(2, 1)

        @pl.when(it == 8)
        def _():
            spread.cross(0, 0, 1)

        @pl.when(it == 10)
        def _():
            spread.cross(0, 1, 1)
            spread.enter(2, 0)
            spread.second(2, 0)
            spread.start(3, 0)
            spread.relay(1, 0)
            spread.relay(1, 1)

        @pl.when(it == 12)
        def _():
            spread.cross(1, 0, 0)
            spread.cross(1, 1, 0)

        @pl.when(it == 14)
        def _():
            spread.cross(1, 0, 1)
            spread.cross(1, 1, 1)
            spread.enter(2, 1)
            spread.second(2, 1)
            spread.start(3, 1)

        @pl.when(s == 0)
        def _():
            spread.c_copy(0, k, off).wait_recv()
            w_copy(0, idx).start()

        @pl.when(it >= 2)
        def _():
            q_copy(it - 2).wait()
            p_copy(it - 2).wait()

        qst[s] = (mm(x[rows, :], wq[k, mo]) + qvb[j]).astype(BF16)
        q_copy(it).start()
        keys, values = qst[s, :, 128:256], qst[s, :, 256:384]
        length = lens[s, m]
        bias = jnp.where(lax.broadcasted_iota(jnp.int32, (1, L), 1) < length, 0.0, -1e30)
        out = [None, None]
        for e in range(2):
            k_e, v_e = lane_half(keys, e), lane_half(values, e)
            for h in range(2):
                half = slice(h * 256, h * 256 + 256)
                scores = mm_nt(qst[s, half, 0:128], k_e) + bias
                top = jnp.max(scores, axis=1, keepdims=True)
                ex = jnp.exp2((scores - top) * (LOG2E * DH ** (-0.5)))
                probs = (ex * (1.0 / jnp.sum(ex, axis=1, keepdims=True))).astype(BF16)
                pst[s, e, half, :] = probs
                part = mm(probs, v_e)
                out[h] = part if out[h] is None else out[h] + part
        p_copy(it).start()
        mixed[rows, aligned(j * 128, 128)] = jnp.concatenate(out, axis=0).astype(BF16)
        return carry

    lax.fori_loop(0, 16, attend, 0)
    for it in (14, 15):
        q_copy(it).wait()
        p_copy(it).wait()
    m_copy = pltpu.make_async_copy(mixed, mixed_hbm, msem.at[0])
    m_copy.start()
    spread.late_planes()
    for k in range(2):
        for off in range(4):
            spread.c_copy(1, k, off).wait_recv()
    for idx in range(8):
        w_copy(1, idx).start()

    def n_copy(i):
        return pltpu.make_async_copy(nst.at[i % 2], n1_hbm.at[aligned(i * 256, 256), :], nsem.at[i % 2])

    def r_copy(i):
        return pltpu.make_async_copy(rst.at[i % 2], rs_hbm.at[aligned(i * 256, 256), :], nsem.at[2 + i % 2])

    def first_norm(i, carry):
        rows = aligned(i * 256, 256)

        @pl.when(i >= 2)
        def _():
            n_copy(i - 2).wait()
            r_copy(i - 2).wait()

        pre = mm(mixed[rows, :], wo[...].reshape(D, D)) + dv[0:1] + x[rows, :].astype(F32)
        cen = pre - row_mean(pre)
        inv = lax.rsqrt(row_mean(cen * cen) + EPSILON)
        n = cen * inv
        nst[i % 2] = n
        rst[i % 2] = jnp.broadcast_to(inv, (256, 128))
        n_copy(i).start()
        r_copy(i).start()
        h = n * dv[1:2] + dv[2:3]
        hid[rows, :] = h
        lowh[rows, :] = h.astype(BF16)
        return carry

    lax.fori_loop(0, 4, first_norm, 0)
    for i in (2, 3):
        n_copy(i).wait()
        r_copy(i).wait()
    h_copy = pltpu.make_async_copy(lowh, lowh_hbm, msem.at[1])
    h_copy.start()

    def g_copy(i):
        k, _, mo = turn_out(m, i)
        return pltpu.make_async_copy(gst.at[i % 2], gp_hbm.at[k * 4 + mo], gsem.at[i % 2])

    def a_copy(i):
        k, _, mo = turn_out(m, i)
        j = k * 4 + mo
        return pltpu.make_async_copy(act.at[:, aligned(j * HALF, HALF)], act_hbm.at[j], asem.at[i])

    def up(idx, carry):
        k, off, mo = turn_out(m, idx)
        j = k * 4 + mo
        cols = aligned(j * HALF, HALF)

        @pl.when(idx == 0)
        def _():
            spread.relay(2, 0)
            spread.cross(2, 0, 0)

        @pl.when(idx == 1)
        def _():
            spread.relay(2, 1)
            spread.cross(2, 1, 0)
            spread.enter(3, 0)
            spread.second(3, 0)

        @pl.when(idx == 3)
        def _():
            spread.enter(3, 1)
            spread.second(3, 1)

        @pl.when(idx == 6)
        def _():
            spread.cross(2, 0, 1)
            spread.cross(2, 1, 1)

        spread.c_copy(2, k, off).wait_recv()
        w_copy(2, idx).start()

        @pl.when(idx >= 2)
        def _():
            g_copy(idx - 2).wait()

        w = wu[k, mo]
        ust[0] = mm(lowh[0:256, :], w)
        for h in range(4):
            sub = slice(h * 256, h * 256 + 256)
            if h < 3:
                ust[(h + 1) % 2] = mm(lowh[h * 256 + 256:h * 256 + 512, :], w)
            a, g = gelu_pair(ust[h % 2] + ubs[j])
            act[sub, cols] = a.astype(BF16)
            gst[idx % 2, sub, :] = g.astype(BF16)
        g_copy(idx).start()
        a_copy(idx).start()
        return carry

    lax.fori_loop(0, 8, up, 0)
    gain_out[...] = jnp.zeros((8, D), F32)
    vec_out[...] = dv[...]
    spread.relay(3, 0)
    spread.cross(3, 0, 0)
    spread.relay(3, 1)
    spread.cross(3, 1, 0)
    spread.late_cross()
    for k in range(2):
        spread.late_c(k).wait_recv()

    def down(idx, carry):
        k, off, mo = turn_out(m, idx)
        cols = aligned((k * 4 + mo) * HALF, HALF)

        @pl.when(idx == 4)
        def _():
            spread.cross(3, 0, 1)
            spread.cross(3, 1, 1)

        spread.c_copy(3, k, off).wait_recv()
        w_copy(3, idx).start()
        for r in range(2):
            for h in range(2):
                rows, side = slice(r * L, r * L + L), slice(h * HALF, h * HALF + HALF)
                hid[rows, side] += mm(act[rows, cols], wd[k, mo, :, side])
        return carry

    lax.fori_loop(0, 8, down, 0)

    def d_copy(i):
        return pltpu.make_async_copy(dst.at[i % 2], dpre_hbm.at[aligned(i * 256, 256), :], dsem.at[i % 2])

    def second_norm(i, carry):
        rows = aligned(i * 256, 256)

        @pl.when(i >= 2)
        def _():
            d_copy(i - 2).wait()

        pre = hid[rows, :] + dv[3:4]
        cen = pre - row_mean(pre)
        inv = lax.rsqrt(row_mean(cen * cen) + EPSILON)
        n = cen * inv
        yst[rows, :] = (n * dv[4:5] + dv[5:6]).astype(BF16)
        pos = (i % 2) * 256 + lax.broadcasted_iota(jnp.int32, (256, 1), 0)
        grad = jnp.where(pos < lens[i // 2, m], cot[rows, :].astype(F32), 0.0)
        g = grad * dv[4:5]
        back = inv * (g - row_mean(g) - n * row_mean(g * n))
        dst[i % 2] = back
        d_copy(i).start()
        gain_out[3:4, :] += jnp.sum(back, axis=0, keepdims=True)
        gain_out[4:5, :] += jnp.sum(grad * n, axis=0, keepdims=True)
        gain_out[5:6, :] += jnp.sum(grad, axis=0, keepdims=True)
        return carry

    for cp in c_copies:
        cp.wait()
    lax.fori_loop(0, 4, second_norm, 0)
    y_copies = column_copies(y_hbm, yst, ysem, True)
    for cp in y_copies:
        cp.start()
    for i in (2, 3):
        d_copy(i).wait()
    for i in (6, 7):
        g_copy(i).wait()

    def finish(i, carry):
        a_copy(i).wait()
        for t in range(4):
            w_copy(t, i).wait()
        return carry

    lax.fori_loop(0, 8, finish, 0)
    m_copy.wait()
    h_copy.wait()
    for cp in y_copies:
        cp.wait()
    spread.drain()


SAVED = (
    ((8, 1024, 384), BF16), ((8, 2, 2, L, L), BF16), ((1024, D), BF16), ((1024, D), BF16), ((1024, D), F32),
    ((1024, 128), F32), ((8, 1024, HALF), BF16), ((8, 1024, HALF), BF16), ((1024, D), F32),
)


def forward(lengths, inputs, cotangent, weights, vectors):
    vm = pl.BlockSpec(memory_space=pltpu.VMEM)
    anywhere = pl.BlockSpec(memory_space=pl.ANY)
    shape = jax.ShapeDtypeStruct
    dma = pltpu.SemaphoreType.DMA
    v = pltpu.VMEM
    scratch = [v(s, BF16) for s in WHOLE] + [
        v((32, 16, 128), BF16), v((1024, D), BF16), v((2, 128, 384), BF16), v((16, 128), BF16), v((2, L, 384), BF16),
        v((2, 2, L, L), BF16), v((1024, D), BF16), v((1024, D), F32), v((1024, D), BF16), v((1024, FF), BF16),
        v((2, 1024, HALF), BF16), v((1024, D), BF16), v((1024, D), BF16), v((2, 256, D), F32), v((2, 256, 128), F32),
        v((2, 256, D), F32), v((8, D), F32), v((8, 1, HALF), F32), v((8, 1, 384), F32), v((2, 256, HALF), F32),
    ] + spread_sems() + [
        dma((32,)), dma((32,)), dma((2, 8)), dma((2, 8)), dma((2, 8)), dma((4, 8)), dma((2,)), dma((2,)), dma((2,)),
        dma((2,)), dma((4,)), dma((2,)), dma((8,)),
    ]
    return pl.pallas_call(
        forward_kernel,
        out_shape=[shape((2, L, D), BF16)] + [shape(s, BF16) for s in WHOLE] + [shape(s, d) for s, d in SAVED]
        + [shape((8, D), F32), shape((8, D), F32)],
        in_specs=[pl.BlockSpec(memory_space=pltpu.SMEM), anywhere, anywhere] + [vm] * 12,
        out_specs=[anywhere] * 14 + [vm, vm],
        scratch_shapes=scratch,
        compiler_params=pltpu.CompilerParams(collective_id=0, has_side_effects=True, vmem_limit_bytes=67000000),
    )(lengths, inputs, cotangent, *weights, *vectors)

class Fold:
    def __init__(self, rc, rx, ry, rz, sems):
        self.rc, self.rx, self.ry, self.rz = rc, rx, ry, rz
        self.cs, self.cr, self.xs, self.xr, self.ys, self.yr, self.zs, self.zr = sems
        self.z, self.c, self.m = place()

    def c_copy(self, t, k, off, src):
        return remote(
            src, self.rc[t].at[k, self.m ^ off], self.cs.at[t, k, off], self.cr.at[t, k, off],
            self.z * 2 + 1 - self.c, self.m,
        )

    def x_copy(self, t, k, i):
        m = self.m ^ (3 if i else 1 + k)
        return remote(
            self.rc[t].at[k, m], self.rx[t].at[k, i], self.xs.at[t, k, i], self.xr.at[t, k, i],
            self.z * 2 + self.c, self.m ^ (1 + k),
        )

    def y_copy(self, t, k):
        m = self.m ^ (2 - k)
        return remote(
            self.rc[t].at[k, m], self.ry[t].at[k], self.ys.at[t, k], self.yr.at[t, k], self.z * 2 + self.c, m
        )

    def z_copy(self, t, k, d):
        z = (self.z + d) % PLANES
        src = span(self.rc[t].at[k, self.m], KINDS[t], z * SIDE, SIDE)
        return remote(
            src, self.rz[t].at[k, d - 1], self.zs.at[t, k, d - 1], self.zr.at[t, k, d - 1], z * 2 + self.c, self.m
        )

    def to_y(self, t, k):
        self.x_copy(t, k, 1).wait_recv()
        add_into(self.rc[t].at[k, self.m ^ (2 - k)], self.rx[t].at[k, 1])
        self.y_copy(t, k).start()

    def to_z(self, t, k):
        self.x_copy(t, k, 0).wait_recv()
        add_into(self.rc[t].at[k, self.m], self.rx[t].at[k, 0])
        self.y_copy(t, k).wait_recv()
        add_into(self.rc[t].at[k, self.m], self.ry[t].at[k])
        for d in range(1, PLANES):
            self.z_copy(t, k, d).start()

    def total(self, t, k):
        for d in range(1, PLANES):
            self.z_copy(t, k, d).wait_recv()
        own = span(self.rc[t].at[k, self.m], KINDS[t], self.z * SIDE, SIDE)[...].astype(F32)
        rz = self.rz[t]
        return own + rz[k, 0].astype(F32) + rz[k, 1].astype(F32) + rz[k, 2].astype(F32)

    def drain(self, t, k):
        self.x_copy(t, k, 0).wait_send()
        self.x_copy(t, k, 1).wait_send()
        self.y_copy(t, k).wait_send()
        for d in range(1, PLANES):
            self.z_copy(t, k, d).wait_send()


def backward_kernel(
    x_hbm, wq_hbm, wo_hbm, wu_hbm, wd_hbm, qkv_hbm, p_hbm, mixed_hbm, lowh_hbm, n1_hbm, rs_hbm, act_hbm, gp_hbm,
    dpre_hbm, dv, gains,
    ig_hbm, oq, oo, ou, od, ov,
    *rest,
):
    rc, rx, ry, rz = rest[0:4], rest[4:8], rest[8:12], rest[12:16]
    (dbr, dh, low, wdj, wuj, ag, gd, gu, mixed, dmix, qkvj, dproj, nst, rst, rv, gv, sums, ubg, qvg) = rest[16:35]
    fold = Fold(rc, rx, ry, rz, rest[35:43])
    vs, vr, lsem, psem, ssem, nsem, isem, xsem = rest[43:]
    z, c, m = place()
    other = 1 - c
    mine, theirs = aligned(c * HALF, HALF), aligned(other * HALF, HALF)

    def turn(idx):
        k, p = idx % 2, idx // 2
        off = jnp.where(p == 0, 3, jnp.where(p == 1, 1 + k, jnp.where(p == 2, 2 - k, 0)))
        return k, p, off

    def down_loads(idx):
        k, _, off = turn(idx)
        mo, slot = m ^ off, idx % 2
        j = k * 4 + mo
        pairs = ((wd_hbm.at[k, mo], wdj.at[slot]), (act_hbm.at[j], ag.at[slot, 0]), (gp_hbm.at[j], ag.at[slot, 1]))
        return [pltpu.make_async_copy(a, b, lsem.at[slot, i]) for i, (a, b) in enumerate(pairs)]

    def up_load(idx):
        k, _, off = turn(idx)
        return pltpu.make_async_copy(wu_hbm.at[k, m ^ off], wuj.at[idx % 2], lsem.at[idx % 2, 3])

    dp_copy = pltpu.make_async_copy(dpre_hbm, dh, ssem.at[0])
    dp_copy.start()
    for cp in down_loads(0):
        cp.start()
    lh_copy = pltpu.make_async_copy(lowh_hbm, low, ssem.at[1])
    lh_copy.start()
    mx_copy = pltpu.make_async_copy(mixed_hbm, mixed, ssem.at[2])
    up_load(0).start()
    up_load(1).start()
    mx_copy.start()
    greet_all()
    sums[...] = gains[...]
    dp_copy.wait()

    def cast(i, carry):
        rows = aligned(i * 128, 128)
        dbr[rows, :] = dh[rows, :].astype(BF16)
        return carry

    lax.fori_loop(0, 8, cast, 0)

    def settle_ffn(t, idx, own):
        k, p, off = turn(idx)
        mo = m ^ off
        fold.c_copy(t, k, off, gd.at[idx % 2]).wait()
        add_into(rc[t].at[k, mo], own.at[idx % 2])

        @pl.when(p == 0)
        def _():
            fold.x_copy(t, k, 1).start()

        @pl.when(p == 1)
        def _():
            fold.x_copy(t, k, 0).start()

    def down_step(idx, carry):
        k, p, off = turn(idx)
        mo, slot = m ^ off, idx % 2
        for cp in down_loads(idx):
            cp.wait()

        @pl.when(idx < 7)
        def _():
            for cp in down_loads(idx + 1):
                cp.start()

        total = jnp.zeros((1, HALF), F32)
        for r in range(2):
            rows = slice(r * L, r * L + L)
            d = (mm_nt(dbr[rows, :], wdj[slot]) * ag[slot, 1, rows, :].astype(F32)).astype(BF16)
            dproj[idx, rows, :] = d
            total = total + jnp.sum(d.astype(F32), axis=0, keepdims=True)
        ubg[k * 4 + mo] = total
        gd[slot] = mm_tn(ag[slot, 0], dbr[:, theirs]).astype(BF16)
        fold.c_copy(3, k, off, gd.at[slot]).start()
        gu[slot] = mm_tn(ag[slot, 0], dbr[:, mine]).astype(BF16)

        @pl.when(idx >= 1)
        def _():
            settle_ffn(3, idx - 1, gu)

        return carry

    lax.fori_loop(0, 8, down_step, 0)
    settle_ffn(3, 7, gu)
    lh_copy.wait()
    for k in range(2):
        fold.to_y(3, k)

    def up_step(idx, carry):
        k, p, off = turn(idx)
        slot = idx % 2
        gd[slot] = mm_tn(low[:, theirs], dproj[idx]).astype(BF16)
        fold.c_copy(2, k, off, gd.at[slot]).start()
        gu[slot] = mm_tn(low[:, mine], dproj[idx]).astype(BF16)
        up_load(idx).wait()
        for r in range(2):
            for h in range(2):
                rows, cols = slice(r * L, r * L + L), slice(h * HALF, h * HALF + HALF)
                dh[rows, cols] += mm_nt(dproj[idx, rows, :], wuj[slot, cols, :])

        @pl.when(idx < 6)
        def _():
            up_load(idx + 2).start()

        @pl.when(idx >= 1)
        def _():
            settle_ffn(2, idx - 1, gu)

        @pl.when(idx == 5)
        def _():
            fold.to_z(3, 1)

        @pl.when(idx == 6)
        def _():
            fold.to_z(3, 0)

        return carry

    lax.fori_loop(0, 8, up_step, 0)
    settle_ffn(2, 7, gu)

    def norm_loads(i):
        rows, slot = aligned(i * 256, 256), i % 2
        return (
            pltpu.make_async_copy(n1_hbm.at[rows, :], nst.at[slot], nsem.at[slot, 0]),
            pltpu.make_async_copy(rs_hbm.at[rows, :], rst.at[slot], nsem.at[slot, 1]),
        )

    for cp in norm_loads(0):
        cp.start()
    wo_copies = [
        pltpu.make_async_copy(
            wo_hbm.at[j // 4, j % 4], wdj.at[j // 4, pl.ds((j % 4) * 128, 128), :], lsem.at[j // 4, j % 4]
        )
        for j in range(8)
    ]
    for cp in wo_copies:
        cp.start()
    x_copies = column_copies(x_hbm, low, xsem, False)
    for cp in x_copies:
        cp.start()

    def attn_loads(idx):
        k, _, off = turn(idx)
        j, slot = k * 4 + (m ^ off), idx % 2
        copies = [pltpu.make_async_copy(qkv_hbm.at[j], qkvj.at[slot], psem.at[slot, 4])]
        for s in range(2):
            for e in range(2):
                copies.append(
                    pltpu.make_async_copy(
                        p_hbm.at[j, s, e], ag.at[slot, s, pl.ds(e * L, L), :], psem.at[slot, 2 * s + e]
                    )
                )
        return copies

    for cp in attn_loads(0):
        cp.start()

    def first_back(i, carry):
        rows, slot = aligned(i * 256, 256), i % 2

        @pl.when(i < 3)
        def _():
            for cp in norm_loads(i + 1):
                cp.start()

        for cp in norm_loads(i):
            cp.wait()
        grad, n = dh[rows, :], nst[slot]
        g = grad * dv[1:2]
        inv = rst[slot][:, 0:1]
        back = inv * (g - row_mean(g) - n * row_mean(g * n))
        dh[rows, :] = back
        dbr[rows, :] = back.astype(BF16)
        sums[0:1, :] += jnp.sum(back, axis=0, keepdims=True)
        sums[1:2, :] += jnp.sum(grad * n, axis=0, keepdims=True)
        sums[2:3, :] += jnp.sum(grad, axis=0, keepdims=True)
        return carry

    lax.fori_loop(0, 4, first_back, 0)
    mx_copy.wait()
    for h in range(2):
        rows = slice(h * L, h * L + L)
        wuj[0, rows, :] = mm_tn(mixed[:, rows], dbr[:, theirs]).astype(BF16)
    for k in range(2):
        for off in range(4):
            src = wuj.at[0, aligned((k * 4 + (m ^ off)) * 128, 128), :]
            fold.c_copy(1, k, off, src).start()
    for cp in wo_copies:
        cp.wait()
    for h in range(2):
        rows = slice(h * L, h * L + L)
        for q in range(2):
            dmix[rows, q * L:q * L + L] = mm_nt(dbr[rows, :], wdj[q]).astype(BF16)
    for h in range(2):
        rows = slice(h * L, h * L + L)
        wuj[1, rows, :] = mm_tn(mixed[:, rows], dbr[:, mine]).astype(BF16)
    for k in range(2):
        for off in (3, 1 + k, 2 - k, 0):
            src = wuj.at[0, aligned((k * 4 + (m ^ off)) * 128, 128), :]
            fold.c_copy(1, k, off, src).wait()
            add_into(rc[1].at[k, m ^ off], wuj.at[1, aligned((k * 4 + (m ^ off)) * 128, 128), :])
            if off == 3:
                fold.x_copy(1, k, 1).start()
            elif off == 1 + k:
                fold.x_copy(1, k, 0).start()
    for cp in x_copies:
        cp.wait()

    def piece(idx):
        return gu.at[idx % 2, :, pl.ds(0, 384)]

    def attend(idx, s):
        k, _, off = turn(idx)
        mo, slot = m ^ off, idx % 2
        j = k * 4 + mo
        rows = slice(s * L, s * L + L)
        dout = dmix[rows, aligned(j * 128, 128)]
        queries, keys, values = (qkvj[slot, rows, i * 128:i * 128 + 128] for i in range(3))
        dq = dk = dval = None
        for e in range(2):
            probs = ag[slot, s, e * L:e * L + L, :]
            p32 = probs.astype(F32)
            t = p32 * mm_nt(dout, lane_half(values, e))
            ds = (t - p32 * jnp.sum(t, axis=1, keepdims=True)).astype(BF16)
            parts = (mm(ds, lane_half(keys, e)), mm_tn(ds, lane_half(queries, e)), mm_tn(probs, lane_half(dout, e)))
            dq, dk, dval = parts if e == 0 else (dq + parts[0], dk + parts[1], dval + parts[2])
        scale = DH ** (-0.5)
        out = jnp.concatenate([dq * scale, dk * scale, dval], axis=1).astype(BF16)
        dproj[idx, rows, 0:384] = out
        return jnp.sum(out.astype(F32), axis=0, keepdims=True)

    def settle(idx):
        k, p, off = turn(idx)
        mo = m ^ off
        fold.c_copy(0, k, off, piece(idx)).wait()
        rc[0][k, mo] = (mm_tn(low[:, mine], dproj[idx, :, 0:384]) + rc[0][k, mo].astype(F32)).astype(BF16)

        @pl.when(p == 0)
        def _():
            fold.x_copy(0, k, 1).start()

        @pl.when(p == 1)
        def _():
            fold.x_copy(0, k, 0).start()

        @pl.when(p == 2)
        def _():
            fold.to_y(0, k)

        @pl.when(p == 3)
        def _():
            fold.to_z(0, k)

    def heads(idx, carry):
        k, p, off = turn(idx)
        j = k * 4 + (m ^ off)
        for cp in attn_loads(idx):
            cp.wait()

        @pl.when(idx < 7)
        def _():
            for cp in attn_loads(idx + 1):
                cp.start()

        first = attend(idx, 0)

        @pl.when(idx >= 1)
        def _():
            settle(idx - 1)

        qvg[j] = first + attend(idx, 1)
        gu[idx % 2, :, 0:384] = mm_tn(low[:, theirs], dproj[idx, :, 0:384]).astype(BF16)
        fold.c_copy(0, k, off, piece(idx)).start()

        @pl.when(idx == 0)
        def _():
            fold.to_y(2, 1)
            fold.to_y(2, 0)

        @pl.when(idx == 2)
        def _():
            fold.to_y(1, 0)
            fold.to_y(1, 1)
            fold.to_z(2, 1)

        @pl.when(idx == 3)
        def _():
            fold.to_z(2, 0)

        @pl.when(idx == 4)
        def _():
            fold.to_z(1, 0)
            fold.to_z(1, 1)

        return carry

    lax.fori_loop(0, 8, heads, 0)

    def wq_load(idx):
        k, _, off = turn(idx)
        return pltpu.make_async_copy(wq_hbm.at[k, m ^ off], qkvj.at[idx % 2], psem.at[idx % 2, 4])

    wq_load(0).start()
    wq_load(1).start()
    settle(7)
    for f in range(8):
        p = (f % 2) * 4 + f // 2
        wide = sums[:, p * SIDE:(p + 1) * SIDE]
        ub = ubg[(f % 2) * 4 + f // 2]
        pad = jnp.zeros((3, 128), F32)
        for mo in range(4):
            kk, e, part = f // 4, (f // 2) % 2, f % 2
            qv = qvg[kk * 4 + mo][:, part * 256 + e * 64:part * 256 + e * 64 + 64]
            gv[mo * 8 + f] = jnp.concatenate(
                [wide] + [ub[:, i * 128:i * 128 + 128] for i in range(4)] + [jnp.concatenate([qv, qv], axis=1), pad],
                axis=0,
            )
    vcopy = swap_vectors(gv, rv, vs, vr, True)
    run_31(lambda d: vcopy(d).start())
    me = m * 8 + z * 2 + c
    rv[me] = gv[me]

    def pull(idx, carry):
        slot = idx % 2
        wq_load(idx).wait()
        for r in range(2):
            for h in range(2):
                rows, cols = slice(r * L, r * L + L), slice(h * HALF, h * HALF + HALF)
                dh[rows, cols] += mm_nt(dproj[idx, rows, 0:384], qkvj[slot, cols, :])

        @pl.when(idx < 6)
        def _():
            wq_load(idx + 2).start()

        return carry

    lax.fori_loop(0, 8, pull, 0)
    i_copies = column_copies(ig_hbm, dh, isem, True)
    for cp in i_copies:
        cp.start()
    run_31(lambda d: vcopy(d).wait())

    def gather_sum(i, acc):
        return acc + rv[i]

    ov[...] = lax.fori_loop(0, 32, gather_sum, jnp.zeros((16, 128), F32))
    for k in range(2):
        od[k * HALF:k * HALF + HALF, :] = fold.total(3, k)
        ou[:, k * HALF:k * HALF + HALF] = fold.total(2, k)
        oo[k * 128:k * 128 + 128, :] = fold.total(1, k)
    for k in range(2):
        t = fold.total(0, k)
        parts = [t[:, i * 128 + e * 64:i * 128 + e * 64 + 64] for e in range(2) for i in range(3)]
        oq[:, k * 384:k * 384 + 384] = jnp.concatenate(parts, axis=1)
    for cp in i_copies:
        cp.wait()
    for t in range(4):
        for k in range(2):
            fold.drain(t, k)


def backward(inputs, weights, saved, dv, gains):
    vm = pl.BlockSpec(memory_space=pltpu.VMEM)
    anywhere = pl.BlockSpec(memory_space=pl.ANY)
    shape = jax.ShapeDtypeStruct
    dma = pltpu.SemaphoreType.DMA
    v = pltpu.VMEM
    bufs, sems = fold_scratch()
    scratch = bufs + [
        v((1024, D), BF16), v((1024, D), F32), v((1024, D), BF16), v((2, HALF, D), BF16), v((2, D, HALF), BF16),
        v((2, 2, 1024, HALF), BF16), v((2, HALF, HALF), BF16), v((2, HALF, HALF), BF16),
        v((1024, D), BF16), v((1024, D), BF16), v((2, 1024, 384), BF16), v((8, 1024, HALF), BF16),
        v((2, 256, D), F32), v((2, 256, 128), F32), v((32, 16, 128), F32), v((32, 16, 128), F32), v((8, D), F32),
        v((8, 1, HALF), F32), v((8, 1, 384), F32),
    ] + sems + [
        dma((32,)), dma((32,)), dma((2, 4)), dma((2, 5)), dma((3,)), dma((2, 2)), dma((2, 8)), dma((2, 8)),
    ]
    return pl.pallas_call(
        backward_kernel,
        out_shape=[
            shape((2, L, D), F32), shape((128, 768), F32), shape((256, 128), F32), shape((128, 1024), F32),
            shape((1024, 128), F32), shape((16, 128), F32),
        ],
        in_specs=[anywhere] * 14 + [vm, vm],
        out_specs=[anywhere] + [vm] * 5,
        scratch_shapes=scratch,
        compiler_params=pltpu.CompilerParams(collective_id=1, has_side_effects=True, vmem_limit_bytes=67000000),
    )(inputs, *weights, *saved, dv, gains)

def fast_body(
    inputs, lengths, qkv_weight, qv_bias, out_weight, out_bias, norm1_gain, norm1_bias, up_weight, up_bias,
    down_weight, down_bias, norm2_gain, norm2_bias, cotangent,
):
    row = lambda v: v.reshape(1, 128)
    results = forward(
        lengths, inputs, cotangent, (qkv_weight, out_weight, up_weight, down_weight),
        (row(out_bias), row(norm1_gain), row(norm1_bias), row(down_bias), row(norm2_gain), row(norm2_bias),
         up_bias.reshape(4, 128), qv_bias.reshape(1, 64)),
    )
    input_grad, oq, oo, ou, od, ov = backward(inputs, results[1:5], results[5:14], results[14], results[15])
    return (
        results[0],
        input_grad,
        oq,
        ov[12, :64],
        oo,
        ov[0],
        ov[1],
        ov[2],
        ou,
        ov[8:12].reshape(512),
        od,
        ov[3],
        ov[4],
        ov[5],
    )


def solution(mesh):
    placed = (
        P(None, ("fsdp", "mp"), None),
        P(None, "fsdp"),
        P("fsdp", "mp"),
        P(("mp", "fsdp")),
        P("mp", "fsdp"),
        P("fsdp"),
        P("fsdp"),
        P("fsdp"),
        P("fsdp", "mp"),
        P("fsdp"),
        P("mp", "fsdp"),
        P("fsdp"),
        P("fsdp"),
        P("fsdp"),
        P(None, ("fsdp", "mp"), None),
    )
    blocks_fit = mesh.shape["fsdp"] == 8 and mesh.shape["mp"] == 4
    return jax.shard_map(
        fast_body if blocks_fit else generic_body,
        mesh=mesh,
        in_specs=placed,
        out_specs=(
            P(None, ("fsdp", "mp"), None),
            P(None, ("fsdp", "mp"), None),
            P("fsdp", "mp"),
            P(("mp", "fsdp")),
            P("mp", "fsdp"),
            P("fsdp"),
            P("fsdp"),
            P("fsdp"),
            P("fsdp", "mp"),
            P("fsdp"),
            P("mp", "fsdp"),
            P("fsdp"),
            P("fsdp"),
            P("fsdp"),
        ),
        check_vma=False,
    )
```

```python
from functools import partial

import jax
import jax.numpy as jnp
from jax import lax
from jax.experimental import pallas as pl
from jax.experimental.pallas import tpu as pltpu
from jax.sharding import PartitionSpec as P

D = 1024
DH = 64
FF = 4096
L = 512
MBS = 2


EPSILON = 1e-06
CONTRACT_ROWS = (((0,), (0,)), ((), ()))
CONTRACT_COLS = (((1,), (1,)), ((), ()))


def normalize(values, scale_vec, shift_vec):
    row_mean = jnp.mean(values, axis=-1, keepdims=True)
    centered = values - row_mean
    spread = jnp.mean(centered * centered, axis=-1, keepdims=True)
    return centered * lax.rsqrt(spread + EPSILON) * scale_vec + shift_vec


def gelu_exact(values):
    return jax.nn.gelu(values, approximate=False)


def collect_forward(shards):
    return (
        lax.all_gather(shards[0], "fsdp", axis=0, tiled=True),
        lax.all_gather(shards[1], "fsdp", axis=0, tiled=True),
        lax.all_gather(shards[2], "fsdp", axis=1, tiled=True),
        lax.all_gather(shards[3], "fsdp", axis=0, tiled=True),
        lax.all_gather(shards[4], "fsdp", axis=0, tiled=True),
        lax.all_gather(shards[5], "fsdp", axis=0, tiled=True),
        lax.all_gather(shards[6], "fsdp", axis=0, tiled=True),
        lax.all_gather(shards[7], "fsdp", axis=0, tiled=True),
        lax.all_gather(shards[8], "fsdp", axis=1, tiled=True),
        lax.all_gather(shards[9], "fsdp", axis=0, tiled=True),
        lax.all_gather(shards[10], "fsdp", axis=0, tiled=True),
        lax.all_gather(shards[11], "fsdp", axis=0, tiled=True),
    )


def collect_backward(shards):
    return (
        lax.all_gather(shards[0], "fsdp", axis=0, tiled=True),
        lax.all_gather(shards[2], "fsdp", axis=1, tiled=True),
        lax.all_gather(shards[4], "fsdp", axis=0, tiled=True),
        lax.all_gather(shards[6], "fsdp", axis=0, tiled=True),
        lax.all_gather(shards[8], "fsdp", axis=1, tiled=True),
        lax.all_gather(shards[10], "fsdp", axis=0, tiled=True),
    )


def attend_forward(packed, scale_value):
    queries, keysets, values, seq_len = packed
    scores = (
        jnp.einsum("qhe,khe->hqk", queries, keysets, preferred_element_type=jnp.float32)
        * scale_value
    )
    live_mask = jnp.arange(scores.shape[-1])[None, None, :] < seq_len
    scores = jnp.where(live_mask, scores, -1000000000.0)
    row_max = jnp.max(scores, axis=-1, keepdims=True)
    exp_scores = jnp.exp(scores - row_max)
    denom_sum = jnp.sum(exp_scores, axis=-1, keepdims=True)
    attn_probs = (exp_scores / denom_sum).astype(jnp.bfloat16)
    mixed_heads = jnp.einsum("hqk,khe->qhe", attn_probs, values, preferred_element_type=jnp.float32)
    return (mixed_heads.astype(jnp.bfloat16), (row_max + jnp.log(denom_sum))[:, :, 0])


def attend_backward(packed, scale_value):
    queries, keysets, values, seq_len, log_sums, d_mixed = packed
    scores = (
        jnp.einsum("qhe,khe->hqk", queries, keysets, preferred_element_type=jnp.float32)
        * scale_value
    )
    live_mask = jnp.arange(scores.shape[-1])[None, None, :] < seq_len
    attn_probs = jnp.where(live_mask, jnp.exp(scores - log_sums[:, :, None]), 0.0)
    low_probs = attn_probs.astype(jnp.bfloat16)
    d_value = jnp.einsum("hqk,qhe->khe", low_probs, d_mixed, preferred_element_type=jnp.float32)
    d_probs = jnp.einsum("qhe,khe->hqk", d_mixed, values, preferred_element_type=jnp.float32)
    row_delta = jnp.sum(attn_probs * d_probs, axis=-1, keepdims=True)
    d_scores = (attn_probs * (d_probs - row_delta)).astype(jnp.bfloat16)
    d_query = (
        jnp.einsum("hqk,khe->qhe", d_scores, keysets, preferred_element_type=jnp.float32)
        * scale_value
    )
    d_key = (
        jnp.einsum("hqk,qhe->khe", d_scores, queries, preferred_element_type=jnp.float32)
        * scale_value
    )
    return jnp.stack([d_query, d_key, d_value], axis=2).astype(jnp.bfloat16)


def generic_body(
    inputs,
    lengths,
    qkv_weight,
    qv_bias,
    out_weight,
    out_bias,
    norm1_gain,
    norm1_bias,
    up_weight,
    up_bias,
    down_weight,
    down_bias,
    norm2_gain,
    norm2_bias,
    cotangent,
):
    shards = (
        qkv_weight,
        qv_bias,
        out_weight,
        out_bias,
        norm1_gain,
        norm1_bias,
        up_weight,
        up_bias,
        down_weight,
        down_bias,
        norm2_gain,
        norm2_bias,
    )
    row_count = inputs.shape[1]
    mp_count = lax.axis_size("mp")
    mp_index = lax.axis_index("mp")
    up_cols = up_weight.shape[1]
    scale_value = DH ** (-0.5)
    group_rows = row_count * mp_count
    head_count = qkv_weight.shape[1] // (3 * DH)
    row_ids = mp_index * row_count + jnp.arange(row_count)
    seq_count = group_rows // L
    head_width = head_count * DH
    seq_ids = row_ids // L
    positions = row_ids % L
    seq_match = seq_ids[:, None] == jnp.arange(seq_count)[None, :]
    grad_qkv = jnp.zeros((D, 3 * head_width), jnp.float32)
    grad_qvb = jnp.zeros((2 * head_width,), jnp.float32)
    grad_out = jnp.zeros((head_width, D), jnp.float32)
    grad_up = jnp.zeros((D, up_cols), jnp.float32)
    grad_down = jnp.zeros((up_cols, D), jnp.float32)
    grad_upb = jnp.zeros((FF,), jnp.float32)
    grad_outb = jnp.zeros((D,), jnp.float32)
    grad_gain1 = jnp.zeros((D,), jnp.float32)
    grad_shift1 = jnp.zeros((D,), jnp.float32)
    grad_downb = jnp.zeros((D,), jnp.float32)
    grad_gain2 = jnp.zeros((D,), jnp.float32)
    grad_shift2 = jnp.zeros((D,), jnp.float32)
    layer_rows = []
    input_rows = []
    for micro_idx in range(MBS):
        fwd_set = collect_forward(shards)
        qkv_full, qvb_full, out_full, outb_full = (fwd_set[0], fwd_set[1], fwd_set[2], fwd_set[3])
        gain_one = fwd_set[4].astype(jnp.float32)
        shift_one = fwd_set[5].astype(jnp.float32)
        up_full, upb_full, down_full = (fwd_set[6], fwd_set[7].astype(jnp.float32), fwd_set[8])
        downb_full = fwd_set[9].astype(jnp.float32)
        gain_two = fwd_set[10].astype(jnp.float32)
        shift_two = fwd_set[11].astype(jnp.float32)
        tokens = inputs[micro_idx]
        upb_used = lax.dynamic_slice_in_dim(upb_full, mp_index * up_cols, up_cols, 0)
        gathered = lax.all_gather(tokens, "mp", axis=0, tiled=True)
        seq_lens = lengths[micro_idx]
        pair_bias = qvb_full.astype(jnp.float32).reshape(head_count, 2, DH)
        bias_full = jnp.stack(
            [pair_bias[:, 0], jnp.zeros_like(pair_bias[:, 0]), pair_bias[:, 1]], axis=1
        )
        project = jnp.dot(
            gathered, qkv_full, preferred_element_type=jnp.float32
        ) + bias_full.reshape(3 * head_width)
        project = project.astype(jnp.bfloat16).reshape(seq_count, L, head_count, 3, DH)
        queries = project[:, :, :, 0]
        keysets = project[:, :, :, 1]
        values = project[:, :, :, 2]
        mixed_heads, log_sums = lax.map(
            partial(attend_forward, scale_value=scale_value), (queries, keysets, values, seq_lens)
        )
        mixed_flat = mixed_heads.reshape(group_rows, head_width)
        attn_own = lax.psum_scatter(
            jnp.dot(mixed_flat, out_full, preferred_element_type=jnp.float32).astype(jnp.bfloat16),
            "mp",
            scatter_dimension=0,
            tiled=True,
        ).astype(jnp.float32)
        pre_norm1 = attn_own + outb_full.astype(jnp.float32) + tokens.astype(jnp.float32)
        hidden = normalize(pre_norm1, gain_one, shift_one)
        low_hidden = hidden.astype(jnp.bfloat16)
        ffn_rows = lax.all_gather(low_hidden, "mp", axis=0, tiled=True)
        inner_sum = jnp.dot(ffn_rows, up_full, preferred_element_type=jnp.float32) + upb_used
        activated = gelu_exact(inner_sum).astype(jnp.bfloat16)
        branch = lax.psum_scatter(
            jnp.dot(activated, down_full, preferred_element_type=jnp.float32).astype(jnp.bfloat16),
            "mp",
            scatter_dimension=0,
            tiled=True,
        ).astype(jnp.float32)
        pre_norm2 = branch + downb_full + hidden
        layer_rows.append(normalize(pre_norm2, gain_two, shift_two).astype(jnp.bfloat16))
        bwd_set = collect_backward(shards)
        qkv_back, out_back = (bwd_set[0], bwd_set[1])
        gain_one_back = bwd_set[2].astype(jnp.float32)
        up_back, down_back = (bwd_set[3], bwd_set[4])
        gain_two_back = bwd_set[5].astype(jnp.float32)
        row_len = jnp.sum(jnp.where(seq_match, seq_lens[None, :], 0), axis=1)
        live_rows = (positions < row_len).astype(jnp.float32)
        grad_rows = cotangent[micro_idx].astype(jnp.float32) * live_rows[:, None]
        _, pull_two = jax.vjp(normalize, pre_norm2, gain_two_back, shift_two)
        d_pre2, d_gain2, d_shift2 = pull_two(grad_rows)
        grad_gain2 = grad_gain2 + d_gain2
        grad_shift2 = grad_shift2 + d_shift2
        grad_downb = grad_downb + jnp.sum(d_pre2, axis=0)
        d_branch = d_pre2.astype(jnp.bfloat16)
        d_rows = lax.all_gather(d_branch, "mp", axis=0, tiled=True)
        d_act = lax.dot_general(
            d_rows, down_back, CONTRACT_COLS, preferred_element_type=jnp.float32
        )
        grad_down = grad_down + lax.dot_general(
            activated, d_rows, CONTRACT_ROWS, preferred_element_type=jnp.float32
        )
        _, pull_gelu = jax.vjp(gelu_exact, inner_sum)
        d_inner = pull_gelu(d_act)[0].astype(jnp.bfloat16)
        bias_term = jnp.sum(d_inner.astype(jnp.float32), axis=0)
        grad_up = grad_up + lax.dot_general(
            ffn_rows, d_inner, CONTRACT_ROWS, preferred_element_type=jnp.float32
        )
        grad_upb = grad_upb + lax.dynamic_update_slice_in_dim(
            jnp.zeros((FF,), jnp.float32), bias_term, mp_index * up_cols, 0
        )
        d_hidden_part = lax.psum_scatter(
            lax.dot_general(
                d_inner, up_back, CONTRACT_COLS, preferred_element_type=jnp.float32
            ).astype(jnp.bfloat16),
            "mp",
            scatter_dimension=0,
            tiled=True,
        ).astype(jnp.float32)
        d_hidden = d_pre2 + d_hidden_part
        _, pull_one = jax.vjp(normalize, pre_norm1, gain_one_back, shift_one)
        d_pre1, d_gain1, d_shift1 = pull_one(d_hidden)
        grad_gain1 = grad_gain1 + d_gain1
        grad_shift1 = grad_shift1 + d_shift1
        grad_outb = grad_outb + jnp.sum(d_pre1, axis=0)
        d_attended = d_pre1.astype(jnp.bfloat16)
        d_attn_rows = lax.all_gather(d_attended, "mp", axis=0, tiled=True)
        d_mixed = lax.dot_general(
            d_attn_rows, out_back, CONTRACT_COLS, preferred_element_type=jnp.float32
        )
        d_mixed = d_mixed.astype(jnp.bfloat16)
        grad_out = grad_out + lax.dot_general(
            mixed_flat, d_attn_rows, CONTRACT_ROWS, preferred_element_type=jnp.float32
        )
        d_project = lax.map(
            partial(attend_backward, scale_value=scale_value),
            (
                queries,
                keysets,
                values,
                seq_lens,
                log_sums,
                d_mixed.reshape(seq_count, L, head_count, DH),
            ),
        )
        d_flat = d_project.reshape(group_rows, 3 * head_width)
        grad_qkv = grad_qkv + lax.dot_general(
            gathered, d_flat, CONTRACT_ROWS, preferred_element_type=jnp.float32
        )
        bias_parts = jnp.sum(d_flat.astype(jnp.float32), axis=0).reshape(head_count, 3, DH)
        grad_qvb = grad_qvb + jnp.stack([bias_parts[:, 0], bias_parts[:, 2]], axis=1).reshape(
            2 * head_width
        )
        input_rows.append(
            d_pre1
            + lax.psum_scatter(
                lax.dot_general(
                    d_flat, qkv_back, CONTRACT_COLS, preferred_element_type=jnp.float32
                ).astype(jnp.bfloat16),
                "mp",
                scatter_dimension=0,
                tiled=True,
            ).astype(jnp.float32)
        )
    summed = (
        lax.psum_scatter(
            grad_qkv.astype(jnp.bfloat16), "fsdp", scatter_dimension=0, tiled=True
        ).astype(jnp.float32),
        lax.psum_scatter(
            grad_qvb.astype(jnp.bfloat16), "fsdp", scatter_dimension=0, tiled=True
        ).astype(jnp.float32),
        lax.psum_scatter(
            grad_out.astype(jnp.bfloat16), "fsdp", scatter_dimension=1, tiled=True
        ).astype(jnp.float32),
        lax.psum_scatter(
            grad_outb.astype(jnp.bfloat16), "fsdp", scatter_dimension=0, tiled=True
        ).astype(jnp.float32),
        lax.psum_scatter(
            grad_gain1.astype(jnp.bfloat16), "fsdp", scatter_dimension=0, tiled=True
        ).astype(jnp.float32),
        lax.psum_scatter(
            grad_shift1.astype(jnp.bfloat16), "fsdp", scatter_dimension=0, tiled=True
        ).astype(jnp.float32),
        lax.psum_scatter(
            grad_up.astype(jnp.bfloat16), "fsdp", scatter_dimension=0, tiled=True
        ).astype(jnp.float32),
        lax.psum_scatter(
            grad_upb.astype(jnp.bfloat16), "fsdp", scatter_dimension=0, tiled=True
        ).astype(jnp.float32),
        lax.psum_scatter(
            grad_down.astype(jnp.bfloat16), "fsdp", scatter_dimension=1, tiled=True
        ).astype(jnp.float32),
        lax.psum_scatter(
            grad_downb.astype(jnp.bfloat16), "fsdp", scatter_dimension=0, tiled=True
        ).astype(jnp.float32),
        lax.psum_scatter(
            grad_gain2.astype(jnp.bfloat16), "fsdp", scatter_dimension=0, tiled=True
        ).astype(jnp.float32),
        lax.psum_scatter(
            grad_shift2.astype(jnp.bfloat16), "fsdp", scatter_dimension=0, tiled=True
        ).astype(jnp.float32),
    )
    vectors = lax.psum(
        (summed[3], summed[4], summed[5], summed[7], summed[9], summed[10], summed[11]), "mp"
    )
    return (
        jnp.stack(layer_rows),
        jnp.stack(input_rows),
        summed[0],
        summed[1],
        summed[2],
        vectors[0],
        vectors[1],
        vectors[2],
        summed[6],
        vectors[3],
        summed[8],
        vectors[4],
        vectors[5],
        vectors[6],
    )


MESH_ID = pl.DeviceIdType.MESH
F32 = jnp.float32
BF16 = jnp.bfloat16
PLANES = 4
SIDE = 128
HALF = 512
KINDS = ("rows", "cols", "rows", "cols")
FIRST = (1, 2)
SECOND = (2, 1)


def place():
    f = lax.axis_index("fsdp")
    return f // 2, f % 2, lax.axis_index("mp")


def span(ref, kind, start, size):
    start = pl.multiple_of(start, SIDE)
    if kind == "rows":
        return ref.at[pl.ds(start, size), :]
    return ref.at[:, pl.ds(start, size)]


def remote(src, dst, send, recv, f, m):
    return pltpu.make_async_remote_copy(
        src_ref=src, dst_ref=dst, send_sem=send, recv_sem=recv, device_id=(f, m), device_id_type=MESH_ID
    )


def greet_start():
    z, c, m = place()
    me = (z * 2 + c) * 4 + m
    barrier = pltpu.get_barrier_semaphore()

    def hello(d, carry):
        other = (me + d) % 32
        pl.semaphore_signal(barrier, inc=1, device_id=(other // 4, other % 4), device_id_type=MESH_ID)
        return carry

    lax.fori_loop(1, 32, hello, 0)


def greet_end():
    pl.semaphore_wait(pltpu.get_barrier_semaphore(), 31)


ROWS_A = 320
ROWS_B = 192


class Spread:
    def __init__(self, shards, wholes, sems):
        self.shards, self.wholes = shards, wholes
        self.zs, self.zr, self.xs, self.xr, self.ys, self.yr, self.cs, self.cr, self.own = sems
        self.z, self.c, self.m = place()
        self.f = self.z * 2 + self.c

    def window(self, t, k, m, start, size):
        start = pl.multiple_of(start, SIDE)
        if t == 3:
            return self.wholes[3].at[k, m, pl.ds(0, ROWS_A), pl.ds(start, size)]
        if t == 4:
            return self.wholes[3].at[k, m, pl.ds(ROWS_A, ROWS_B), pl.ds(start, size)]
        return span(self.wholes[t].at[k, m], KINDS[t], start, size)

    def block(self, t, k):
        return self.window(t, k, self.m, self.c * HALF + self.z * SIDE, SIDE)

    def z_copy(self, t, k, d):
        z = (self.z + d) % PLANES
        return remote(
            self.shards[t][k], self.block(t, k), self.zs.at[t, k, d - 1], self.zr.at[t, k, d - 1], z * 2 + self.c, self.m
        )

    def own_copy(self, t, k):
        return pltpu.make_async_copy(self.shards[t][k], self.block(t, k), self.own.at[t, k])

    def x_copy(self, t, k):
        blk = self.window(t, k, self.m, self.c * HALF, HALF)
        return remote(blk, blk, self.xs.at[t, k], self.xr.at[t, k], self.f, self.m ^ FIRST[k])

    def y_copy(self, t, k, i):
        blk = self.window(t, k, self.m ^ (FIRST[k] if i else 0), self.c * HALF, HALF)
        return remote(blk, blk, self.ys.at[t, k, i], self.yr.at[t, k, i], self.f, self.m ^ SECOND[k])

    def c_copy(self, t, k, off):
        blk = self.window(t, k, self.m ^ off, self.c * HALF, HALF)
        return remote(blk, blk, self.cs.at[t, k, off], self.cr.at[t, k, off], self.z * 2 + 1 - self.c, self.m)

    def start(self, t, k):
        for d in range(1, PLANES):
            self.z_copy(t, k, d).start()
        self.own_copy(t, k).start()

    def enter(self, t, k):
        self.own_copy(t, k).wait()
        for d in range(1, PLANES):
            self.z_copy(t, k, d).wait_recv()
        self.x_copy(t, k).start()
        self.c_copy(t, k, 0).start()

    def second(self, t, k):
        self.y_copy(t, k, 0).start()

    def relay(self, t, k):
        self.x_copy(t, k).wait_recv()
        self.y_copy(t, k, 1).start()
        self.c_copy(t, k, FIRST[k]).start()

    def cross(self, t, k, i):
        self.y_copy(t, k, i).wait_recv()
        self.c_copy(t, k, 3 if i else SECOND[k]).start()

    def late_x(self, k):
        blk = self.block(4, k)
        return remote(self.shards[4][k], blk, self.xs.at[4, k], self.xr.at[4, k], self.f, self.m ^ FIRST[k])

    def late_y(self, k, i):
        dst = self.window(4, k, self.m ^ (FIRST[k] if i else 0), self.c * HALF + self.z * SIDE, SIDE)
        src = dst if i else self.shards[4][k]
        return remote(src, dst, self.ys.at[4, k, i], self.yr.at[4, k, i], self.f, self.m ^ SECOND[k])

    def plane(self, k, start, size):
        return self.wholes[3].at[k, :, pl.ds(ROWS_A, ROWS_B), pl.ds(pl.multiple_of(start, SIDE), size)]

    def late_z(self, k, d):
        z = (self.z + d) % PLANES
        blk = self.plane(k, self.c * HALF + self.z * SIDE, SIDE)
        return remote(blk, blk, self.zs.at[4, k, d - 1], self.zr.at[4, k, d - 1], z * 2 + self.c, self.m)

    def late_c(self, k):
        blk = self.plane(k, self.c * HALF, HALF)
        return remote(blk, blk, self.cs.at[4, k, 0], self.cr.at[4, k, 0], self.z * 2 + 1 - self.c, self.m)

    def late_start(self):
        for k in range(2):
            self.late_x(k).start()
            self.late_y(k, 0).start()
            self.own_copy(4, k).start()

    def late_relay(self):
        for k in range(2):
            self.late_x(k).wait_recv()
            self.late_y(k, 1).start()

    def late_planes(self):
        for k in range(2):
            self.own_copy(4, k).wait()
            self.late_y(k, 0).wait_recv()
            self.late_y(k, 1).wait_recv()
            for d in range(1, PLANES):
                self.late_z(k, d).start()

    def late_cross(self):
        for k in range(2):
            for d in range(1, PLANES):
                self.late_z(k, d).wait_recv()
            self.late_c(k).start()

    def drain(self):
        for k in range(2):
            for t in range(4):
                for d in range(1, PLANES):
                    self.z_copy(t, k, d).wait_send()
                self.x_copy(t, k).wait_send()
                self.y_copy(t, k, 0).wait_send()
                self.y_copy(t, k, 1).wait_send()
                for off in range(4):
                    self.c_copy(t, k, off).wait_send()
            self.late_x(k).wait_send()
            self.late_y(k, 0).wait_send()
            self.late_y(k, 1).wait_send()
            for d in range(1, PLANES):
                self.late_z(k, d).wait_send()
            self.late_c(k).wait_send()


def spread_sems():
    dma = pltpu.SemaphoreType.DMA
    return [
        dma((5, 2, 3)), dma((5, 2, 3)), dma((5, 2)), dma((5, 2)), dma((5, 2, 2)), dma((5, 2, 2)),
        dma((5, 2, 4)), dma((5, 2, 4)), dma((5, 2)),
    ]


def swap_vectors(src, dst, send, recv, chunked):
    z, c, m = place()
    f = z * 2 + c
    me = f * 4 + m

    def copy(d):
        other = (me + d) % 32
        fo, mo = other // 4, other % 4
        piece = src.at[mo * 8 + fo] if chunked else src
        return remote(piece, dst.at[m * 8 + f], send.at[d], recv.at[d], fo, mo)

    return copy


def share_vectors(src, dst, send, recv):
    z, c, m = place()
    f = z * 2 + c

    def copy(d):
        return remote(src, dst.at[f], send.at[d], recv.at[d], (f + d) % 8, m)

    return copy


def run_31(fn):
    def step(d, carry):
        fn(d)
        return carry

    lax.fori_loop(1, 32, step, 0)


WHOLE = ((2, 4, 1024, 384), (2, 4, 128, 1024), (2, 4, 1024, 512), (2, 4, 512, 1024))


def add_into(dst, src, step=64):
    rows = dst.shape[0]
    step = min(step, rows)

    def body(i, carry):
        r = pl.ds(pl.multiple_of(i * step, step), step)
        dst[r, :] = (dst[r, :].astype(F32) + src[r, :].astype(F32)).astype(BF16)
        return carry

    lax.fori_loop(0, rows // step, body, 0)


def fold_shapes():
    halves, blocks = [], []
    for (_, _, r, c), kind in zip(WHOLE, KINDS):
        halves.append((HALF, c) if kind == "rows" else (r, HALF))
        blocks.append((SIDE, c) if kind == "rows" else (r, SIDE))
    return halves, blocks


def fold_scratch():
    dma = pltpu.SemaphoreType.DMA
    halves, blocks = fold_shapes()
    return (
        [pltpu.VMEM((2, 4) + h, BF16) for h in halves]
        + [pltpu.VMEM((2, 2) + h, BF16) for h in halves]
        + [pltpu.VMEM((2,) + h, BF16) for h in halves]
        + [pltpu.VMEM((2, 3) + b, BF16) for b in blocks],
        [dma((4, 2, 4)), dma((4, 2, 4)), dma((4, 2, 2)), dma((4, 2, 2)), dma((4, 2)), dma((4, 2)),
         dma((4, 2, 3)), dma((4, 2, 3))],
    )


LOG2E = 1.4426950408889634
ERFC_P = 0.4
ERFC = (
    0.11596272084822187, 0.08090171204448858, 0.23416118618048126, -0.18548266222668147, 0.3545906580628177,
    -0.10013362874972173,
)
NT = (((1,), (1,)), ((), ()))
TN = (((0,), (0,)), ((), ()))


def mm(a, b):
    return jnp.dot(a, b, preferred_element_type=F32)


def mm_nt(a, b):
    return lax.dot_general(a, b, NT, preferred_element_type=F32)


def mm_tn(a, b):
    return lax.dot_general(a, b, TN, preferred_element_type=F32)


def aligned(start, size):
    return pl.ds(pl.multiple_of(start, size), size)


def gelu_pair(u):
    e = jnp.exp2(u * u * (-0.5 * LOG2E))
    d = 1.0 + (ERFC_P * 0.7071067811865476) * jnp.abs(u)
    t = pl.reciprocal(d, approx=True)
    t = t * (2.0 - d * t)
    p = ERFC[-1]
    for coef in ERFC[-2::-1]:
        p = p * t + coef
    tail = p * t * e
    phi = jnp.where(u >= 0.0, 1.0 - tail, tail)
    return u * phi, phi + u * (e * 0.3989422804014327)


def column_copies(hbm, vmem, sems, store):
    copies = []
    for s in range(2):
        for p in range(8):
            f = (p % 4) * 2 + p // 4
            outside = hbm.at[s, :, pl.ds(f * SIDE, SIDE)]
            inside = vmem.at[pl.ds(s * L, L), pl.ds(p * SIDE, SIDE)]
            pair = (inside, outside) if store else (outside, inside)
            copies.append(pltpu.make_async_copy(pair[0], pair[1], sems.at[s, p]))
    return copies


def lane_half(value, e):
    lane = lax.broadcasted_iota(jnp.int32, (1, value.shape[1]), 1)
    return jnp.where((lane < 64) if e == 0 else (lane >= 64), value, jnp.zeros_like(value))


def row_mean(v):
    return jnp.sum(v, axis=1, keepdims=True) * (1.0 / D)


def turn_out(m, idx):
    k, p = idx % 2, idx // 2
    off = jnp.where(p == 0, 0, jnp.where(p == 1, 1 + k, jnp.where(p == 2, 2 - k, 3)))
    return k, off, m ^ off


def forward_kernel(
    lens, x_hbm, cot_hbm, sqr, sor, sur, sdr, ob, g1, b1, db, g2, b2, ub, qb,
    y_hbm, wq_hbm, wo_hbm, wu_hbm, wd_hbm, qkv_hbm, p_hbm, mixed_hbm, lowh_hbm, n1_hbm, rs_hbm, act_hbm, gp_hbm,
    dpre_hbm, vec_out, gain_out,
    wq, wo, wu, wd, vec, x, sqp, sv, qst, pst, mixed, hid, lowh, act, gst, cot, yst, nst, rst, dst, dv, ubs, qvb, ust, sq,
    vecq,
    *sems,
):
    (vs, vr, us, ur, xsem, csem, ysem, wsem, qsem, psem, msem, gsem, nsem, dsem, asem) = sems[9:]
    z, c, m = place()
    zero = jnp.zeros((1, 128), F32)

    def prepare():
        for e in range(6):
            pair, part = e // 3, e % 3
            halves = [
                sqr[:, (pair * 2 + h) * 192 + part * 64:(pair * 2 + h) * 192 + part * 64 + 64].astype(F32)
                for h in range(2)
            ]
            sqp[pair, :, part * 128:part * 128 + 128] = jnp.concatenate(halves, axis=1).astype(BF16)
        q1 = qb[...].astype(F32)
        sv[...] = jnp.concatenate(
            [r[...].astype(F32) for r in (ob, g1, b1, db, g2, b2)] + [zero, zero, ub[...].astype(F32)]
            + [zero, zero, zero, zero], axis=0
        ).astype(BF16)
        sq[...] = jnp.concatenate([q1, q1], axis=1)

    greet_start()
    prepare()
    greet_end()
    shards = (
        [sqp.at[k] for k in range(2)],
        [sor.at[pl.ds(k * 128, 128), :] for k in range(2)],
        [sur.at[:, pl.ds(k * HALF, HALF)] for k in range(2)],
        [sdr.at[pl.ds(k * HALF, ROWS_A), :] for k in range(2)],
        [sdr.at[pl.ds(k * HALF + ROWS_A, ROWS_B), :] for k in range(2)],
    )
    spread = Spread(shards, (wq, wo, wu, wd), sems[:9])
    spread.start(0, 0)
    spread.late_start()
    vcopy = share_vectors(sv, vec, us, ur)
    for d in range(1, 8):
        vcopy(d).start()
    qcopy = swap_vectors(sq, vecq, vs, vr, False)
    run_31(lambda d: qcopy(d).start())
    vec[z * 2 + c] = sv[...]
    vecq[m * 8 + z * 2 + c] = sq[...]
    x_copies = column_copies(x_hbm, x, xsem, False)
    c_copies = column_copies(cot_hbm, cot, csem, False)
    for cp in x_copies:
        cp.start()
    spread.late_relay()
    spread.enter(0, 0)
    spread.second(0, 0)
    spread.start(0, 1)
    spread.start(1, 0)
    for d in range(1, 8):
        vcopy(d).wait()
    run_31(lambda d: qcopy(d).wait())
    for p in range(8):
        dv[:, p * SIDE:(p + 1) * SIDE] = vec[(p % 4) * 2 + p // 4].astype(F32)[0:8]
    lane = lax.broadcasted_iota(jnp.int32, (1, 128), 1)
    for j in range(8):
        k, mo = j // 4, j % 4
        t = vec[mo * 2 + k].astype(F32)
        ubs[j] = jnp.concatenate([t[8:9], t[9:10], t[10:11], t[11:12]], axis=1)
        rows = [vecq[mo * 8 + 4 * k + i] for i in range(4)]
        qvb[j] = jnp.concatenate(
            [jnp.where(lane < 64, rows[0], rows[2]), zero, jnp.where(lane < 64, rows[1], rows[3])], axis=1
        )
    for cp in x_copies:
        cp.wait()
    for cp in c_copies:
        cp.start()

    def w_copy(t, idx):
        k, _, mo = turn_out(m, idx)
        src, dst = ((wq, wq_hbm), (wo, wo_hbm), (wu, wu_hbm), (wd, wd_hbm))[t]
        return pltpu.make_async_copy(src.at[k, mo], dst.at[k, mo], wsem.at[t, idx])

    def q_copy(it):
        k, _, mo = turn_out(m, it // 2)
        s = it % 2
        return pltpu.make_async_copy(qst.at[s], qkv_hbm.at[k * 4 + mo, aligned(s * L, L), :], qsem.at[s])

    def p_copy(it):
        k, _, mo = turn_out(m, it // 2)
        s = it % 2
        return pltpu.make_async_copy(pst.at[s], p_hbm.at[k * 4 + mo, s], psem.at[s])

    def attend(it, carry):
        idx, s = it // 2, it % 2
        k, off, mo = turn_out(m, idx)
        j = k * 4 + mo
        rows = aligned(s * L, L)

        @pl.when(it == 2)
        def _():
            spread.enter(0, 1)
            spread.second(0, 1)
            spread.start(1, 1)
            spread.start(2, 0)
            spread.relay(0, 0)
            spread.cross(0, 0, 0)

        @pl.when(it == 4)
        def _():
            spread.enter(1, 0)
            spread.second(1, 0)

        @pl.when(it == 6)
        def _():
            spread.enter(1, 1)
            spread.second(1, 1)
            spread.relay(0, 1)
            spread.cross(0, 1, 0)
            spread.start(2, 1)

        @pl.when(it == 8)
        def _():
            spread.cross(0, 0, 1)

        @pl.when(it == 10)
        def _():
            spread.cross(0, 1, 1)
            spread.enter(2, 0)
            spread.second(2, 0)
            spread.start(3, 0)
            spread.relay(1, 0)
            spread.relay(1, 1)

        @pl.when(it == 12)
        def _():
            spread.cross(1, 0, 0)
            spread.cross(1, 1, 0)

        @pl.when(it == 14)
        def _():
            spread.cross(1, 0, 1)
            spread.cross(1, 1, 1)
            spread.enter(2, 1)
            spread.second(2, 1)
            spread.start(3, 1)

        @pl.when(s == 0)
        def _():
            spread.c_copy(0, k, off).wait_recv()
            w_copy(0, idx).start()

        @pl.when(it >= 2)
        def _():
            q_copy(it - 2).wait()
            p_copy(it - 2).wait()

        qst[s] = (mm(x[rows, :], wq[k, mo]) + qvb[j]).astype(BF16)
        q_copy(it).start()
        keys, values = qst[s, :, 128:256], qst[s, :, 256:384]
        length = lens[s, m]
        bias = jnp.where(lax.broadcasted_iota(jnp.int32, (1, L), 1) < length, 0.0, -1e30)
        out = [None, None]
        for e in range(2):
            k_e, v_e = lane_half(keys, e), lane_half(values, e)
            for h in range(2):
                half = slice(h * 256, h * 256 + 256)
                scores = mm_nt(qst[s, half, 0:128], k_e) + bias
                top = jnp.max(scores, axis=1, keepdims=True)
                ex = jnp.exp2((scores - top) * (LOG2E * DH ** (-0.5)))
                probs = (ex * (1.0 / jnp.sum(ex, axis=1, keepdims=True))).astype(BF16)
                pst[s, e, half, :] = probs
                part = mm(probs, v_e)
                out[h] = part if out[h] is None else out[h] + part
        p_copy(it).start()
        mixed[rows, aligned(j * 128, 128)] = jnp.concatenate(out, axis=0).astype(BF16)
        return carry

    lax.fori_loop(0, 16, attend, 0)
    for it in (14, 15):
        q_copy(it).wait()
        p_copy(it).wait()
    m_copy = pltpu.make_async_copy(mixed, mixed_hbm, msem.at[0])
    m_copy.start()
    spread.late_planes()
    for k in range(2):
        for off in range(4):
            spread.c_copy(1, k, off).wait_recv()
    for idx in range(8):
        w_copy(1, idx).start()

    def n_copy(i):
        return pltpu.make_async_copy(nst.at[i % 2], n1_hbm.at[aligned(i * 256, 256), :], nsem.at[i % 2])

    def r_copy(i):
        return pltpu.make_async_copy(rst.at[i % 2], rs_hbm.at[aligned(i * 256, 256), :], nsem.at[2 + i % 2])

    def first_norm(i, carry):
        rows = aligned(i * 256, 256)

        @pl.when(i >= 2)
        def _():
            n_copy(i - 2).wait()
            r_copy(i - 2).wait()

        pre = mm(mixed[rows, :], wo[...].reshape(D, D)) + dv[0:1] + x[rows, :].astype(F32)
        cen = pre - row_mean(pre)
        inv = lax.rsqrt(row_mean(cen * cen) + EPSILON)
        n = cen * inv
        nst[i % 2] = n
        rst[i % 2] = jnp.broadcast_to(inv, (256, 128))
        n_copy(i).start()
        r_copy(i).start()
        h = n * dv[1:2] + dv[2:3]
        hid[rows, :] = h
        lowh[rows, :] = h.astype(BF16)
        return carry

    lax.fori_loop(0, 4, first_norm, 0)
    for i in (2, 3):
        n_copy(i).wait()
        r_copy(i).wait()
    h_copy = pltpu.make_async_copy(lowh, lowh_hbm, msem.at[1])
    h_copy.start()

    def g_copy(i):
        k, _, mo = turn_out(m, i)
        return pltpu.make_async_copy(gst.at[i % 2], gp_hbm.at[k * 4 + mo], gsem.at[i % 2])

    def a_copy(i):
        k, _, mo = turn_out(m, i)
        j = k * 4 + mo
        return pltpu.make_async_copy(act.at[:, aligned(j * HALF, HALF)], act_hbm.at[j], asem.at[i])

    def up(idx, carry):
        k, off, mo = turn_out(m, idx)
        j = k * 4 + mo
        cols = aligned(j * HALF, HALF)

        @pl.when(idx == 0)
        def _():
            spread.relay(2, 0)
            spread.cross(2, 0, 0)

        @pl.when(idx == 1)
        def _():
            spread.relay(2, 1)
            spread.cross(2, 1, 0)
            spread.enter(3, 0)
            spread.second(3, 0)

        @pl.when(idx == 3)
        def _():
            spread.enter(3, 1)
            spread.second(3, 1)

        @pl.when(idx == 6)
        def _():
            spread.cross(2, 0, 1)
            spread.cross(2, 1, 1)

        spread.c_copy(2, k, off).wait_recv()
        w_copy(2, idx).start()

        @pl.when(idx >= 2)
        def _():
            g_copy(idx - 2).wait()

        w = wu[k, mo]
        ust[0] = mm(lowh[0:256, :], w)
        for h in range(4):
            if h < 3:
                ust[(h + 1) % 2] = mm(lowh[h * 256 + 256:h * 256 + 512, :], w)
            bias = ubs[j]
            for r in range(0, 256, 16):
                sub = slice(h * 256 + r, h * 256 + r + 16)
                a, g = gelu_pair(ust[h % 2, r:r + 16, :] + bias)
                act[sub, cols] = a.astype(BF16)
                gst[idx % 2, sub, :] = g.astype(BF16)
        g_copy(idx).start()
        a_copy(idx).start()
        return carry

    lax.fori_loop(0, 8, up, 0)
    gain_out[...] = jnp.zeros((8, D), F32)
    vec_out[...] = dv[...]
    spread.relay(3, 0)
    spread.cross(3, 0, 0)
    spread.relay(3, 1)
    spread.cross(3, 1, 0)
    spread.late_cross()
    for k in range(2):
        spread.late_c(k).wait_recv()

    def down(idx, carry):
        k, off, mo = turn_out(m, idx)
        cols = aligned((k * 4 + mo) * HALF, HALF)

        @pl.when(idx == 4)
        def _():
            spread.cross(3, 0, 1)
            spread.cross(3, 1, 1)

        spread.c_copy(3, k, off).wait_recv()
        w_copy(3, idx).start()
        for r in range(2):
            for h in range(2):
                rows, side = slice(r * L, r * L + L), slice(h * HALF, h * HALF + HALF)
                hid[rows, side] += mm(act[rows, cols], wd[k, mo, :, side])
        return carry

    lax.fori_loop(0, 8, down, 0)

    def d_copy(i):
        return pltpu.make_async_copy(dst.at[i % 2], dpre_hbm.at[aligned(i * 256, 256), :], dsem.at[i % 2])

    def second_norm(i, carry):
        rows = aligned(i * 256, 256)

        @pl.when(i >= 2)
        def _():
            d_copy(i - 2).wait()

        pre = hid[rows, :] + dv[3:4]
        cen = pre - row_mean(pre)
        inv = lax.rsqrt(row_mean(cen * cen) + EPSILON)
        n = cen * inv
        yst[rows, :] = (n * dv[4:5] + dv[5:6]).astype(BF16)
        pos = (i % 2) * 256 + lax.broadcasted_iota(jnp.int32, (256, 1), 0)
        grad = jnp.where(pos < lens[i // 2, m], cot[rows, :].astype(F32), 0.0)
        g = grad * dv[4:5]
        back = inv * (g - row_mean(g) - n * row_mean(g * n))
        dst[i % 2] = back
        d_copy(i).start()
        gain_out[3:4, :] += jnp.sum(back, axis=0, keepdims=True)
        gain_out[4:5, :] += jnp.sum(grad * n, axis=0, keepdims=True)
        gain_out[5:6, :] += jnp.sum(grad, axis=0, keepdims=True)
        return carry

    for cp in c_copies:
        cp.wait()
    lax.fori_loop(0, 4, second_norm, 0)
    y_copies = column_copies(y_hbm, yst, ysem, True)
    for cp in y_copies:
        cp.start()
    for i in (2, 3):
        d_copy(i).wait()
    for i in (6, 7):
        g_copy(i).wait()

    def finish(i, carry):
        a_copy(i).wait()
        for t in range(4):
            w_copy(t, i).wait()
        return carry

    lax.fori_loop(0, 8, finish, 0)
    m_copy.wait()
    h_copy.wait()
    for cp in y_copies:
        cp.wait()
    spread.drain()


SAVED = (
    ((8, 1024, 384), BF16), ((8, 2, 2, L, L), BF16), ((1024, D), BF16), ((1024, D), BF16), ((1024, D), F32),
    ((1024, 128), F32), ((8, 1024, HALF), BF16), ((8, 1024, HALF), BF16), ((1024, D), F32),
)


def forward(lengths, inputs, cotangent, weights, vectors):
    vm = pl.BlockSpec(memory_space=pltpu.VMEM)
    anywhere = pl.BlockSpec(memory_space=pl.ANY)
    shape = jax.ShapeDtypeStruct
    dma = pltpu.SemaphoreType.DMA
    v = pltpu.VMEM
    scratch = [v(s, BF16) for s in WHOLE] + [
        v((8, 16, 128), BF16), v((1024, D), BF16), v((2, 128, 384), BF16), v((16, 128), BF16), v((2, L, 384), BF16),
        v((2, 2, L, L), BF16), v((1024, D), BF16), v((1024, D), F32), v((1024, D), BF16), v((1024, FF), BF16),
        v((2, 1024, HALF), BF16), v((1024, D), BF16), v((1024, D), BF16), v((2, 256, D), F32), v((2, 256, 128), F32),
        v((2, 256, D), F32), v((8, D), F32), v((8, 1, HALF), F32), v((8, 1, 384), F32), v((2, 256, HALF), F32), v((1, 128), F32),
        v((32, 1, 128), F32),
    ] + spread_sems() + [
        dma((32,)), dma((32,)), dma((8,)), dma((8,)), dma((2, 8)), dma((2, 8)), dma((2, 8)), dma((4, 8)), dma((2,)), dma((2,)), dma((2,)),
        dma((2,)), dma((4,)), dma((2,)), dma((8,)),
    ]
    return pl.pallas_call(
        forward_kernel,
        out_shape=[shape((2, L, D), BF16)] + [shape(s, BF16) for s in WHOLE] + [shape(s, d) for s, d in SAVED]
        + [shape((8, D), F32), shape((8, D), F32)],
        in_specs=[pl.BlockSpec(memory_space=pltpu.SMEM), anywhere, anywhere] + [vm] * 12,
        out_specs=[anywhere] * 14 + [vm, vm],
        scratch_shapes=scratch,
        compiler_params=pltpu.CompilerParams(collective_id=0, has_side_effects=True, vmem_limit_bytes=67000000),
    )(lengths, inputs, cotangent, *weights, *vectors)

class Fold:
    def __init__(self, rc, rx, ry, rz, sems):
        self.rc, self.rx, self.ry, self.rz = rc, rx, ry, rz
        self.cs, self.cr, self.xs, self.xr, self.ys, self.yr, self.zs, self.zr = sems
        self.z, self.c, self.m = place()

    def c_copy(self, t, k, off, src):
        return remote(
            src, self.rc[t].at[k, self.m ^ off], self.cs.at[t, k, off], self.cr.at[t, k, off],
            self.z * 2 + 1 - self.c, self.m,
        )

    def x_copy(self, t, k, i):
        m = self.m ^ (3 if i else 1 + k)
        return remote(
            self.rc[t].at[k, m], self.rx[t].at[k, i], self.xs.at[t, k, i], self.xr.at[t, k, i],
            self.z * 2 + self.c, self.m ^ (1 + k),
        )

    def y_copy(self, t, k):
        m = self.m ^ (2 - k)
        return remote(
            self.rc[t].at[k, m], self.ry[t].at[k], self.ys.at[t, k], self.yr.at[t, k], self.z * 2 + self.c, m
        )

    def z_copy(self, t, k, d):
        z = (self.z + d) % PLANES
        src = span(self.rc[t].at[k, self.m], KINDS[t], z * SIDE, SIDE)
        return remote(
            src, self.rz[t].at[k, d - 1], self.zs.at[t, k, d - 1], self.zr.at[t, k, d - 1], z * 2 + self.c, self.m
        )

    def to_y(self, t, k):
        self.x_copy(t, k, 1).wait_recv()
        add_into(self.rc[t].at[k, self.m ^ (2 - k)], self.rx[t].at[k, 1])
        self.y_copy(t, k).start()

    def to_z(self, t, k):
        self.x_copy(t, k, 0).wait_recv()
        add_into(self.rc[t].at[k, self.m], self.rx[t].at[k, 0])
        self.y_copy(t, k).wait_recv()
        add_into(self.rc[t].at[k, self.m], self.ry[t].at[k])
        for d in range(1, PLANES):
            self.z_copy(t, k, d).start()

    def total(self, t, k):
        for d in range(1, PLANES):
            self.z_copy(t, k, d).wait_recv()
        own = span(self.rc[t].at[k, self.m], KINDS[t], self.z * SIDE, SIDE)[...].astype(F32)
        rz = self.rz[t]
        return own + rz[k, 0].astype(F32) + rz[k, 1].astype(F32) + rz[k, 2].astype(F32)

    def drain(self, t, k):
        self.x_copy(t, k, 0).wait_send()
        self.x_copy(t, k, 1).wait_send()
        self.y_copy(t, k).wait_send()
        for d in range(1, PLANES):
            self.z_copy(t, k, d).wait_send()


def backward_kernel(
    x_hbm, wq_hbm, wo_hbm, wu_hbm, wd_hbm, qkv_hbm, p_hbm, mixed_hbm, lowh_hbm, n1_hbm, rs_hbm, act_hbm, gp_hbm,
    dpre_hbm, dv, gains,
    ig_hbm, oq, oo, ou, od, ov,
    *rest,
):
    rc, rx, ry, rz = rest[0:4], rest[4:8], rest[8:12], rest[12:16]
    (dbr, dh, low, wdj, wuj, ag, gd, gu, mixed, dmix, qkvj, dproj, nst, rst, rv, gv, sums, ubg, qvg, rw, gw) = rest[16:37]
    fold = Fold(rc, rx, ry, rz, rest[37:45])
    vs, vr, us, ur, lsem, psem, ssem, nsem, isem, xsem = rest[45:]
    z, c, m = place()
    other = 1 - c
    mine, theirs = aligned(c * HALF, HALF), aligned(other * HALF, HALF)

    def turn(idx):
        k, p = idx % 2, idx // 2
        off = jnp.where(p == 0, 3, jnp.where(p == 1, 1 + k, jnp.where(p == 2, 2 - k, 0)))
        return k, p, off

    def down_loads(idx):
        k, _, off = turn(idx)
        mo, slot = m ^ off, idx % 2
        j = k * 4 + mo
        pairs = ((wd_hbm.at[k, mo], wdj.at[slot]), (act_hbm.at[j], ag.at[slot, 0]), (gp_hbm.at[j], ag.at[slot, 1]))
        return [pltpu.make_async_copy(a, b, lsem.at[slot, i]) for i, (a, b) in enumerate(pairs)]

    def up_load(idx):
        k, _, off = turn(idx)
        return pltpu.make_async_copy(wu_hbm.at[k, m ^ off], wuj.at[idx % 2], lsem.at[idx % 2, 3])

    greet_start()
    dp_copy = pltpu.make_async_copy(dpre_hbm, dh, ssem.at[0])
    dp_copy.start()
    for cp in down_loads(0):
        cp.start()
    lh_copy = pltpu.make_async_copy(lowh_hbm, low, ssem.at[1])
    mx_copy = pltpu.make_async_copy(mixed_hbm, mixed, ssem.at[2])
    sums[...] = gains[...]
    dp_copy.wait()

    def cast(i, carry):
        rows = aligned(i * 128, 128)
        dbr[rows, :] = dh[rows, :].astype(BF16)
        return carry

    lax.fori_loop(0, 8, cast, 0)

    def settle_ffn(t, idx, own):
        k, p, off = turn(idx)
        mo = m ^ off
        fold.c_copy(t, k, off, gd.at[idx % 2]).wait()
        add_into(rc[t].at[k, mo], own.at[idx % 2])

        @pl.when(p == 0)
        def _():
            fold.x_copy(t, k, 1).start()

        @pl.when(p == 1)
        def _():
            fold.x_copy(t, k, 0).start()

    def down_step(idx, carry):
        k, p, off = turn(idx)
        mo, slot = m ^ off, idx % 2
        for cp in down_loads(idx):
            cp.wait()

        @pl.when(idx < 7)
        def _():
            for cp in down_loads(idx + 1):
                cp.start()

        @pl.when(idx == 3)
        def _():
            lh_copy.start()
            up_load(0).start()
            up_load(1).start()

        @pl.when(idx == 5)
        def _():
            mx_copy.start()

        total = jnp.zeros((1, HALF), F32)
        for r in range(2):
            rows = slice(r * L, r * L + L)
            d = (mm_nt(dbr[rows, :], wdj[slot]) * ag[slot, 1, rows, :].astype(F32)).astype(BF16)
            dproj[idx, rows, :] = d
            total = total + jnp.sum(d.astype(F32), axis=0, keepdims=True)
        ubg[k * 4 + mo] = total
        gd[slot] = mm_tn(ag[slot, 0], dbr[:, theirs]).astype(BF16)

        @pl.when(idx == 0)
        def _():
            greet_end()

        fold.c_copy(3, k, off, gd.at[slot]).start()
        gu[slot] = mm_tn(ag[slot, 0], dbr[:, mine]).astype(BF16)

        @pl.when(idx >= 1)
        def _():
            settle_ffn(3, idx - 1, gu)

        return carry

    lax.fori_loop(0, 8, down_step, 0)
    lh_copy.wait()
    for k in range(2):
        fold.to_y(3, k)

    def up_step(idx, carry):
        k, p, off = turn(idx)
        slot = idx % 2
        gd[slot] = mm_tn(low[:, theirs], dproj[idx]).astype(BF16)
        fold.c_copy(2, k, off, gd.at[slot]).start()
        gu[slot] = mm_tn(low[:, mine], dproj[idx]).astype(BF16)
        up_load(idx).wait()
        for r in range(2):
            for h in range(2):
                rows, cols = slice(r * L, r * L + L), slice(h * HALF, h * HALF + HALF)
                dh[rows, cols] += mm_nt(dproj[idx, rows, :], wuj[slot, cols, :])

        @pl.when(idx < 6)
        def _():
            up_load(idx + 2).start()

        @pl.when(idx == 0)
        def _():
            settle_ffn(3, 7, gu)

        @pl.when(idx == 7)
        def _():
            fold.to_z(3, 1)
            fold.to_z(3, 0)

        @pl.when(idx >= 1)
        def _():
            settle_ffn(2, idx - 1, gu)

        return carry

    lax.fori_loop(0, 8, up_step, 0)

    def norm_loads(i):
        rows, slot = aligned(i * 256, 256), i % 2
        return (
            pltpu.make_async_copy(n1_hbm.at[rows, :], nst.at[slot], nsem.at[slot, 0]),
            pltpu.make_async_copy(rs_hbm.at[rows, :], rst.at[slot], nsem.at[slot, 1]),
        )

    for cp in norm_loads(0):
        cp.start()
    wo_copies = [
        pltpu.make_async_copy(
            wo_hbm.at[j // 4, j % 4], wdj.at[j // 4, pl.ds((j % 4) * 128, 128), :], lsem.at[j // 4, j % 4]
        )
        for j in range(8)
    ]
    for cp in wo_copies:
        cp.start()
    x_copies = column_copies(x_hbm, low, xsem, False)
    for cp in x_copies:
        cp.start()

    def attn_loads(idx):
        k, _, off = turn(idx)
        j, slot = k * 4 + (m ^ off), idx % 2
        copies = [pltpu.make_async_copy(qkv_hbm.at[j], qkvj.at[slot], psem.at[slot, 4])]
        for s in range(2):
            for e in range(2):
                copies.append(
                    pltpu.make_async_copy(
                        p_hbm.at[j, s, e], ag.at[slot, s, pl.ds(e * L, L), :], psem.at[slot, 2 * s + e]
                    )
                )
        return copies

    for cp in attn_loads(0):
        cp.start()

    def first_back(i, carry):
        rows, slot = aligned(i * 256, 256), i % 2

        @pl.when(i < 3)
        def _():
            for cp in norm_loads(i + 1):
                cp.start()

        for cp in norm_loads(i):
            cp.wait()
        grad, n = dh[rows, :], nst[slot]
        g = grad * dv[1:2]
        inv = rst[slot][:, 0:1]
        back = inv * (g - row_mean(g) - n * row_mean(g * n))
        dh[rows, :] = back
        dbr[rows, :] = back.astype(BF16)
        sums[0:1, :] += jnp.sum(back, axis=0, keepdims=True)
        sums[1:2, :] += jnp.sum(grad * n, axis=0, keepdims=True)
        sums[2:3, :] += jnp.sum(grad, axis=0, keepdims=True)
        return carry

    lax.fori_loop(0, 4, first_back, 0)
    settle_ffn(2, 7, gu)
    mx_copy.wait()
    for h in range(2):
        rows = slice(h * L, h * L + L)
        wuj[0, rows, :] = mm_tn(mixed[:, rows], dbr[:, theirs]).astype(BF16)
    for k in range(2):
        for off in range(4):
            src = wuj.at[0, aligned((k * 4 + (m ^ off)) * 128, 128), :]
            fold.c_copy(1, k, off, src).start()
    for cp in wo_copies:
        cp.wait()
    for h in range(2):
        rows = slice(h * L, h * L + L)
        for q in range(2):
            dmix[rows, q * L:q * L + L] = mm_nt(dbr[rows, :], wdj[q]).astype(BF16)
    for h in range(2):
        rows = slice(h * L, h * L + L)
        wuj[1, rows, :] = mm_tn(mixed[:, rows], dbr[:, mine]).astype(BF16)
    for k in range(2):
        for off in (3, 1 + k, 2 - k, 0):
            src = wuj.at[0, aligned((k * 4 + (m ^ off)) * 128, 128), :]
            fold.c_copy(1, k, off, src).wait()
            add_into(rc[1].at[k, m ^ off], wuj.at[1, aligned((k * 4 + (m ^ off)) * 128, 128), :])
            if off == 3:
                fold.x_copy(1, k, 1).start()
            elif off == 1 + k:
                fold.x_copy(1, k, 0).start()
    for cp in x_copies:
        cp.wait()

    def piece(idx):
        return gu.at[idx % 2, :, pl.ds(0, 384)]

    def attend(idx, s):
        k, _, off = turn(idx)
        mo, slot = m ^ off, idx % 2
        j = k * 4 + mo
        rows = slice(s * L, s * L + L)
        dout = dmix[rows, aligned(j * 128, 128)]
        queries, keys, values = (qkvj[slot, rows, i * 128:i * 128 + 128] for i in range(3))
        dq = dk = dval = None
        for e in range(2):
            probs = ag[slot, s, e * L:e * L + L, :]
            p32 = probs.astype(F32)
            t = p32 * mm_nt(dout, lane_half(values, e))
            ds = (t - p32 * jnp.sum(t, axis=1, keepdims=True)).astype(BF16)
            parts = (mm(ds, lane_half(keys, e)), mm_tn(ds, lane_half(queries, e)), mm_tn(probs, lane_half(dout, e)))
            dq, dk, dval = parts if e == 0 else (dq + parts[0], dk + parts[1], dval + parts[2])
        scale = DH ** (-0.5)
        out = jnp.concatenate([dq * scale, dk * scale, dval], axis=1).astype(BF16)
        dproj[idx, rows, 0:384] = out
        return jnp.sum(out.astype(F32), axis=0, keepdims=True)

    def settle(idx):
        k, p, off = turn(idx)
        mo = m ^ off
        fold.c_copy(0, k, off, piece(idx)).wait()
        rc[0][k, mo] = (mm_tn(low[:, mine], dproj[idx, :, 0:384]) + rc[0][k, mo].astype(F32)).astype(BF16)

        @pl.when(p == 0)
        def _():
            fold.x_copy(0, k, 1).start()

        @pl.when(p == 1)
        def _():
            fold.x_copy(0, k, 0).start()

        @pl.when(p == 2)
        def _():
            fold.to_y(0, k)

        @pl.when(p == 3)
        def _():
            fold.to_z(0, k)

    def heads(idx, carry):
        k, p, off = turn(idx)
        j = k * 4 + (m ^ off)
        for cp in attn_loads(idx):
            cp.wait()

        @pl.when(idx < 7)
        def _():
            for cp in attn_loads(idx + 1):
                cp.start()

        qvg[j] = attend(idx, 0) + attend(idx, 1)

        @pl.when(idx >= 1)
        def _():
            settle(idx - 1)

        gu[idx % 2, :, 0:384] = mm_tn(low[:, theirs], dproj[idx, :, 0:384]).astype(BF16)
        fold.c_copy(0, k, off, piece(idx)).start()

        @pl.when(idx == 0)
        def _():
            fold.to_y(2, 0)
            fold.to_y(2, 1)

        @pl.when(idx == 2)
        def _():
            fold.to_y(1, 0)
            fold.to_y(1, 1)

        @pl.when(idx == 3)
        def _():
            fold.to_z(2, 1)
            fold.to_z(2, 0)

        @pl.when(idx == 5)
        def _():
            fold.to_z(1, 0)
            fold.to_z(1, 1)

        return carry

    for f in range(8):
        p = (f % 2) * 4 + f // 2
        ub = ubg[p]
        pad = jnp.zeros((4, 128), F32)
        tile = jnp.concatenate(
            [sums[:, p * SIDE:(p + 1) * SIDE]] + [ub[:, i * 128:i * 128 + 128] for i in range(4)] + [pad], axis=0
        ).astype(BF16)
        for mo in range(4):
            gv[mo * 8 + f] = tile
    vcopy = swap_vectors(gv, rv, us, ur, True)
    run_31(lambda d: vcopy(d).start())
    me = m * 8 + z * 2 + c
    rv[me] = gv[me]
    lax.fori_loop(0, 8, heads, 0)

    def wq_load(idx):
        k, _, off = turn(idx)
        return pltpu.make_async_copy(wq_hbm.at[k, m ^ off], qkvj.at[idx % 2], psem.at[idx % 2, 4])

    wq_load(0).start()
    wq_load(1).start()
    settle(7)
    for f in range(8):
        for mo in range(4):
            kk, e, part = f // 4, (f // 2) % 2, f % 2
            qv = qvg[kk * 4 + mo][:, part * 256 + e * 64:part * 256 + e * 64 + 64]
            gw[mo * 8 + f] = jnp.concatenate([qv, qv], axis=1)
    wcopy = swap_vectors(gw, rw, vs, vr, True)
    run_31(lambda d: wcopy(d).start())
    rw[me] = gw[me]

    def pull(idx, carry):
        slot = idx % 2
        wq_load(idx).wait()
        for r in range(2):
            for h in range(2):
                rows, cols = slice(r * L, r * L + L), slice(h * HALF, h * HALF + HALF)
                dh[rows, cols] += mm_nt(dproj[idx, rows, 0:384], qkvj[slot, cols, :])

        @pl.when(idx < 6)
        def _():
            wq_load(idx + 2).start()

        return carry

    lax.fori_loop(0, 8, pull, 0)
    i_copies = column_copies(ig_hbm, dh, isem, True)
    for cp in i_copies:
        cp.start()
    run_31(lambda d: vcopy(d).wait())
    run_31(lambda d: wcopy(d).wait())

    def gather_sum(i, acc):
        return acc[0] + rv[i].astype(F32), acc[1] + rw[i]

    wide, narrow = lax.fori_loop(0, 32, gather_sum, (jnp.zeros((16, 128), F32), jnp.zeros((1, 128), F32)))
    ov[...] = wide
    ov[12:13, :] = narrow
    for k in range(2):
        od[k * HALF:k * HALF + HALF, :] = fold.total(3, k)
        ou[:, k * HALF:k * HALF + HALF] = fold.total(2, k)
        oo[k * 128:k * 128 + 128, :] = fold.total(1, k)
    for k in range(2):
        t = fold.total(0, k)
        parts = [t[:, i * 128 + e * 64:i * 128 + e * 64 + 64] for e in range(2) for i in range(3)]
        oq[:, k * 384:k * 384 + 384] = jnp.concatenate(parts, axis=1)
    for cp in i_copies:
        cp.wait()
    for t in range(4):
        for k in range(2):
            fold.drain(t, k)


def export_kernel(y, ig, oq, oo, ou, od, ov, *rest):
    outs, bufs, sems = rest[:14], rest[14:20], rest[20]
    pairs = list(zip((y, ig, oq, oo, ou, od), bufs, (outs[0], outs[1], outs[2], outs[4], outs[8], outs[10])))
    pieces = []
    for n, (src, buf, dst) in enumerate(pairs):
        for h in range(2):
            at = (pl.ds(h, 1),) if n < 2 else (pl.ds(h * (src.shape[0] // 2), src.shape[0] // 2),)
            pieces.append((
                pltpu.make_async_copy(src.at[at], buf.at[at], sems.at[0, n, h]),
                pltpu.make_async_copy(buf.at[at], dst.at[at], sems.at[1, n, h]),
            ))
    for inward, _ in pieces:
        inward.start()
    for n, r in ((5, 0), (6, 1), (7, 2), (11, 3), (12, 4), (13, 5)):
        outs[n][...] = ov[r]
    outs[3][...] = ov[12, :64]
    for r in range(4):
        outs[9][r * 128:r * 128 + 128] = ov[8 + r]
    for inward, outward in pieces:
        inward.wait()
        outward.start()
    for _, outward in pieces:
        outward.wait()


def export(y, results):
    vm = pl.BlockSpec(memory_space=pltpu.VMEM)
    anywhere = pl.BlockSpec(memory_space=pl.ANY)
    shape = jax.ShapeDtypeStruct
    big = [shape(v.shape, v.dtype) for v in (y,) + tuple(results[:5])]
    vec = lambda n: shape((n,), F32)
    return pl.pallas_call(
        export_kernel,
        out_shape=[
            big[0], big[1], big[2], vec(64), big[3], vec(128), vec(128), vec(128), big[4], vec(512), big[5], vec(128),
            vec(128), vec(128),
        ],
        in_specs=[anywhere] * 6 + [vm],
        out_specs=[anywhere if i in (0, 1, 2, 4, 8, 10) else vm for i in range(14)],
        scratch_shapes=[pltpu.VMEM(b.shape, b.dtype) for b in big] + [pltpu.SemaphoreType.DMA((2, 6, 2))],
        compiler_params=pltpu.CompilerParams(vmem_limit_bytes=67000000),
    )(y, *results)


def backward(inputs, weights, saved, dv, gains):
    vm = pl.BlockSpec(memory_space=pltpu.VMEM)
    anywhere = pl.BlockSpec(memory_space=pl.ANY)
    shape = jax.ShapeDtypeStruct
    dma = pltpu.SemaphoreType.DMA
    v = pltpu.VMEM
    bufs, sems = fold_scratch()
    scratch = bufs + [
        v((1024, D), BF16), v((1024, D), F32), v((1024, D), BF16), v((2, HALF, D), BF16), v((2, D, HALF), BF16),
        v((2, 2, 1024, HALF), BF16), v((2, HALF, HALF), BF16), v((2, HALF, HALF), BF16),
        v((1024, D), BF16), v((1024, D), BF16), v((2, 1024, 384), BF16), v((8, 1024, HALF), BF16),
        v((2, 256, D), F32), v((2, 256, 128), F32), v((32, 16, 128), BF16), v((32, 16, 128), BF16), v((8, D), F32),
        v((8, 1, HALF), F32), v((8, 1, 384), F32), v((32, 1, 128), F32), v((32, 1, 128), F32),
    ] + sems + [
        dma((32,)), dma((32,)), dma((32,)), dma((32,)), dma((2, 4)), dma((2, 5)), dma((3,)), dma((2, 2)), dma((2, 8)), dma((2, 8)),
    ]
    return pl.pallas_call(
        backward_kernel,
        out_shape=[
            shape((2, L, D), F32), shape((128, 768), F32), shape((256, 128), F32), shape((128, 1024), F32),
            shape((1024, 128), F32), shape((16, 128), F32),
        ],
        in_specs=[anywhere] * 14 + [vm, vm],
        out_specs=[anywhere] + [vm] * 5,
        scratch_shapes=scratch,
        compiler_params=pltpu.CompilerParams(collective_id=1, has_side_effects=True, vmem_limit_bytes=67000000),
    )(inputs, *weights, *saved, dv, gains)

def fast_body(
    inputs, lengths, qkv_weight, qv_bias, out_weight, out_bias, norm1_gain, norm1_bias, up_weight, up_bias,
    down_weight, down_bias, norm2_gain, norm2_bias, cotangent,
):
    row = lambda v: v.reshape(1, 128)
    results = forward(
        lengths, inputs, cotangent, (qkv_weight, out_weight, up_weight, down_weight),
        (row(out_bias), row(norm1_gain), row(norm1_bias), row(down_bias), row(norm2_gain), row(norm2_bias),
         up_bias.reshape(4, 128), qv_bias.reshape(1, 64)),
    )
    return tuple(export(results[0], backward(inputs, results[1:5], results[5:14], results[14], results[15])))


def solution(mesh):
    placed = (
        P(None, ("fsdp", "mp"), None),
        P(None, "fsdp"),
        P("fsdp", "mp"),
        P(("mp", "fsdp")),
        P("mp", "fsdp"),
        P("fsdp"),
        P("fsdp"),
        P("fsdp"),
        P("fsdp", "mp"),
        P("fsdp"),
        P("mp", "fsdp"),
        P("fsdp"),
        P("fsdp"),
        P("fsdp"),
        P(None, ("fsdp", "mp"), None),
    )
    blocks_fit = mesh.shape["fsdp"] == 8 and mesh.shape["mp"] == 4
    return jax.shard_map(
        fast_body if blocks_fit else generic_body,
        mesh=mesh,
        in_specs=placed,
        out_specs=(
            P(None, ("fsdp", "mp"), None),
            P(None, ("fsdp", "mp"), None),
            P("fsdp", "mp"),
            P(("mp", "fsdp")),
            P("mp", "fsdp"),
            P("fsdp"),
            P("fsdp"),
            P("fsdp"),
            P("fsdp", "mp"),
            P("fsdp"),
            P("mp", "fsdp"),
            P("fsdp"),
            P("fsdp"),
            P("fsdp"),
        ),
        check_vma=False,
    )
```

```python
from functools import partial

import jax
import jax.numpy as jnp
from jax import lax
from jax.experimental import pallas as pl
from jax.experimental.pallas import tpu as pltpu
from jax.sharding import PartitionSpec as P

D = 1024
DH = 64
FF = 4096
L = 512
MBS = 2


EPSILON = 1e-06
CONTRACT_ROWS = (((0,), (0,)), ((), ()))
CONTRACT_COLS = (((1,), (1,)), ((), ()))


def normalize(values, scale_vec, shift_vec):
    row_mean = jnp.mean(values, axis=-1, keepdims=True)
    centered = values - row_mean
    spread = jnp.mean(centered * centered, axis=-1, keepdims=True)
    return centered * lax.rsqrt(spread + EPSILON) * scale_vec + shift_vec


def gelu_exact(values):
    return jax.nn.gelu(values, approximate=False)


def collect_forward(shards):
    return (
        lax.all_gather(shards[0], "fsdp", axis=0, tiled=True),
        lax.all_gather(shards[1], "fsdp", axis=0, tiled=True),
        lax.all_gather(shards[2], "fsdp", axis=1, tiled=True),
        lax.all_gather(shards[3], "fsdp", axis=0, tiled=True),
        lax.all_gather(shards[4], "fsdp", axis=0, tiled=True),
        lax.all_gather(shards[5], "fsdp", axis=0, tiled=True),
        lax.all_gather(shards[6], "fsdp", axis=0, tiled=True),
        lax.all_gather(shards[7], "fsdp", axis=0, tiled=True),
        lax.all_gather(shards[8], "fsdp", axis=1, tiled=True),
        lax.all_gather(shards[9], "fsdp", axis=0, tiled=True),
        lax.all_gather(shards[10], "fsdp", axis=0, tiled=True),
        lax.all_gather(shards[11], "fsdp", axis=0, tiled=True),
    )


def collect_backward(shards):
    return (
        lax.all_gather(shards[0], "fsdp", axis=0, tiled=True),
        lax.all_gather(shards[2], "fsdp", axis=1, tiled=True),
        lax.all_gather(shards[4], "fsdp", axis=0, tiled=True),
        lax.all_gather(shards[6], "fsdp", axis=0, tiled=True),
        lax.all_gather(shards[8], "fsdp", axis=1, tiled=True),
        lax.all_gather(shards[10], "fsdp", axis=0, tiled=True),
    )


def attend_forward(packed, scale_value):
    queries, keysets, values, seq_len = packed
    scores = (
        jnp.einsum("qhe,khe->hqk", queries, keysets, preferred_element_type=jnp.float32)
        * scale_value
    )
    live_mask = jnp.arange(scores.shape[-1])[None, None, :] < seq_len
    scores = jnp.where(live_mask, scores, -1000000000.0)
    row_max = jnp.max(scores, axis=-1, keepdims=True)
    exp_scores = jnp.exp(scores - row_max)
    denom_sum = jnp.sum(exp_scores, axis=-1, keepdims=True)
    attn_probs = (exp_scores / denom_sum).astype(jnp.bfloat16)
    mixed_heads = jnp.einsum("hqk,khe->qhe", attn_probs, values, preferred_element_type=jnp.float32)
    return (mixed_heads.astype(jnp.bfloat16), (row_max + jnp.log(denom_sum))[:, :, 0])


def attend_backward(packed, scale_value):
    queries, keysets, values, seq_len, log_sums, d_mixed = packed
    scores = (
        jnp.einsum("qhe,khe->hqk", queries, keysets, preferred_element_type=jnp.float32)
        * scale_value
    )
    live_mask = jnp.arange(scores.shape[-1])[None, None, :] < seq_len
    attn_probs = jnp.where(live_mask, jnp.exp(scores - log_sums[:, :, None]), 0.0)
    low_probs = attn_probs.astype(jnp.bfloat16)
    d_value = jnp.einsum("hqk,qhe->khe", low_probs, d_mixed, preferred_element_type=jnp.float32)
    d_probs = jnp.einsum("qhe,khe->hqk", d_mixed, values, preferred_element_type=jnp.float32)
    row_delta = jnp.sum(attn_probs * d_probs, axis=-1, keepdims=True)
    d_scores = (attn_probs * (d_probs - row_delta)).astype(jnp.bfloat16)
    d_query = (
        jnp.einsum("hqk,khe->qhe", d_scores, keysets, preferred_element_type=jnp.float32)
        * scale_value
    )
    d_key = (
        jnp.einsum("hqk,qhe->khe", d_scores, queries, preferred_element_type=jnp.float32)
        * scale_value
    )
    return jnp.stack([d_query, d_key, d_value], axis=2).astype(jnp.bfloat16)


def generic_body(
    inputs,
    lengths,
    qkv_weight,
    qv_bias,
    out_weight,
    out_bias,
    norm1_gain,
    norm1_bias,
    up_weight,
    up_bias,
    down_weight,
    down_bias,
    norm2_gain,
    norm2_bias,
    cotangent,
):
    shards = (
        qkv_weight,
        qv_bias,
        out_weight,
        out_bias,
        norm1_gain,
        norm1_bias,
        up_weight,
        up_bias,
        down_weight,
        down_bias,
        norm2_gain,
        norm2_bias,
    )
    row_count = inputs.shape[1]
    mp_count = lax.axis_size("mp")
    mp_index = lax.axis_index("mp")
    up_cols = up_weight.shape[1]
    scale_value = DH ** (-0.5)
    group_rows = row_count * mp_count
    head_count = qkv_weight.shape[1] // (3 * DH)
    row_ids = mp_index * row_count + jnp.arange(row_count)
    seq_count = group_rows // L
    head_width = head_count * DH
    seq_ids = row_ids // L
    positions = row_ids % L
    seq_match = seq_ids[:, None] == jnp.arange(seq_count)[None, :]
    grad_qkv = jnp.zeros((D, 3 * head_width), jnp.float32)
    grad_qvb = jnp.zeros((2 * head_width,), jnp.float32)
    grad_out = jnp.zeros((head_width, D), jnp.float32)
    grad_up = jnp.zeros((D, up_cols), jnp.float32)
    grad_down = jnp.zeros((up_cols, D), jnp.float32)
    grad_upb = jnp.zeros((FF,), jnp.float32)
    grad_outb = jnp.zeros((D,), jnp.float32)
    grad_gain1 = jnp.zeros((D,), jnp.float32)
    grad_shift1 = jnp.zeros((D,), jnp.float32)
    grad_downb = jnp.zeros((D,), jnp.float32)
    grad_gain2 = jnp.zeros((D,), jnp.float32)
    grad_shift2 = jnp.zeros((D,), jnp.float32)
    layer_rows = []
    input_rows = []
    for micro_idx in range(MBS):
        fwd_set = collect_forward(shards)
        qkv_full, qvb_full, out_full, outb_full = (fwd_set[0], fwd_set[1], fwd_set[2], fwd_set[3])
        gain_one = fwd_set[4].astype(jnp.float32)
        shift_one = fwd_set[5].astype(jnp.float32)
        up_full, upb_full, down_full = (fwd_set[6], fwd_set[7].astype(jnp.float32), fwd_set[8])
        downb_full = fwd_set[9].astype(jnp.float32)
        gain_two = fwd_set[10].astype(jnp.float32)
        shift_two = fwd_set[11].astype(jnp.float32)
        tokens = inputs[micro_idx]
        upb_used = lax.dynamic_slice_in_dim(upb_full, mp_index * up_cols, up_cols, 0)
        gathered = lax.all_gather(tokens, "mp", axis=0, tiled=True)
        seq_lens = lengths[micro_idx]
        pair_bias = qvb_full.astype(jnp.float32).reshape(head_count, 2, DH)
        bias_full = jnp.stack(
            [pair_bias[:, 0], jnp.zeros_like(pair_bias[:, 0]), pair_bias[:, 1]], axis=1
        )
        project = jnp.dot(
            gathered, qkv_full, preferred_element_type=jnp.float32
        ) + bias_full.reshape(3 * head_width)
        project = project.astype(jnp.bfloat16).reshape(seq_count, L, head_count, 3, DH)
        queries = project[:, :, :, 0]
        keysets = project[:, :, :, 1]
        values = project[:, :, :, 2]
        mixed_heads, log_sums = lax.map(
            partial(attend_forward, scale_value=scale_value), (queries, keysets, values, seq_lens)
        )
        mixed_flat = mixed_heads.reshape(group_rows, head_width)
        attn_own = lax.psum_scatter(
            jnp.dot(mixed_flat, out_full, preferred_element_type=jnp.float32).astype(jnp.bfloat16),
            "mp",
            scatter_dimension=0,
            tiled=True,
        ).astype(jnp.float32)
        pre_norm1 = attn_own + outb_full.astype(jnp.float32) + tokens.astype(jnp.float32)
        hidden = normalize(pre_norm1, gain_one, shift_one)
        low_hidden = hidden.astype(jnp.bfloat16)
        ffn_rows = lax.all_gather(low_hidden, "mp", axis=0, tiled=True)
        inner_sum = jnp.dot(ffn_rows, up_full, preferred_element_type=jnp.float32) + upb_used
        activated = gelu_exact(inner_sum).astype(jnp.bfloat16)
        branch = lax.psum_scatter(
            jnp.dot(activated, down_full, preferred_element_type=jnp.float32).astype(jnp.bfloat16),
            "mp",
            scatter_dimension=0,
            tiled=True,
        ).astype(jnp.float32)
        pre_norm2 = branch + downb_full + hidden
        layer_rows.append(normalize(pre_norm2, gain_two, shift_two).astype(jnp.bfloat16))
        bwd_set = collect_backward(shards)
        qkv_back, out_back = (bwd_set[0], bwd_set[1])
        gain_one_back = bwd_set[2].astype(jnp.float32)
        up_back, down_back = (bwd_set[3], bwd_set[4])
        gain_two_back = bwd_set[5].astype(jnp.float32)
        row_len = jnp.sum(jnp.where(seq_match, seq_lens[None, :], 0), axis=1)
        live_rows = (positions < row_len).astype(jnp.float32)
        grad_rows = cotangent[micro_idx].astype(jnp.float32) * live_rows[:, None]
        _, pull_two = jax.vjp(normalize, pre_norm2, gain_two_back, shift_two)
        d_pre2, d_gain2, d_shift2 = pull_two(grad_rows)
        grad_gain2 = grad_gain2 + d_gain2
        grad_shift2 = grad_shift2 + d_shift2
        grad_downb = grad_downb + jnp.sum(d_pre2, axis=0)
        d_branch = d_pre2.astype(jnp.bfloat16)
        d_rows = lax.all_gather(d_branch, "mp", axis=0, tiled=True)
        d_act = lax.dot_general(
            d_rows, down_back, CONTRACT_COLS, preferred_element_type=jnp.float32
        )
        grad_down = grad_down + lax.dot_general(
            activated, d_rows, CONTRACT_ROWS, preferred_element_type=jnp.float32
        )
        _, pull_gelu = jax.vjp(gelu_exact, inner_sum)
        d_inner = pull_gelu(d_act)[0].astype(jnp.bfloat16)
        bias_term = jnp.sum(d_inner.astype(jnp.float32), axis=0)
        grad_up = grad_up + lax.dot_general(
            ffn_rows, d_inner, CONTRACT_ROWS, preferred_element_type=jnp.float32
        )
        grad_upb = grad_upb + lax.dynamic_update_slice_in_dim(
            jnp.zeros((FF,), jnp.float32), bias_term, mp_index * up_cols, 0
        )
        d_hidden_part = lax.psum_scatter(
            lax.dot_general(
                d_inner, up_back, CONTRACT_COLS, preferred_element_type=jnp.float32
            ).astype(jnp.bfloat16),
            "mp",
            scatter_dimension=0,
            tiled=True,
        ).astype(jnp.float32)
        d_hidden = d_pre2 + d_hidden_part
        _, pull_one = jax.vjp(normalize, pre_norm1, gain_one_back, shift_one)
        d_pre1, d_gain1, d_shift1 = pull_one(d_hidden)
        grad_gain1 = grad_gain1 + d_gain1
        grad_shift1 = grad_shift1 + d_shift1
        grad_outb = grad_outb + jnp.sum(d_pre1, axis=0)
        d_attended = d_pre1.astype(jnp.bfloat16)
        d_attn_rows = lax.all_gather(d_attended, "mp", axis=0, tiled=True)
        d_mixed = lax.dot_general(
            d_attn_rows, out_back, CONTRACT_COLS, preferred_element_type=jnp.float32
        )
        d_mixed = d_mixed.astype(jnp.bfloat16)
        grad_out = grad_out + lax.dot_general(
            mixed_flat, d_attn_rows, CONTRACT_ROWS, preferred_element_type=jnp.float32
        )
        d_project = lax.map(
            partial(attend_backward, scale_value=scale_value),
            (
                queries,
                keysets,
                values,
                seq_lens,
                log_sums,
                d_mixed.reshape(seq_count, L, head_count, DH),
            ),
        )
        d_flat = d_project.reshape(group_rows, 3 * head_width)
        grad_qkv = grad_qkv + lax.dot_general(
            gathered, d_flat, CONTRACT_ROWS, preferred_element_type=jnp.float32
        )
        bias_parts = jnp.sum(d_flat.astype(jnp.float32), axis=0).reshape(head_count, 3, DH)
        grad_qvb = grad_qvb + jnp.stack([bias_parts[:, 0], bias_parts[:, 2]], axis=1).reshape(
            2 * head_width
        )
        input_rows.append(
            d_pre1
            + lax.psum_scatter(
                lax.dot_general(
                    d_flat, qkv_back, CONTRACT_COLS, preferred_element_type=jnp.float32
                ).astype(jnp.bfloat16),
                "mp",
                scatter_dimension=0,
                tiled=True,
            ).astype(jnp.float32)
        )
    summed = (
        lax.psum_scatter(
            grad_qkv.astype(jnp.bfloat16), "fsdp", scatter_dimension=0, tiled=True
        ).astype(jnp.float32),
        lax.psum_scatter(
            grad_qvb.astype(jnp.bfloat16), "fsdp", scatter_dimension=0, tiled=True
        ).astype(jnp.float32),
        lax.psum_scatter(
            grad_out.astype(jnp.bfloat16), "fsdp", scatter_dimension=1, tiled=True
        ).astype(jnp.float32),
        lax.psum_scatter(
            grad_outb.astype(jnp.bfloat16), "fsdp", scatter_dimension=0, tiled=True
        ).astype(jnp.float32),
        lax.psum_scatter(
            grad_gain1.astype(jnp.bfloat16), "fsdp", scatter_dimension=0, tiled=True
        ).astype(jnp.float32),
        lax.psum_scatter(
            grad_shift1.astype(jnp.bfloat16), "fsdp", scatter_dimension=0, tiled=True
        ).astype(jnp.float32),
        lax.psum_scatter(
            grad_up.astype(jnp.bfloat16), "fsdp", scatter_dimension=0, tiled=True
        ).astype(jnp.float32),
        lax.psum_scatter(
            grad_upb.astype(jnp.bfloat16), "fsdp", scatter_dimension=0, tiled=True
        ).astype(jnp.float32),
        lax.psum_scatter(
            grad_down.astype(jnp.bfloat16), "fsdp", scatter_dimension=1, tiled=True
        ).astype(jnp.float32),
        lax.psum_scatter(
            grad_downb.astype(jnp.bfloat16), "fsdp", scatter_dimension=0, tiled=True
        ).astype(jnp.float32),
        lax.psum_scatter(
            grad_gain2.astype(jnp.bfloat16), "fsdp", scatter_dimension=0, tiled=True
        ).astype(jnp.float32),
        lax.psum_scatter(
            grad_shift2.astype(jnp.bfloat16), "fsdp", scatter_dimension=0, tiled=True
        ).astype(jnp.float32),
    )
    vectors = lax.psum(
        (summed[3], summed[4], summed[5], summed[7], summed[9], summed[10], summed[11]), "mp"
    )
    return (
        jnp.stack(layer_rows),
        jnp.stack(input_rows),
        summed[0],
        summed[1],
        summed[2],
        vectors[0],
        vectors[1],
        vectors[2],
        summed[6],
        vectors[3],
        summed[8],
        vectors[4],
        vectors[5],
        vectors[6],
    )


MESH_ID = pl.DeviceIdType.MESH
F32 = jnp.float32
BF16 = jnp.bfloat16
PLANES = 4
SIDE = 128
HALF = 512
KINDS = ("rows", "cols", "rows", "cols")
FIRST = (1, 2)
SECOND = (2, 1)


def place():
    f = lax.axis_index("fsdp")
    return f // 2, f % 2, lax.axis_index("mp")


def span(ref, kind, start, size):
    start = pl.multiple_of(start, SIDE)
    if kind == "rows":
        return ref.at[pl.ds(start, size), :]
    return ref.at[:, pl.ds(start, size)]


def remote(src, dst, send, recv, f, m):
    return pltpu.make_async_remote_copy(
        src_ref=src, dst_ref=dst, send_sem=send, recv_sem=recv, device_id=(f, m), device_id_type=MESH_ID
    )


def greet_start():
    z, c, m = place()
    me = (z * 2 + c) * 4 + m
    barrier = pltpu.get_barrier_semaphore()

    def hello(d, carry):
        other = (me + d) % 32
        pl.semaphore_signal(barrier, inc=1, device_id=(other // 4, other % 4), device_id_type=MESH_ID)
        return carry

    lax.fori_loop(1, 32, hello, 0)


def greet_end():
    pl.semaphore_wait(pltpu.get_barrier_semaphore(), 31)


ROWS_A = 320
ROWS_B = 192


class Spread:
    def __init__(self, shards, wholes, sems):
        self.shards, self.wholes = shards, wholes
        self.zs, self.zr, self.xs, self.xr, self.ys, self.yr, self.cs, self.cr, self.own = sems
        self.z, self.c, self.m = place()
        self.f = self.z * 2 + self.c

    def window(self, t, k, m, start, size):
        start = pl.multiple_of(start, SIDE)
        if t == 3:
            return self.wholes[3].at[k, m, pl.ds(0, ROWS_A), pl.ds(start, size)]
        if t == 4:
            return self.wholes[3].at[k, m, pl.ds(ROWS_A, ROWS_B), pl.ds(start, size)]
        return span(self.wholes[t].at[k, m], KINDS[t], start, size)

    def block(self, t, k):
        return self.window(t, k, self.m, self.c * HALF + self.z * SIDE, SIDE)

    def z_copy(self, t, k, d):
        z = (self.z + d) % PLANES
        return remote(
            self.shards[t][k], self.block(t, k), self.zs.at[t, k, d - 1], self.zr.at[t, k, d - 1], z * 2 + self.c, self.m
        )

    def own_copy(self, t, k):
        return pltpu.make_async_copy(self.shards[t][k], self.block(t, k), self.own.at[t, k])

    def x_copy(self, t, k):
        blk = self.window(t, k, self.m, self.c * HALF, HALF)
        return remote(blk, blk, self.xs.at[t, k], self.xr.at[t, k], self.f, self.m ^ FIRST[k])

    def y_copy(self, t, k, i):
        blk = self.window(t, k, self.m ^ (FIRST[k] if i else 0), self.c * HALF, HALF)
        return remote(blk, blk, self.ys.at[t, k, i], self.yr.at[t, k, i], self.f, self.m ^ SECOND[k])

    def c_copy(self, t, k, off):
        blk = self.window(t, k, self.m ^ off, self.c * HALF, HALF)
        return remote(blk, blk, self.cs.at[t, k, off], self.cr.at[t, k, off], self.z * 2 + 1 - self.c, self.m)

    def start(self, t, k):
        for d in range(1, PLANES):
            self.z_copy(t, k, d).start()
        self.own_copy(t, k).start()

    def enter(self, t, k):
        self.own_copy(t, k).wait()
        for d in range(1, PLANES):
            self.z_copy(t, k, d).wait_recv()
        self.x_copy(t, k).start()
        self.c_copy(t, k, 0).start()

    def second(self, t, k):
        self.y_copy(t, k, 0).start()

    def relay(self, t, k):
        self.x_copy(t, k).wait_recv()
        self.y_copy(t, k, 1).start()
        self.c_copy(t, k, FIRST[k]).start()

    def cross(self, t, k, i):
        self.y_copy(t, k, i).wait_recv()
        self.c_copy(t, k, 3 if i else SECOND[k]).start()

    def late_x(self, k):
        blk = self.block(4, k)
        return remote(self.shards[4][k], blk, self.xs.at[4, k], self.xr.at[4, k], self.f, self.m ^ FIRST[k])

    def late_y(self, k, i):
        dst = self.window(4, k, self.m ^ (FIRST[k] if i else 0), self.c * HALF + self.z * SIDE, SIDE)
        src = dst if i else self.shards[4][k]
        return remote(src, dst, self.ys.at[4, k, i], self.yr.at[4, k, i], self.f, self.m ^ SECOND[k])

    def plane(self, k, start, size):
        return self.wholes[3].at[k, :, pl.ds(ROWS_A, ROWS_B), pl.ds(pl.multiple_of(start, SIDE), size)]

    def late_z(self, k, d):
        z = (self.z + d) % PLANES
        blk = self.plane(k, self.c * HALF + self.z * SIDE, SIDE)
        return remote(blk, blk, self.zs.at[4, k, d - 1], self.zr.at[4, k, d - 1], z * 2 + self.c, self.m)

    def late_c(self, k):
        blk = self.plane(k, self.c * HALF, HALF)
        return remote(blk, blk, self.cs.at[4, k, 0], self.cr.at[4, k, 0], self.z * 2 + 1 - self.c, self.m)

    def late_start(self):
        for k in range(2):
            self.late_x(k).start()
            self.late_y(k, 0).start()
            self.own_copy(4, k).start()

    def late_relay(self):
        for k in range(2):
            self.late_x(k).wait_recv()
            self.late_y(k, 1).start()

    def late_planes(self):
        for k in range(2):
            self.own_copy(4, k).wait()
            self.late_y(k, 0).wait_recv()
            self.late_y(k, 1).wait_recv()
            for d in range(1, PLANES):
                self.late_z(k, d).start()

    def late_cross(self):
        for k in range(2):
            for d in range(1, PLANES):
                self.late_z(k, d).wait_recv()
            self.late_c(k).start()

    def drain(self):
        for k in range(2):
            for t in range(4):
                for d in range(1, PLANES):
                    self.z_copy(t, k, d).wait_send()
                self.x_copy(t, k).wait_send()
                self.y_copy(t, k, 0).wait_send()
                self.y_copy(t, k, 1).wait_send()
                for off in range(4):
                    self.c_copy(t, k, off).wait_send()
            self.late_x(k).wait_send()
            self.late_y(k, 0).wait_send()
            self.late_y(k, 1).wait_send()
            for d in range(1, PLANES):
                self.late_z(k, d).wait_send()
            self.late_c(k).wait_send()


def spread_sems():
    dma = pltpu.SemaphoreType.DMA
    return [
        dma((5, 2, 3)), dma((5, 2, 3)), dma((5, 2)), dma((5, 2)), dma((5, 2, 2)), dma((5, 2, 2)),
        dma((5, 2, 4)), dma((5, 2, 4)), dma((5, 2)),
    ]


def swap_vectors(src, dst, send, recv, chunked):
    z, c, m = place()
    f = z * 2 + c
    me = f * 4 + m

    def copy(d):
        other = (me + d) % 32
        fo, mo = other // 4, other % 4
        piece = src.at[mo * 8 + fo] if chunked else src
        return remote(piece, dst.at[m * 8 + f], send.at[d], recv.at[d], fo, mo)

    return copy


def share_vectors(src, dst, send, recv):
    z, c, m = place()
    f = z * 2 + c

    def copy(d):
        return remote(src, dst.at[f], send.at[d], recv.at[d], (f + d) % 8, m)

    return copy


def run_31(fn):
    def step(d, carry):
        fn(d)
        return carry

    lax.fori_loop(1, 32, step, 0)


WHOLE = ((2, 4, 1024, 384), (2, 4, 128, 1024), (2, 4, 1024, 512), (2, 4, 512, 1024))


def add_into(dst, src, step=64):
    rows = dst.shape[0]
    step = min(step, rows)

    def body(i, carry):
        r = pl.ds(pl.multiple_of(i * step, step), step)
        dst[r, :] = (dst[r, :].astype(F32) + src[r, :].astype(F32)).astype(BF16)
        return carry

    lax.fori_loop(0, rows // step, body, 0)


def fold_shapes():
    halves, blocks = [], []
    for (_, _, r, c), kind in zip(WHOLE, KINDS):
        halves.append((HALF, c) if kind == "rows" else (r, HALF))
        blocks.append((SIDE, c) if kind == "rows" else (r, SIDE))
    return halves, blocks


def fold_scratch():
    dma = pltpu.SemaphoreType.DMA
    halves, blocks = fold_shapes()
    return (
        [pltpu.VMEM((2, 4) + h, BF16) for h in halves]
        + [pltpu.VMEM((2, 2) + h, BF16) for h in halves]
        + [pltpu.VMEM((2,) + h, BF16) for h in halves]
        + [pltpu.VMEM((2, 3) + b, BF16) for b in blocks],
        [dma((4, 2, 4)), dma((4, 2, 4)), dma((4, 2, 2)), dma((4, 2, 2)), dma((4, 2)), dma((4, 2)),
         dma((4, 2, 3)), dma((4, 2, 3))],
    )


LOG2E = 1.4426950408889634
ERFC_P = 0.4
ERFC = (
    0.11596272084822187, 0.08090171204448858, 0.23416118618048126, -0.18548266222668147, 0.3545906580628177,
    -0.10013362874972173,
)
NT = (((1,), (1,)), ((), ()))
TN = (((0,), (0,)), ((), ()))


def mm(a, b):
    return jnp.dot(a, b, preferred_element_type=F32)


def mm_nt(a, b):
    return lax.dot_general(a, b, NT, preferred_element_type=F32)


def mm_tn(a, b):
    return lax.dot_general(a, b, TN, preferred_element_type=F32)


def aligned(start, size):
    return pl.ds(pl.multiple_of(start, size), size)


def gelu_pair(u):
    e = jnp.exp2(u * u * (-0.5 * LOG2E))
    d = 1.0 + (ERFC_P * 0.7071067811865476) * jnp.abs(u)
    t = pl.reciprocal(d, approx=True)
    t = t * (2.0 - d * t)
    p = ERFC[-1]
    for coef in ERFC[-2::-1]:
        p = p * t + coef
    tail = p * t * e
    phi = jnp.where(u >= 0.0, 1.0 - tail, tail)
    return u * phi, phi + u * (e * 0.3989422804014327)


def column_copies(hbm, vmem, sems, store):
    copies = []
    for s in range(2):
        for p in range(8):
            f = (p % 4) * 2 + p // 4
            outside = hbm.at[s, :, pl.ds(f * SIDE, SIDE)]
            inside = vmem.at[pl.ds(s * L, L), pl.ds(p * SIDE, SIDE)]
            pair = (inside, outside) if store else (outside, inside)
            copies.append(pltpu.make_async_copy(pair[0], pair[1], sems.at[s, p]))
    return copies


def lane_half(value, e):
    lane = lax.broadcasted_iota(jnp.int32, (1, value.shape[1]), 1)
    return jnp.where((lane < 64) if e == 0 else (lane >= 64), value, jnp.zeros_like(value))


def row_mean(v):
    return jnp.sum(v, axis=1, keepdims=True) * (1.0 / D)


def turn_out(m, idx):
    k, p = idx % 2, idx // 2
    off = jnp.where(p == 0, 0, jnp.where(p == 1, 1 + k, jnp.where(p == 2, 2 - k, 3)))
    return k, off, m ^ off


def forward_kernel(
    lens, x_hbm, cot_hbm, sqr, sor, sur, sdr, ob, g1, b1, db, g2, b2, ub, qb,
    y_hbm, wq_hbm, wo_hbm, wu_hbm, wd_hbm, qkv_hbm, p_hbm, mixed_hbm, lowh_hbm, n1_hbm, rs_hbm, act_hbm, gp_hbm,
    dpre_hbm, vec_out, gain_out,
    wq, wo, wu, wd, vec, x, sqp, sv, qst, pst, mixed, hid, lowh, act, gst, cot, yst, nst, rst, dst, dv, ubs, qvb, ust, sq,
    vecq,
    *sems,
):
    (vs, vr, us, ur, xsem, csem, ysem, wsem, qsem, psem, msem, gsem, nsem, dsem, asem) = sems[9:]
    z, c, m = place()
    zero = jnp.zeros((1, 128), F32)

    def prepare():
        for e in range(6):
            pair, part = e // 3, e % 3
            halves = [
                sqr[:, (pair * 2 + h) * 192 + part * 64:(pair * 2 + h) * 192 + part * 64 + 64].astype(F32)
                for h in range(2)
            ]
            sqp[pair, :, part * 128:part * 128 + 128] = jnp.concatenate(halves, axis=1).astype(BF16)
        q1 = qb[...].astype(F32)
        sv[...] = jnp.concatenate(
            [r[...].astype(F32) for r in (ob, g1, b1, db, g2, b2)] + [zero, zero, ub[...].astype(F32)]
            + [zero, zero, zero, zero], axis=0
        ).astype(BF16)
        sq[...] = jnp.concatenate([q1, q1], axis=1)

    greet_start()
    prepare()
    greet_end()
    shards = (
        [sqp.at[k] for k in range(2)],
        [sor.at[pl.ds(k * 128, 128), :] for k in range(2)],
        [sur.at[:, pl.ds(k * HALF, HALF)] for k in range(2)],
        [sdr.at[pl.ds(k * HALF, ROWS_A), :] for k in range(2)],
        [sdr.at[pl.ds(k * HALF + ROWS_A, ROWS_B), :] for k in range(2)],
    )
    spread = Spread(shards, (wq, wo, wu, wd), sems[:9])
    spread.start(0, 0)
    spread.late_start()
    vcopy = share_vectors(sv, vec, us, ur)
    for d in range(1, 8):
        vcopy(d).start()
    qcopy = swap_vectors(sq, vecq, vs, vr, False)
    run_31(lambda d: qcopy(d).start())
    vec[z * 2 + c] = sv[...]
    vecq[m * 8 + z * 2 + c] = sq[...]
    x_copies = column_copies(x_hbm, x, xsem, False)
    c_copies = column_copies(cot_hbm, cot, csem, False)
    for cp in x_copies:
        cp.start()
    spread.late_relay()
    spread.enter(0, 0)
    spread.second(0, 0)
    spread.start(0, 1)
    spread.start(1, 0)
    for d in range(1, 8):
        vcopy(d).wait()
    run_31(lambda d: qcopy(d).wait())
    for p in range(8):
        dv[:, p * SIDE:(p + 1) * SIDE] = vec[(p % 4) * 2 + p // 4].astype(F32)[0:8]
    lane = lax.broadcasted_iota(jnp.int32, (1, 128), 1)
    for j in range(8):
        k, mo = j // 4, j % 4
        t = vec[mo * 2 + k].astype(F32)
        ubs[j] = jnp.concatenate([t[8:9], t[9:10], t[10:11], t[11:12]], axis=1)
        rows = [vecq[mo * 8 + 4 * k + i] for i in range(4)]
        qvb[j] = jnp.concatenate(
            [jnp.where(lane < 64, rows[0], rows[2]), zero, jnp.where(lane < 64, rows[1], rows[3])], axis=1
        )
    for cp in x_copies:
        cp.wait()
    for cp in c_copies:
        cp.start()

    def w_copy(t, idx):
        k, _, mo = turn_out(m, idx)
        src, dst = ((wq, wq_hbm), (wo, wo_hbm), (wu, wu_hbm), (wd, wd_hbm))[t]
        return pltpu.make_async_copy(src.at[k, mo], dst.at[k, mo], wsem.at[t, idx])

    def q_copy(it):
        k, _, mo = turn_out(m, it // 2)
        s = it % 2
        return pltpu.make_async_copy(qst.at[s], qkv_hbm.at[k * 4 + mo, aligned(s * L, L), :], qsem.at[s])

    def p_copy(it):
        k, _, mo = turn_out(m, it // 2)
        s = it % 2
        return pltpu.make_async_copy(pst.at[s], p_hbm.at[k * 4 + mo, s], psem.at[s])

    def attend(it, carry):
        idx, s = it // 2, it % 2
        k, off, mo = turn_out(m, idx)
        j = k * 4 + mo
        rows = aligned(s * L, L)

        @pl.when(it == 2)
        def _():
            spread.enter(0, 1)
            spread.second(0, 1)
            spread.start(1, 1)
            spread.start(2, 0)
            spread.relay(0, 0)
            spread.cross(0, 0, 0)

        @pl.when(it == 4)
        def _():
            spread.enter(1, 0)
            spread.second(1, 0)

        @pl.when(it == 6)
        def _():
            spread.enter(1, 1)
            spread.second(1, 1)
            spread.relay(0, 1)
            spread.cross(0, 1, 0)
            spread.start(2, 1)

        @pl.when(it == 8)
        def _():
            spread.cross(0, 0, 1)

        @pl.when(it == 10)
        def _():
            spread.cross(0, 1, 1)
            spread.enter(2, 0)
            spread.second(2, 0)
            spread.start(3, 0)
            spread.relay(1, 0)
            spread.relay(1, 1)

        @pl.when(it == 12)
        def _():
            spread.cross(1, 0, 0)
            spread.cross(1, 1, 0)

        @pl.when(it == 14)
        def _():
            spread.cross(1, 0, 1)
            spread.cross(1, 1, 1)
            spread.enter(2, 1)
            spread.second(2, 1)
            spread.start(3, 1)

        @pl.when(s == 0)
        def _():
            spread.c_copy(0, k, off).wait_recv()
            w_copy(0, idx).start()

        @pl.when(it >= 2)
        def _():
            q_copy(it - 2).wait()
            p_copy(it - 2).wait()

        qst[s] = (mm(x[rows, :], wq[k, mo]) + qvb[j]).astype(BF16)
        q_copy(it).start()
        keys, values = qst[s, :, 128:256], qst[s, :, 256:384]
        length = lens[s, m]
        bias = jnp.where(lax.broadcasted_iota(jnp.int32, (1, L), 1) < length, 0.0, -1e30)
        out = [None, None]
        for e in range(2):
            k_e, v_e = lane_half(keys, e), lane_half(values, e)
            for h in range(2):
                half = slice(h * 256, h * 256 + 256)
                scores = mm_nt(qst[s, half, 0:128], k_e) + bias
                top = jnp.max(scores, axis=1, keepdims=True)
                ex = jnp.exp2((scores - top) * (LOG2E * DH ** (-0.5)))
                probs = (ex * (1.0 / jnp.sum(ex, axis=1, keepdims=True))).astype(BF16)
                pst[s, e, half, :] = probs
                part = mm(probs, v_e)
                out[h] = part if out[h] is None else out[h] + part
        p_copy(it).start()
        mixed[rows, aligned(j * 128, 128)] = jnp.concatenate(out, axis=0).astype(BF16)
        return carry

    lax.fori_loop(0, 16, attend, 0)
    for it in (14, 15):
        q_copy(it).wait()
        p_copy(it).wait()
    m_copy = pltpu.make_async_copy(mixed, mixed_hbm, msem.at[0])
    m_copy.start()
    spread.late_planes()
    for k in range(2):
        for off in range(4):
            spread.c_copy(1, k, off).wait_recv()
    for idx in range(8):
        w_copy(1, idx).start()

    def n_copy(i):
        return pltpu.make_async_copy(nst.at[i % 2], n1_hbm.at[aligned(i * 256, 256), :], nsem.at[i % 2])

    def r_copy(i):
        return pltpu.make_async_copy(rst.at[i % 2], rs_hbm.at[aligned(i * 256, 256), :], nsem.at[2 + i % 2])

    def first_norm(i, carry):
        rows = aligned(i * 256, 256)

        @pl.when(i >= 2)
        def _():
            n_copy(i - 2).wait()
            r_copy(i - 2).wait()

        pre = mm(mixed[rows, :], wo[...].reshape(D, D)) + dv[0:1] + x[rows, :].astype(F32)
        cen = pre - row_mean(pre)
        inv = lax.rsqrt(row_mean(cen * cen) + EPSILON)
        n = cen * inv
        nst[i % 2] = n
        rst[i % 2] = jnp.broadcast_to(inv, (256, 128))
        n_copy(i).start()
        r_copy(i).start()
        h = n * dv[1:2] + dv[2:3]
        hid[rows, :] = h
        lowh[rows, :] = h.astype(BF16)
        return carry

    lax.fori_loop(0, 4, first_norm, 0)
    for i in (2, 3):
        n_copy(i).wait()
        r_copy(i).wait()
    h_copy = pltpu.make_async_copy(lowh, lowh_hbm, msem.at[1])
    h_copy.start()

    def g_copy(i):
        k, _, mo = turn_out(m, i)
        return pltpu.make_async_copy(gst.at[i % 2], gp_hbm.at[k * 4 + mo], gsem.at[i % 2])

    def a_copy(i):
        k, _, mo = turn_out(m, i)
        j = k * 4 + mo
        return pltpu.make_async_copy(act.at[:, aligned(j * HALF, HALF)], act_hbm.at[j], asem.at[i])

    def up(idx, carry):
        k, off, mo = turn_out(m, idx)
        j = k * 4 + mo
        cols = aligned(j * HALF, HALF)

        @pl.when(idx == 0)
        def _():
            spread.relay(2, 0)
            spread.cross(2, 0, 0)

        @pl.when(idx == 1)
        def _():
            spread.relay(2, 1)
            spread.cross(2, 1, 0)
            spread.enter(3, 0)
            spread.second(3, 0)

        @pl.when(idx == 3)
        def _():
            spread.enter(3, 1)
            spread.second(3, 1)

        @pl.when(idx == 6)
        def _():
            spread.cross(2, 0, 1)
            spread.cross(2, 1, 1)

        spread.c_copy(2, k, off).wait_recv()
        w_copy(2, idx).start()

        @pl.when(idx >= 2)
        def _():
            g_copy(idx - 2).wait()

        w = wu[k, mo]
        ust[0] = mm(lowh[0:256, :], w)
        for h in range(4):
            if h < 3:
                ust[(h + 1) % 2] = mm(lowh[h * 256 + 256:h * 256 + 512, :], w)
            bias = ubs[j]
            for r in range(0, 256, 16):
                sub = slice(h * 256 + r, h * 256 + r + 16)
                a, g = gelu_pair(ust[h % 2, r:r + 16, :] + bias)
                act[sub, cols] = a.astype(BF16)
                gst[idx % 2, sub, :] = g.astype(BF16)
        g_copy(idx).start()
        a_copy(idx).start()
        return carry

    lax.fori_loop(0, 8, up, 0)
    gain_out[...] = jnp.zeros((8, D), F32)
    vec_out[...] = dv[...]
    spread.relay(3, 0)
    spread.cross(3, 0, 0)
    spread.relay(3, 1)
    spread.cross(3, 1, 0)
    spread.late_cross()
    for k in range(2):
        spread.late_c(k).wait_recv()

    def down(idx, carry):
        k, off, mo = turn_out(m, idx)
        cols = aligned((k * 4 + mo) * HALF, HALF)

        @pl.when(idx == 4)
        def _():
            spread.cross(3, 0, 1)
            spread.cross(3, 1, 1)

        spread.c_copy(3, k, off).wait_recv()
        w_copy(3, idx).start()
        for r in range(2):
            for h in range(2):
                rows, side = slice(r * L, r * L + L), slice(h * HALF, h * HALF + HALF)
                hid[rows, side] += mm(act[rows, cols], wd[k, mo, :, side])
        return carry

    lax.fori_loop(0, 8, down, 0)

    def d_copy(i):
        return pltpu.make_async_copy(dst.at[i % 2], dpre_hbm.at[aligned(i * 256, 256), :], dsem.at[i % 2])

    def second_norm(i, carry):
        rows = aligned(i * 256, 256)

        @pl.when(i >= 2)
        def _():
            d_copy(i - 2).wait()

        pre = hid[rows, :] + dv[3:4]
        cen = pre - row_mean(pre)
        inv = lax.rsqrt(row_mean(cen * cen) + EPSILON)
        n = cen * inv
        yst[rows, :] = (n * dv[4:5] + dv[5:6]).astype(BF16)
        pos = (i % 2) * 256 + lax.broadcasted_iota(jnp.int32, (256, 1), 0)
        grad = jnp.where(pos < lens[i // 2, m], cot[rows, :].astype(F32), 0.0)
        g = grad * dv[4:5]
        back = inv * (g - row_mean(g) - n * row_mean(g * n))
        dst[i % 2] = back
        d_copy(i).start()
        gain_out[3:4, :] += jnp.sum(back, axis=0, keepdims=True)
        gain_out[4:5, :] += jnp.sum(grad * n, axis=0, keepdims=True)
        gain_out[5:6, :] += jnp.sum(grad, axis=0, keepdims=True)
        return carry

    for cp in c_copies:
        cp.wait()
    lax.fori_loop(0, 4, second_norm, 0)
    y_copies = column_copies(y_hbm, yst, ysem, True)
    for cp in y_copies:
        cp.start()
    for i in (2, 3):
        d_copy(i).wait()
    for i in (6, 7):
        g_copy(i).wait()

    def finish(i, carry):
        a_copy(i).wait()
        for t in range(4):
            w_copy(t, i).wait()
        return carry

    lax.fori_loop(0, 8, finish, 0)
    m_copy.wait()
    h_copy.wait()
    for cp in y_copies:
        cp.wait()
    spread.drain()


SAVED = (
    ((8, 1024, 384), BF16), ((8, 2, 2, L, L), BF16), ((1024, D), BF16), ((1024, D), BF16), ((1024, D), F32),
    ((1024, 128), F32), ((8, 1024, HALF), BF16), ((8, 1024, HALF), BF16), ((1024, D), F32),
)


def forward(lengths, inputs, cotangent, weights, vectors):
    vm = pl.BlockSpec(memory_space=pltpu.VMEM)
    anywhere = pl.BlockSpec(memory_space=pl.ANY)
    shape = jax.ShapeDtypeStruct
    dma = pltpu.SemaphoreType.DMA
    v = pltpu.VMEM
    scratch = [v(s, BF16) for s in WHOLE] + [
        v((8, 16, 128), BF16), v((1024, D), BF16), v((2, 128, 384), BF16), v((16, 128), BF16), v((2, L, 384), BF16),
        v((2, 2, L, L), BF16), v((1024, D), BF16), v((1024, D), F32), v((1024, D), BF16), v((1024, FF), BF16),
        v((2, 1024, HALF), BF16), v((1024, D), BF16), v((1024, D), BF16), v((2, 256, D), F32), v((2, 256, 128), F32),
        v((2, 256, D), F32), v((8, D), F32), v((8, 1, HALF), F32), v((8, 1, 384), F32), v((2, 256, HALF), F32), v((1, 128), F32),
        v((32, 1, 128), F32),
    ] + spread_sems() + [
        dma((32,)), dma((32,)), dma((8,)), dma((8,)), dma((2, 8)), dma((2, 8)), dma((2, 8)), dma((4, 8)), dma((2,)), dma((2,)), dma((2,)),
        dma((2,)), dma((4,)), dma((2,)), dma((8,)),
    ]
    return pl.pallas_call(
        forward_kernel,
        out_shape=[shape((2, L, D), BF16)] + [shape(s, BF16) for s in WHOLE] + [shape(s, d) for s, d in SAVED]
        + [shape((8, D), F32), shape((8, D), F32)],
        in_specs=[pl.BlockSpec(memory_space=pltpu.SMEM), anywhere, anywhere] + [vm] * 12,
        out_specs=[anywhere] * 14 + [vm, vm],
        scratch_shapes=scratch,
        compiler_params=pltpu.CompilerParams(collective_id=0, has_side_effects=True, vmem_limit_bytes=67000000),
    )(lengths, inputs, cotangent, *weights, *vectors)

EARLY = 192


class Fold:
    def __init__(self, rc, rx, ry, rz, rl, sems, late):
        self.rc, self.rx, self.ry, self.rz, self.rl = rc, rx, ry, rz, rl
        self.cs, self.cr, self.xs, self.xr, self.ys, self.yr, self.zs, self.zr = sems
        self.ls, self.lr, self.lxs, self.lxr, self.lys, self.lyr = late
        self.z, self.c, self.m = place()

    def cut(self, t, ref):
        return ref.at[pl.ds(0, HALF - EARLY), :] if t == 3 else ref

    def patch(self, ref, z=None):
        start = pl.multiple_of((self.z if z is None else z) * SIDE, SIDE)
        return ref.at[pl.ds(HALF - EARLY, EARLY), pl.ds(start, SIDE)]

    def early_z(self, k, off, d):
        z, mo = (self.z + d) % PLANES, self.m ^ off
        return remote(
            self.patch(self.rc[3].at[k, mo], z), self.rl.at[k, mo, d - 1], self.ls.at[k, off, d - 1],
            self.lr.at[k, off, d - 1], z * 2 + self.c, self.m,
        )

    def early_x(self, k, i):
        src = self.patch(self.rc[3].at[k, self.m ^ (3 if i else 1 + k)])
        return remote(
            src, self.patch(self.rx[3].at[k, i]), self.lxs.at[k, i], self.lxr.at[k, i], self.z * 2 + self.c,
            self.m ^ (1 + k),
        )

    def early_y(self, k):
        m = self.m ^ (2 - k)
        return remote(
            self.patch(self.rc[3].at[k, m]), self.patch(self.ry[3].at[k]), self.lys.at[k], self.lyr.at[k],
            self.z * 2 + self.c, m,
        )

    def early_sum(self, k):
        for i, off in enumerate((3, 1 + k, 2 - k, 0)):
            mo = self.m ^ off
            for d in range(1, PLANES):
                self.early_z(k, off, d).wait_recv()
            own = self.patch(self.rc[3].at[k, mo])
            for r in range(0, EARLY, 64):
                rows = slice(r, r + 64)
                total = own[rows, :].astype(F32) + self.rl[k, mo, 0, rows, :].astype(F32)
                total = total + self.rl[k, mo, 1, rows, :].astype(F32) + self.rl[k, mo, 2, rows, :].astype(F32)
                own[rows, :] = total.astype(BF16)
            if i < 2:
                self.early_x(k, 1 - i).start()

    def early_to_y(self, k):
        self.early_x(k, 1).wait_recv()
        add_into(self.patch(self.rc[3].at[k, self.m ^ (2 - k)]), self.patch(self.rx[3].at[k, 1]))
        self.early_y(k).start()

    def early_total(self, k):
        self.early_x(k, 0).wait_recv()
        self.early_y(k).wait_recv()
        refs = (self.rc[3].at[k, self.m], self.rx[3].at[k, 0], self.ry[3].at[k])
        a, b, c = (self.patch(r)[...].astype(F32) for r in refs)
        return a + b + c

    def early_drain(self, k):
        for off in range(4):
            for d in range(1, PLANES):
                self.early_z(k, off, d).wait_send()
        self.early_x(k, 0).wait_send()
        self.early_x(k, 1).wait_send()
        self.early_y(k).wait_send()

    def c_copy(self, t, k, off, src):
        return remote(
            src, self.rc[t].at[k, self.m ^ off], self.cs.at[t, k, off], self.cr.at[t, k, off],
            self.z * 2 + 1 - self.c, self.m,
        )

    def x_copy(self, t, k, i):
        m = self.m ^ (3 if i else 1 + k)
        return remote(
            self.cut(t, self.rc[t].at[k, m]), self.cut(t, self.rx[t].at[k, i]), self.xs.at[t, k, i], self.xr.at[t, k, i],
            self.z * 2 + self.c, self.m ^ (1 + k),
        )

    def y_copy(self, t, k):
        m = self.m ^ (2 - k)
        return remote(
            self.cut(t, self.rc[t].at[k, m]), self.cut(t, self.ry[t].at[k]), self.ys.at[t, k], self.yr.at[t, k], self.z * 2 + self.c, m
        )

    def z_copy(self, t, k, d):
        z = (self.z + d) % PLANES
        src = span(self.cut(t, self.rc[t].at[k, self.m]), KINDS[t], z * SIDE, SIDE)
        return remote(
            src, self.cut(t, self.rz[t].at[k, d - 1]), self.zs.at[t, k, d - 1], self.zr.at[t, k, d - 1], z * 2 + self.c, self.m
        )

    def to_y(self, t, k):
        self.x_copy(t, k, 1).wait_recv()
        add_into(self.cut(t, self.rc[t].at[k, self.m ^ (2 - k)]), self.cut(t, self.rx[t].at[k, 1]))
        self.y_copy(t, k).start()

    def to_z(self, t, k):
        self.x_copy(t, k, 0).wait_recv()
        add_into(self.cut(t, self.rc[t].at[k, self.m]), self.cut(t, self.rx[t].at[k, 0]))
        self.y_copy(t, k).wait_recv()
        add_into(self.cut(t, self.rc[t].at[k, self.m]), self.cut(t, self.ry[t].at[k]))
        for d in range(1, PLANES):
            self.z_copy(t, k, d).start()

    def total(self, t, k):
        for d in range(1, PLANES):
            self.z_copy(t, k, d).wait_recv()
        own = span(self.cut(t, self.rc[t].at[k, self.m]), KINDS[t], self.z * SIDE, SIDE)[...].astype(F32)
        a, b, c = (self.cut(t, self.rz[t].at[k, i])[...].astype(F32) for i in range(3))
        return own + a + b + c

    def drain(self, t, k):
        self.x_copy(t, k, 0).wait_send()
        self.x_copy(t, k, 1).wait_send()
        self.y_copy(t, k).wait_send()
        for d in range(1, PLANES):
            self.z_copy(t, k, d).wait_send()


def backward_kernel(
    x_hbm, wq_hbm, wo_hbm, wu_hbm, wd_hbm, qkv_hbm, p_hbm, mixed_hbm, lowh_hbm, n1_hbm, rs_hbm, act_hbm, gp_hbm,
    dpre_hbm, dv, gains,
    ig_hbm, oq, oo, ou, od, ov,
    *rest,
):
    rc, rx, ry, rz = rest[0:4], rest[4:8], rest[8:12], rest[12:16]
    (dbr, dh, low, wdj, wuj, ag, gd, gu, dmix, qkvj, dproj, nst, rst, rv, gv, sums, ubg, qvg, rw, gw) = rest[16:36]
    fold = Fold(rc, rx, ry, rz, rest[44], rest[36:44], rest[45:51])
    vs, vr, us, ur, lsem, psem, ssem, nsem, isem, xsem = rest[51:]
    z, c, m = place()
    other = 1 - c
    mine, theirs = aligned(c * HALF, HALF), aligned(other * HALF, HALF)

    def turn(idx):
        k, p = idx % 2, idx // 2
        off = jnp.where(p == 0, 3, jnp.where(p == 1, 1 + k, jnp.where(p == 2, 2 - k, 0)))
        return k, p, off

    def down_loads(idx):
        k, _, off = turn(idx)
        mo, slot = m ^ off, idx % 2
        j = k * 4 + mo
        pairs = ((wd_hbm.at[k, mo], wdj.at[slot]), (act_hbm.at[j], ag.at[slot, 0]), (gp_hbm.at[j], ag.at[slot, 1]))
        return [pltpu.make_async_copy(a, b, lsem.at[slot, i]) for i, (a, b) in enumerate(pairs)]

    def up_load(idx):
        k, _, off = turn(idx)
        return pltpu.make_async_copy(wu_hbm.at[k, m ^ off], wuj.at[idx % 2], lsem.at[idx % 2, 3])

    greet_start()
    dp_copy = pltpu.make_async_copy(dpre_hbm, dh, ssem.at[0])
    dp_copy.start()
    for cp in down_loads(0):
        cp.start()
    lh_copy = pltpu.make_async_copy(lowh_hbm, low, ssem.at[1])
    mx_copies = [
        pltpu.make_async_copy(mixed_hbm.at[:, pl.ds(h * L, L)], ag.at[1, h], ssem.at[2 + h]) for h in range(2)
    ]
    sums[...] = gains[...]
    dp_copy.wait()

    def cast(i, carry):
        rows = aligned(i * 128, 128)
        dbr[rows, :] = dh[rows, :].astype(BF16)
        return carry

    lax.fori_loop(0, 8, cast, 0)

    def settle_ffn(t, idx, own):
        k, p, off = turn(idx)
        mo = m ^ off
        fold.c_copy(t, k, off, gd.at[idx % 2]).wait()
        add_into(rc[t].at[k, mo], own.at[idx % 2])
        if t == 3:
            for d in range(1, PLANES):
                fold.early_z(k, off, d).start()

        @pl.when(p == 0)
        def _():
            fold.x_copy(t, k, 1).start()

        @pl.when(p == 1)
        def _():
            fold.x_copy(t, k, 0).start()

    def down_step(idx, carry):
        k, p, off = turn(idx)
        mo, slot = m ^ off, idx % 2
        for cp in down_loads(idx):
            cp.wait()

        @pl.when(idx < 7)
        def _():
            for cp in down_loads(idx + 1):
                cp.start()

        @pl.when(idx == 3)
        def _():
            lh_copy.start()
            up_load(0).start()
            up_load(1).start()

        total = jnp.zeros((1, HALF), F32)
        for r in range(2):
            rows = slice(r * L, r * L + L)
            d = (mm_nt(dbr[rows, :], wdj[slot]) * ag[slot, 1, rows, :].astype(F32)).astype(BF16)
            dproj[idx, rows, :] = d
            total = total + jnp.sum(d.astype(F32), axis=0, keepdims=True)
        ubg[k * 4 + mo] = total
        gd[slot] = mm_tn(ag[slot, 0], dbr[:, theirs]).astype(BF16)

        @pl.when(idx == 0)
        def _():
            greet_end()

        fold.c_copy(3, k, off, gd.at[slot]).start()
        gu[slot] = mm_tn(ag[slot, 0], dbr[:, mine]).astype(BF16)

        @pl.when(idx >= 1)
        def _():
            settle_ffn(3, idx - 1, gu)

        return carry

    lax.fori_loop(0, 8, down_step, 0)
    for cp in mx_copies:
        cp.start()
    lh_copy.wait()
    for k in range(2):
        fold.to_y(3, k)

    def up_step(idx, carry):
        k, p, off = turn(idx)
        slot = idx % 2
        gd[slot] = mm_tn(low[:, theirs], dproj[idx]).astype(BF16)
        fold.c_copy(2, k, off, gd.at[slot]).start()
        gu[slot] = mm_tn(low[:, mine], dproj[idx]).astype(BF16)
        up_load(idx).wait()
        for r in range(2):
            for h in range(2):
                rows, cols = slice(r * L, r * L + L), slice(h * HALF, h * HALF + HALF)
                dh[rows, cols] += mm_nt(dproj[idx, rows, :], wuj[slot, cols, :])

        @pl.when(idx < 6)
        def _():
            up_load(idx + 2).start()

        @pl.when(idx == 0)
        def _():
            settle_ffn(3, 7, gu)

        @pl.when(idx == 5)
        def _():
            fold.to_z(3, 1)

        @pl.when(idx == 6)
        def _():
            fold.to_z(3, 0)

        @pl.when(idx == 7)
        def _():
            fold.early_sum(0)
            fold.early_sum(1)

        @pl.when(idx >= 1)
        def _():
            settle_ffn(2, idx - 1, gu)

        return carry

    lax.fori_loop(0, 8, up_step, 0)
    fold.to_y(2, 0)
    fold.to_y(2, 1)

    def norm_loads(i):
        rows, slot = aligned(i * 256, 256), i % 2
        return (
            pltpu.make_async_copy(n1_hbm.at[rows, :], nst.at[slot], nsem.at[slot, 0]),
            pltpu.make_async_copy(rs_hbm.at[rows, :], rst.at[slot], nsem.at[slot, 1]),
        )

    for cp in norm_loads(0):
        cp.start()
    wo_copies = [
        pltpu.make_async_copy(
            wo_hbm.at[j // 4, j % 4], wdj.at[j // 4, pl.ds((j % 4) * 128, 128), :], lsem.at[j // 4, j % 4]
        )
        for j in range(8)
    ]
    for cp in wo_copies:
        cp.start()
    x_copies = column_copies(x_hbm, low, xsem, False)
    for cp in x_copies:
        cp.start()

    def attn_loads(idx):
        k, _, off = turn(idx)
        j, slot = k * 4 + (m ^ off), idx % 2
        copies = [pltpu.make_async_copy(qkv_hbm.at[j], qkvj.at[slot], psem.at[slot, 4])]
        for s in range(2):
            for e in range(2):
                copies.append(
                    pltpu.make_async_copy(
                        p_hbm.at[j, s, e], ag.at[slot, s, pl.ds(e * L, L), :], psem.at[slot, 2 * s + e]
                    )
                )
        return copies

    for cp in attn_loads(0):
        cp.start()

    def first_back(i, carry):
        rows, slot = aligned(i * 256, 256), i % 2

        @pl.when(i < 3)
        def _():
            for cp in norm_loads(i + 1):
                cp.start()

        for cp in norm_loads(i):
            cp.wait()
        grad, n = dh[rows, :], nst[slot]
        g = grad * dv[1:2]
        inv = rst[slot][:, 0:1]
        back = inv * (g - row_mean(g) - n * row_mean(g * n))
        dh[rows, :] = back
        dbr[rows, :] = back.astype(BF16)
        sums[0:1, :] += jnp.sum(back, axis=0, keepdims=True)
        sums[1:2, :] += jnp.sum(grad * n, axis=0, keepdims=True)
        sums[2:3, :] += jnp.sum(grad, axis=0, keepdims=True)
        return carry

    lax.fori_loop(0, 4, first_back, 0)
    settle_ffn(2, 7, gu)
    fold.early_to_y(0)
    fold.early_to_y(1)
    for cp in mx_copies:
        cp.wait()
    for h in range(2):
        rows = slice(h * L, h * L + L)
        wuj[0, rows, :] = mm_tn(ag[1, h], dbr[:, theirs]).astype(BF16)
    for k in range(2):
        for off in range(4):
            src = wuj.at[0, aligned((k * 4 + (m ^ off)) * 128, 128), :]
            fold.c_copy(1, k, off, src).start()
    for cp in wo_copies:
        cp.wait()
    for h in range(2):
        rows = slice(h * L, h * L + L)
        for q in range(2):
            dmix[rows, q * L:q * L + L] = mm_nt(dbr[rows, :], wdj[q]).astype(BF16)
    for h in range(2):
        rows = slice(h * L, h * L + L)
        wuj[1, rows, :] = mm_tn(ag[1, h], dbr[:, mine]).astype(BF16)
    for k in range(2):
        for off in (3, 1 + k, 2 - k, 0):
            src = wuj.at[0, aligned((k * 4 + (m ^ off)) * 128, 128), :]
            fold.c_copy(1, k, off, src).wait()
            add_into(rc[1].at[k, m ^ off], wuj.at[1, aligned((k * 4 + (m ^ off)) * 128, 128), :])
            if off == 3:
                fold.x_copy(1, k, 1).start()
            elif off == 1 + k:
                fold.x_copy(1, k, 0).start()
    for cp in x_copies:
        cp.wait()

    def piece(idx):
        return gu.at[idx % 2, :, pl.ds(0, 384)]

    def attend(idx, s):
        k, _, off = turn(idx)
        mo, slot = m ^ off, idx % 2
        j = k * 4 + mo
        rows = slice(s * L, s * L + L)
        dout = dmix[rows, aligned(j * 128, 128)]
        queries, keys, values = (qkvj[slot, rows, i * 128:i * 128 + 128] for i in range(3))
        dq = dk = dval = None
        for e in range(2):
            probs = ag[slot, s, e * L:e * L + L, :]
            p32 = probs.astype(F32)
            t = p32 * mm_nt(dout, lane_half(values, e))
            ds = (t - p32 * jnp.sum(t, axis=1, keepdims=True)).astype(BF16)
            parts = (mm(ds, lane_half(keys, e)), mm_tn(ds, lane_half(queries, e)), mm_tn(probs, lane_half(dout, e)))
            dq, dk, dval = parts if e == 0 else (dq + parts[0], dk + parts[1], dval + parts[2])
        scale = DH ** (-0.5)
        out = jnp.concatenate([dq * scale, dk * scale, dval], axis=1).astype(BF16)
        dproj[idx, rows, 0:384] = out
        return jnp.sum(out.astype(F32), axis=0, keepdims=True)

    def settle(idx):
        k, p, off = turn(idx)
        mo = m ^ off
        fold.c_copy(0, k, off, piece(idx)).wait()
        rc[0][k, mo] = (mm_tn(low[:, mine], dproj[idx, :, 0:384]) + rc[0][k, mo].astype(F32)).astype(BF16)

        @pl.when(p == 0)
        def _():
            fold.x_copy(0, k, 1).start()

        @pl.when(p == 1)
        def _():
            fold.x_copy(0, k, 0).start()

        @pl.when(p == 2)
        def _():
            fold.to_y(0, k)

        @pl.when(p == 3)
        def _():
            fold.to_z(0, k)

    def heads(idx, carry):
        k, p, off = turn(idx)
        j = k * 4 + (m ^ off)
        for cp in attn_loads(idx):
            cp.wait()

        @pl.when(idx < 7)
        def _():
            for cp in attn_loads(idx + 1):
                cp.start()

        qvg[j] = attend(idx, 0) + attend(idx, 1)

        @pl.when(idx >= 1)
        def _():
            settle(idx - 1)

        gu[idx % 2, :, 0:384] = mm_tn(low[:, theirs], dproj[idx, :, 0:384]).astype(BF16)
        fold.c_copy(0, k, off, piece(idx)).start()

        @pl.when(idx == 1)
        def _():
            fold.to_z(2, 1)
            fold.to_y(1, 0)
            fold.to_y(1, 1)

        @pl.when(idx == 2)
        def _():
            fold.to_z(2, 0)

        @pl.when(idx == 4)
        def _():
            fold.to_z(1, 0)
            fold.to_z(1, 1)

        return carry

    for f in range(8):
        p = (f % 2) * 4 + f // 2
        ub = ubg[p]
        pad = jnp.zeros((4, 128), F32)
        tile = jnp.concatenate(
            [sums[:, p * SIDE:(p + 1) * SIDE]] + [ub[:, i * 128:i * 128 + 128] for i in range(4)] + [pad], axis=0
        ).astype(BF16)
        for mo in range(4):
            gv[mo * 8 + f] = tile
    vcopy = swap_vectors(gv, rv, us, ur, True)
    run_31(lambda d: vcopy(d).start())
    me = m * 8 + z * 2 + c
    rv[me] = gv[me]
    lax.fori_loop(0, 8, heads, 0)

    def wq_load(idx):
        k, _, off = turn(idx)
        return pltpu.make_async_copy(wq_hbm.at[k, m ^ off], qkvj.at[idx % 2], psem.at[idx % 2, 4])

    wq_load(0).start()
    wq_load(1).start()
    settle(7)
    for f in range(8):
        for mo in range(4):
            kk, e, part = f // 4, (f // 2) % 2, f % 2
            qv = qvg[kk * 4 + mo][:, part * 256 + e * 64:part * 256 + e * 64 + 64]
            gw[mo * 8 + f] = jnp.concatenate([qv, qv], axis=1)
    wcopy = swap_vectors(gw, rw, vs, vr, True)
    run_31(lambda d: wcopy(d).start())
    rw[me] = gw[me]

    def pull(idx, carry):
        slot = idx % 2
        wq_load(idx).wait()
        for r in range(2):
            for h in range(2):
                rows, cols = slice(r * L, r * L + L), slice(h * HALF, h * HALF + HALF)
                dh[rows, cols] += mm_nt(dproj[idx, rows, 0:384], qkvj[slot, cols, :])

        @pl.when(idx < 6)
        def _():
            wq_load(idx + 2).start()

        return carry

    lax.fori_loop(0, 8, pull, 0)
    i_copies = column_copies(ig_hbm, dh, isem, True)
    for cp in i_copies:
        cp.start()
    run_31(lambda d: vcopy(d).wait())
    run_31(lambda d: wcopy(d).wait())

    def gather_sum(i, acc):
        return acc[0] + rv[i].astype(F32), acc[1] + rw[i]

    wide, narrow = lax.fori_loop(0, 32, gather_sum, (jnp.zeros((16, 128), F32), jnp.zeros((1, 128), F32)))
    ov[...] = wide
    ov[12:13, :] = narrow
    for k in range(2):
        od[k * HALF:k * HALF + HALF - EARLY, :] = fold.total(3, k)
        od[k * HALF + HALF - EARLY:k * HALF + HALF, :] = fold.early_total(k)
        ou[:, k * HALF:k * HALF + HALF] = fold.total(2, k)
        oo[k * 128:k * 128 + 128, :] = fold.total(1, k)
    for k in range(2):
        t = fold.total(0, k)
        parts = [t[:, i * 128 + e * 64:i * 128 + e * 64 + 64] for e in range(2) for i in range(3)]
        oq[:, k * 384:k * 384 + 384] = jnp.concatenate(parts, axis=1)
    for cp in i_copies:
        cp.wait()
    for k in range(2):
        for t in range(4):
            fold.drain(t, k)
        fold.early_drain(k)


def export_kernel(y, ig, oq, oo, ou, od, ov, *rest):
    outs, bufs, sems = rest[:14], rest[14:20], rest[20]
    pairs = list(zip((y, ig, oq, oo, ou, od), bufs, (outs[0], outs[1], outs[2], outs[4], outs[8], outs[10])))
    pieces = []
    for n, (src, buf, dst) in enumerate(pairs):
        for h in range(2):
            at = (pl.ds(h, 1),) if n < 2 else (pl.ds(h * (src.shape[0] // 2), src.shape[0] // 2),)
            pieces.append((
                pltpu.make_async_copy(src.at[at], buf.at[at], sems.at[0, n, h]),
                pltpu.make_async_copy(buf.at[at], dst.at[at], sems.at[1, n, h]),
            ))
    for inward, _ in pieces:
        inward.start()
    for n, r in ((5, 0), (6, 1), (7, 2), (11, 3), (12, 4), (13, 5)):
        outs[n][...] = ov[r]
    outs[3][...] = ov[12, :64]
    for r in range(4):
        outs[9][r * 128:r * 128 + 128] = ov[8 + r]
    for inward, outward in pieces:
        inward.wait()
        outward.start()
    for _, outward in pieces:
        outward.wait()


def export(y, results):
    vm = pl.BlockSpec(memory_space=pltpu.VMEM)
    anywhere = pl.BlockSpec(memory_space=pl.ANY)
    shape = jax.ShapeDtypeStruct
    big = [shape(v.shape, v.dtype) for v in (y,) + tuple(results[:5])]
    vec = lambda n: shape((n,), F32)
    return pl.pallas_call(
        export_kernel,
        out_shape=[
            big[0], big[1], big[2], vec(64), big[3], vec(128), vec(128), vec(128), big[4], vec(512), big[5], vec(128),
            vec(128), vec(128),
        ],
        in_specs=[anywhere] * 6 + [vm],
        out_specs=[anywhere if i in (0, 1, 2, 4, 8, 10) else vm for i in range(14)],
        scratch_shapes=[pltpu.VMEM(b.shape, b.dtype) for b in big] + [pltpu.SemaphoreType.DMA((2, 6, 2))],
        compiler_params=pltpu.CompilerParams(vmem_limit_bytes=67000000),
    )(y, *results)


def backward(inputs, weights, saved, dv, gains):
    vm = pl.BlockSpec(memory_space=pltpu.VMEM)
    anywhere = pl.BlockSpec(memory_space=pl.ANY)
    shape = jax.ShapeDtypeStruct
    dma = pltpu.SemaphoreType.DMA
    v = pltpu.VMEM
    bufs, sems = fold_scratch()
    scratch = bufs + [
        v((1024, D), BF16), v((1024, D), F32), v((1024, D), BF16), v((2, HALF, D), BF16), v((2, D, HALF), BF16),
        v((2, 2, 1024, HALF), BF16), v((2, HALF, HALF), BF16), v((2, HALF, HALF), BF16),
        v((1024, D), BF16), v((2, 1024, 384), BF16), v((8, 1024, HALF), BF16),
        v((2, 256, D), F32), v((2, 256, 128), F32), v((32, 16, 128), BF16), v((32, 16, 128), BF16), v((8, D), F32),
        v((8, 1, HALF), F32), v((8, 1, 384), F32), v((32, 1, 128), F32), v((32, 1, 128), F32),
    ] + sems + [
        v((2, 4, 3, EARLY, SIDE), BF16), dma((2, 4, 3)), dma((2, 4, 3)), dma((2, 2)), dma((2, 2)), dma((2,)), dma((2,)),
        dma((32,)), dma((32,)), dma((32,)), dma((32,)), dma((2, 4)), dma((2, 5)), dma((4,)), dma((2, 2)), dma((2, 8)), dma((2, 8)),
    ]
    return pl.pallas_call(
        backward_kernel,
        out_shape=[
            shape((2, L, D), F32), shape((128, 768), F32), shape((256, 128), F32), shape((128, 1024), F32),
            shape((1024, 128), F32), shape((16, 128), F32),
        ],
        in_specs=[anywhere] * 14 + [vm, vm],
        out_specs=[anywhere] + [vm] * 5,
        scratch_shapes=scratch,
        compiler_params=pltpu.CompilerParams(collective_id=1, has_side_effects=True, vmem_limit_bytes=67000000),
    )(inputs, *weights, *saved, dv, gains)

def fast_body(
    inputs, lengths, qkv_weight, qv_bias, out_weight, out_bias, norm1_gain, norm1_bias, up_weight, up_bias,
    down_weight, down_bias, norm2_gain, norm2_bias, cotangent,
):
    row = lambda v: v.reshape(1, 128)
    results = forward(
        lengths, inputs, cotangent, (qkv_weight, out_weight, up_weight, down_weight),
        (row(out_bias), row(norm1_gain), row(norm1_bias), row(down_bias), row(norm2_gain), row(norm2_bias),
         up_bias.reshape(4, 128), qv_bias.reshape(1, 64)),
    )
    return tuple(export(results[0], backward(inputs, results[1:5], results[5:14], results[14], results[15])))


def solution(mesh):
    placed = (
        P(None, ("fsdp", "mp"), None),
        P(None, "fsdp"),
        P("fsdp", "mp"),
        P(("mp", "fsdp")),
        P("mp", "fsdp"),
        P("fsdp"),
        P("fsdp"),
        P("fsdp"),
        P("fsdp", "mp"),
        P("fsdp"),
        P("mp", "fsdp"),
        P("fsdp"),
        P("fsdp"),
        P("fsdp"),
        P(None, ("fsdp", "mp"), None),
    )
    blocks_fit = mesh.shape["fsdp"] == 8 and mesh.shape["mp"] == 4
    return jax.shard_map(
        fast_body if blocks_fit else generic_body,
        mesh=mesh,
        in_specs=placed,
        out_specs=(
            P(None, ("fsdp", "mp"), None),
            P(None, ("fsdp", "mp"), None),
            P("fsdp", "mp"),
            P(("mp", "fsdp")),
            P("mp", "fsdp"),
            P("fsdp"),
            P("fsdp"),
            P("fsdp"),
            P("fsdp", "mp"),
            P("fsdp"),
            P("mp", "fsdp"),
            P("fsdp"),
            P("fsdp"),
            P("fsdp"),
        ),
        check_vma=False,
    )
```

```python
from functools import partial

import jax
import jax.numpy as jnp
from jax import lax
from jax.experimental import pallas as pl
from jax.experimental.pallas import tpu as pltpu
from jax.sharding import PartitionSpec as P

D = 1024
DH = 64
FF = 4096
L = 512
MBS = 2


EPSILON = 1e-06
CONTRACT_ROWS = (((0,), (0,)), ((), ()))
CONTRACT_COLS = (((1,), (1,)), ((), ()))


def normalize(values, scale_vec, shift_vec):
    row_mean = jnp.mean(values, axis=-1, keepdims=True)
    centered = values - row_mean
    spread = jnp.mean(centered * centered, axis=-1, keepdims=True)
    return centered * lax.rsqrt(spread + EPSILON) * scale_vec + shift_vec


def gelu_exact(values):
    return jax.nn.gelu(values, approximate=False)


def collect_forward(shards):
    return (
        lax.all_gather(shards[0], "fsdp", axis=0, tiled=True),
        lax.all_gather(shards[1], "fsdp", axis=0, tiled=True),
        lax.all_gather(shards[2], "fsdp", axis=1, tiled=True),
        lax.all_gather(shards[3], "fsdp", axis=0, tiled=True),
        lax.all_gather(shards[4], "fsdp", axis=0, tiled=True),
        lax.all_gather(shards[5], "fsdp", axis=0, tiled=True),
        lax.all_gather(shards[6], "fsdp", axis=0, tiled=True),
        lax.all_gather(shards[7], "fsdp", axis=0, tiled=True),
        lax.all_gather(shards[8], "fsdp", axis=1, tiled=True),
        lax.all_gather(shards[9], "fsdp", axis=0, tiled=True),
        lax.all_gather(shards[10], "fsdp", axis=0, tiled=True),
        lax.all_gather(shards[11], "fsdp", axis=0, tiled=True),
    )


def collect_backward(shards):
    return (
        lax.all_gather(shards[0], "fsdp", axis=0, tiled=True),
        lax.all_gather(shards[2], "fsdp", axis=1, tiled=True),
        lax.all_gather(shards[4], "fsdp", axis=0, tiled=True),
        lax.all_gather(shards[6], "fsdp", axis=0, tiled=True),
        lax.all_gather(shards[8], "fsdp", axis=1, tiled=True),
        lax.all_gather(shards[10], "fsdp", axis=0, tiled=True),
    )


def attend_forward(packed, scale_value):
    queries, keysets, values, seq_len = packed
    scores = (
        jnp.einsum("qhe,khe->hqk", queries, keysets, preferred_element_type=jnp.float32)
        * scale_value
    )
    live_mask = jnp.arange(scores.shape[-1])[None, None, :] < seq_len
    scores = jnp.where(live_mask, scores, -1000000000.0)
    row_max = jnp.max(scores, axis=-1, keepdims=True)
    exp_scores = jnp.exp(scores - row_max)
    denom_sum = jnp.sum(exp_scores, axis=-1, keepdims=True)
    attn_probs = (exp_scores / denom_sum).astype(jnp.bfloat16)
    mixed_heads = jnp.einsum("hqk,khe->qhe", attn_probs, values, preferred_element_type=jnp.float32)
    return (mixed_heads.astype(jnp.bfloat16), (row_max + jnp.log(denom_sum))[:, :, 0])


def attend_backward(packed, scale_value):
    queries, keysets, values, seq_len, log_sums, d_mixed = packed
    scores = (
        jnp.einsum("qhe,khe->hqk", queries, keysets, preferred_element_type=jnp.float32)
        * scale_value
    )
    live_mask = jnp.arange(scores.shape[-1])[None, None, :] < seq_len
    attn_probs = jnp.where(live_mask, jnp.exp(scores - log_sums[:, :, None]), 0.0)
    low_probs = attn_probs.astype(jnp.bfloat16)
    d_value = jnp.einsum("hqk,qhe->khe", low_probs, d_mixed, preferred_element_type=jnp.float32)
    d_probs = jnp.einsum("qhe,khe->hqk", d_mixed, values, preferred_element_type=jnp.float32)
    row_delta = jnp.sum(attn_probs * d_probs, axis=-1, keepdims=True)
    d_scores = (attn_probs * (d_probs - row_delta)).astype(jnp.bfloat16)
    d_query = (
        jnp.einsum("hqk,khe->qhe", d_scores, keysets, preferred_element_type=jnp.float32)
        * scale_value
    )
    d_key = (
        jnp.einsum("hqk,qhe->khe", d_scores, queries, preferred_element_type=jnp.float32)
        * scale_value
    )
    return jnp.stack([d_query, d_key, d_value], axis=2).astype(jnp.bfloat16)


def generic_body(
    inputs,
    lengths,
    qkv_weight,
    qv_bias,
    out_weight,
    out_bias,
    norm1_gain,
    norm1_bias,
    up_weight,
    up_bias,
    down_weight,
    down_bias,
    norm2_gain,
    norm2_bias,
    cotangent,
):
    shards = (
        qkv_weight,
        qv_bias,
        out_weight,
        out_bias,
        norm1_gain,
        norm1_bias,
        up_weight,
        up_bias,
        down_weight,
        down_bias,
        norm2_gain,
        norm2_bias,
    )
    row_count = inputs.shape[1]
    mp_count = lax.axis_size("mp")
    mp_index = lax.axis_index("mp")
    up_cols = up_weight.shape[1]
    scale_value = DH ** (-0.5)
    group_rows = row_count * mp_count
    head_count = qkv_weight.shape[1] // (3 * DH)
    row_ids = mp_index * row_count + jnp.arange(row_count)
    seq_count = group_rows // L
    head_width = head_count * DH
    seq_ids = row_ids // L
    positions = row_ids % L
    seq_match = seq_ids[:, None] == jnp.arange(seq_count)[None, :]
    grad_qkv = jnp.zeros((D, 3 * head_width), jnp.float32)
    grad_qvb = jnp.zeros((2 * head_width,), jnp.float32)
    grad_out = jnp.zeros((head_width, D), jnp.float32)
    grad_up = jnp.zeros((D, up_cols), jnp.float32)
    grad_down = jnp.zeros((up_cols, D), jnp.float32)
    grad_upb = jnp.zeros((FF,), jnp.float32)
    grad_outb = jnp.zeros((D,), jnp.float32)
    grad_gain1 = jnp.zeros((D,), jnp.float32)
    grad_shift1 = jnp.zeros((D,), jnp.float32)
    grad_downb = jnp.zeros((D,), jnp.float32)
    grad_gain2 = jnp.zeros((D,), jnp.float32)
    grad_shift2 = jnp.zeros((D,), jnp.float32)
    layer_rows = []
    input_rows = []
    for micro_idx in range(MBS):
        fwd_set = collect_forward(shards)
        qkv_full, qvb_full, out_full, outb_full = (fwd_set[0], fwd_set[1], fwd_set[2], fwd_set[3])
        gain_one = fwd_set[4].astype(jnp.float32)
        shift_one = fwd_set[5].astype(jnp.float32)
        up_full, upb_full, down_full = (fwd_set[6], fwd_set[7].astype(jnp.float32), fwd_set[8])
        downb_full = fwd_set[9].astype(jnp.float32)
        gain_two = fwd_set[10].astype(jnp.float32)
        shift_two = fwd_set[11].astype(jnp.float32)
        tokens = inputs[micro_idx]
        upb_used = lax.dynamic_slice_in_dim(upb_full, mp_index * up_cols, up_cols, 0)
        gathered = lax.all_gather(tokens, "mp", axis=0, tiled=True)
        seq_lens = lengths[micro_idx]
        pair_bias = qvb_full.astype(jnp.float32).reshape(head_count, 2, DH)
        bias_full = jnp.stack(
            [pair_bias[:, 0], jnp.zeros_like(pair_bias[:, 0]), pair_bias[:, 1]], axis=1
        )
        project = jnp.dot(
            gathered, qkv_full, preferred_element_type=jnp.float32
        ) + bias_full.reshape(3 * head_width)
        project = project.astype(jnp.bfloat16).reshape(seq_count, L, head_count, 3, DH)
        queries = project[:, :, :, 0]
        keysets = project[:, :, :, 1]
        values = project[:, :, :, 2]
        mixed_heads, log_sums = lax.map(
            partial(attend_forward, scale_value=scale_value), (queries, keysets, values, seq_lens)
        )
        mixed_flat = mixed_heads.reshape(group_rows, head_width)
        attn_own = lax.psum_scatter(
            jnp.dot(mixed_flat, out_full, preferred_element_type=jnp.float32).astype(jnp.bfloat16),
            "mp",
            scatter_dimension=0,
            tiled=True,
        ).astype(jnp.float32)
        pre_norm1 = attn_own + outb_full.astype(jnp.float32) + tokens.astype(jnp.float32)
        hidden = normalize(pre_norm1, gain_one, shift_one)
        low_hidden = hidden.astype(jnp.bfloat16)
        ffn_rows = lax.all_gather(low_hidden, "mp", axis=0, tiled=True)
        inner_sum = jnp.dot(ffn_rows, up_full, preferred_element_type=jnp.float32) + upb_used
        activated = gelu_exact(inner_sum).astype(jnp.bfloat16)
        branch = lax.psum_scatter(
            jnp.dot(activated, down_full, preferred_element_type=jnp.float32).astype(jnp.bfloat16),
            "mp",
            scatter_dimension=0,
            tiled=True,
        ).astype(jnp.float32)
        pre_norm2 = branch + downb_full + hidden
        layer_rows.append(normalize(pre_norm2, gain_two, shift_two).astype(jnp.bfloat16))
        bwd_set = collect_backward(shards)
        qkv_back, out_back = (bwd_set[0], bwd_set[1])
        gain_one_back = bwd_set[2].astype(jnp.float32)
        up_back, down_back = (bwd_set[3], bwd_set[4])
        gain_two_back = bwd_set[5].astype(jnp.float32)
        row_len = jnp.sum(jnp.where(seq_match, seq_lens[None, :], 0), axis=1)
        live_rows = (positions < row_len).astype(jnp.float32)
        grad_rows = cotangent[micro_idx].astype(jnp.float32) * live_rows[:, None]
        _, pull_two = jax.vjp(normalize, pre_norm2, gain_two_back, shift_two)
        d_pre2, d_gain2, d_shift2 = pull_two(grad_rows)
        grad_gain2 = grad_gain2 + d_gain2
        grad_shift2 = grad_shift2 + d_shift2
        grad_downb = grad_downb + jnp.sum(d_pre2, axis=0)
        d_branch = d_pre2.astype(jnp.bfloat16)
        d_rows = lax.all_gather(d_branch, "mp", axis=0, tiled=True)
        d_act = lax.dot_general(
            d_rows, down_back, CONTRACT_COLS, preferred_element_type=jnp.float32
        )
        grad_down = grad_down + lax.dot_general(
            activated, d_rows, CONTRACT_ROWS, preferred_element_type=jnp.float32
        )
        _, pull_gelu = jax.vjp(gelu_exact, inner_sum)
        d_inner = pull_gelu(d_act)[0].astype(jnp.bfloat16)
        bias_term = jnp.sum(d_inner.astype(jnp.float32), axis=0)
        grad_up = grad_up + lax.dot_general(
            ffn_rows, d_inner, CONTRACT_ROWS, preferred_element_type=jnp.float32
        )
        grad_upb = grad_upb + lax.dynamic_update_slice_in_dim(
            jnp.zeros((FF,), jnp.float32), bias_term, mp_index * up_cols, 0
        )
        d_hidden_part = lax.psum_scatter(
            lax.dot_general(
                d_inner, up_back, CONTRACT_COLS, preferred_element_type=jnp.float32
            ).astype(jnp.bfloat16),
            "mp",
            scatter_dimension=0,
            tiled=True,
        ).astype(jnp.float32)
        d_hidden = d_pre2 + d_hidden_part
        _, pull_one = jax.vjp(normalize, pre_norm1, gain_one_back, shift_one)
        d_pre1, d_gain1, d_shift1 = pull_one(d_hidden)
        grad_gain1 = grad_gain1 + d_gain1
        grad_shift1 = grad_shift1 + d_shift1
        grad_outb = grad_outb + jnp.sum(d_pre1, axis=0)
        d_attended = d_pre1.astype(jnp.bfloat16)
        d_attn_rows = lax.all_gather(d_attended, "mp", axis=0, tiled=True)
        d_mixed = lax.dot_general(
            d_attn_rows, out_back, CONTRACT_COLS, preferred_element_type=jnp.float32
        )
        d_mixed = d_mixed.astype(jnp.bfloat16)
        grad_out = grad_out + lax.dot_general(
            mixed_flat, d_attn_rows, CONTRACT_ROWS, preferred_element_type=jnp.float32
        )
        d_project = lax.map(
            partial(attend_backward, scale_value=scale_value),
            (
                queries,
                keysets,
                values,
                seq_lens,
                log_sums,
                d_mixed.reshape(seq_count, L, head_count, DH),
            ),
        )
        d_flat = d_project.reshape(group_rows, 3 * head_width)
        grad_qkv = grad_qkv + lax.dot_general(
            gathered, d_flat, CONTRACT_ROWS, preferred_element_type=jnp.float32
        )
        bias_parts = jnp.sum(d_flat.astype(jnp.float32), axis=0).reshape(head_count, 3, DH)
        grad_qvb = grad_qvb + jnp.stack([bias_parts[:, 0], bias_parts[:, 2]], axis=1).reshape(
            2 * head_width
        )
        input_rows.append(
            d_pre1
            + lax.psum_scatter(
                lax.dot_general(
                    d_flat, qkv_back, CONTRACT_COLS, preferred_element_type=jnp.float32
                ).astype(jnp.bfloat16),
                "mp",
                scatter_dimension=0,
                tiled=True,
            ).astype(jnp.float32)
        )
    summed = (
        lax.psum_scatter(
            grad_qkv.astype(jnp.bfloat16), "fsdp", scatter_dimension=0, tiled=True
        ).astype(jnp.float32),
        lax.psum_scatter(
            grad_qvb.astype(jnp.bfloat16), "fsdp", scatter_dimension=0, tiled=True
        ).astype(jnp.float32),
        lax.psum_scatter(
            grad_out.astype(jnp.bfloat16), "fsdp", scatter_dimension=1, tiled=True
        ).astype(jnp.float32),
        lax.psum_scatter(
            grad_outb.astype(jnp.bfloat16), "fsdp", scatter_dimension=0, tiled=True
        ).astype(jnp.float32),
        lax.psum_scatter(
            grad_gain1.astype(jnp.bfloat16), "fsdp", scatter_dimension=0, tiled=True
        ).astype(jnp.float32),
        lax.psum_scatter(
            grad_shift1.astype(jnp.bfloat16), "fsdp", scatter_dimension=0, tiled=True
        ).astype(jnp.float32),
        lax.psum_scatter(
            grad_up.astype(jnp.bfloat16), "fsdp", scatter_dimension=0, tiled=True
        ).astype(jnp.float32),
        lax.psum_scatter(
            grad_upb.astype(jnp.bfloat16), "fsdp", scatter_dimension=0, tiled=True
        ).astype(jnp.float32),
        lax.psum_scatter(
            grad_down.astype(jnp.bfloat16), "fsdp", scatter_dimension=1, tiled=True
        ).astype(jnp.float32),
        lax.psum_scatter(
            grad_downb.astype(jnp.bfloat16), "fsdp", scatter_dimension=0, tiled=True
        ).astype(jnp.float32),
        lax.psum_scatter(
            grad_gain2.astype(jnp.bfloat16), "fsdp", scatter_dimension=0, tiled=True
        ).astype(jnp.float32),
        lax.psum_scatter(
            grad_shift2.astype(jnp.bfloat16), "fsdp", scatter_dimension=0, tiled=True
        ).astype(jnp.float32),
    )
    vectors = lax.psum(
        (summed[3], summed[4], summed[5], summed[7], summed[9], summed[10], summed[11]), "mp"
    )
    return (
        jnp.stack(layer_rows),
        jnp.stack(input_rows),
        summed[0],
        summed[1],
        summed[2],
        vectors[0],
        vectors[1],
        vectors[2],
        summed[6],
        vectors[3],
        summed[8],
        vectors[4],
        vectors[5],
        vectors[6],
    )


MESH_ID = pl.DeviceIdType.MESH
F32 = jnp.float32
BF16 = jnp.bfloat16
PLANES = 4
SIDE = 128
HALF = 512
KINDS = ("rows", "cols", "rows", "cols")
FIRST = (1, 2)
SECOND = (2, 1)


def place():
    f = lax.axis_index("fsdp")
    return f // 2, f % 2, lax.axis_index("mp")


def span(ref, kind, start, size):
    start = pl.multiple_of(start, SIDE)
    if kind == "rows":
        return ref.at[pl.ds(start, size), :]
    return ref.at[:, pl.ds(start, size)]


def remote(src, dst, send, recv, f, m):
    return pltpu.make_async_remote_copy(
        src_ref=src, dst_ref=dst, send_sem=send, recv_sem=recv, device_id=(f, m), device_id_type=MESH_ID
    )


def greet_start():
    z, c, m = place()
    me = (z * 2 + c) * 4 + m
    barrier = pltpu.get_barrier_semaphore()

    def hello(d, carry):
        other = (me + d) % 32
        pl.semaphore_signal(barrier, inc=1, device_id=(other // 4, other % 4), device_id_type=MESH_ID)
        return carry

    lax.fori_loop(1, 32, hello, 0)


def greet_end():
    pl.semaphore_wait(pltpu.get_barrier_semaphore(), 31)


ROWS_A = 320
ROWS_B = 192


class Spread:
    def __init__(self, shards, wholes, sems):
        self.shards, self.wholes = shards, wholes
        self.zs, self.zr, self.xs, self.xr, self.ys, self.yr, self.cs, self.cr, self.own = sems
        self.z, self.c, self.m = place()
        self.f = self.z * 2 + self.c

    def window(self, t, k, m, start, size):
        start = pl.multiple_of(start, SIDE)
        if t == 3:
            return self.wholes[3].at[k, m, pl.ds(0, ROWS_A), pl.ds(start, size)]
        if t == 4:
            return self.wholes[3].at[k, m, pl.ds(ROWS_A, ROWS_B), pl.ds(start, size)]
        return span(self.wholes[t].at[k, m], KINDS[t], start, size)

    def block(self, t, k):
        return self.window(t, k, self.m, self.c * HALF + self.z * SIDE, SIDE)

    def z_copy(self, t, k, d):
        z = (self.z + d) % PLANES
        return remote(
            self.shards[t][k], self.block(t, k), self.zs.at[t, k, d - 1], self.zr.at[t, k, d - 1], z * 2 + self.c, self.m
        )

    def own_copy(self, t, k):
        return pltpu.make_async_copy(self.shards[t][k], self.block(t, k), self.own.at[t, k])

    def x_copy(self, t, k):
        blk = self.window(t, k, self.m, self.c * HALF, HALF)
        return remote(blk, blk, self.xs.at[t, k], self.xr.at[t, k], self.f, self.m ^ FIRST[k])

    def y_copy(self, t, k, i):
        blk = self.window(t, k, self.m ^ (FIRST[k] if i else 0), self.c * HALF, HALF)
        return remote(blk, blk, self.ys.at[t, k, i], self.yr.at[t, k, i], self.f, self.m ^ SECOND[k])

    def c_copy(self, t, k, off):
        blk = self.window(t, k, self.m ^ off, self.c * HALF, HALF)
        return remote(blk, blk, self.cs.at[t, k, off], self.cr.at[t, k, off], self.z * 2 + 1 - self.c, self.m)

    def start(self, t, k):
        for d in range(1, PLANES):
            self.z_copy(t, k, d).start()
        self.own_copy(t, k).start()

    def enter(self, t, k):
        self.own_copy(t, k).wait()
        for d in range(1, PLANES):
            self.z_copy(t, k, d).wait_recv()
        self.x_copy(t, k).start()
        self.c_copy(t, k, 0).start()

    def second(self, t, k):
        self.y_copy(t, k, 0).start()

    def relay(self, t, k):
        self.x_copy(t, k).wait_recv()
        self.y_copy(t, k, 1).start()
        self.c_copy(t, k, FIRST[k]).start()

    def cross(self, t, k, i):
        self.y_copy(t, k, i).wait_recv()
        self.c_copy(t, k, 3 if i else SECOND[k]).start()

    def late_x(self, k):
        blk = self.block(4, k)
        return remote(self.shards[4][k], blk, self.xs.at[4, k], self.xr.at[4, k], self.f, self.m ^ FIRST[k])

    def late_y(self, k, i):
        dst = self.window(4, k, self.m ^ (FIRST[k] if i else 0), self.c * HALF + self.z * SIDE, SIDE)
        src = dst if i else self.shards[4][k]
        return remote(src, dst, self.ys.at[4, k, i], self.yr.at[4, k, i], self.f, self.m ^ SECOND[k])

    def plane(self, k, start, size):
        return self.wholes[3].at[k, :, pl.ds(ROWS_A, ROWS_B), pl.ds(pl.multiple_of(start, SIDE), size)]

    def late_z(self, k, d):
        z = (self.z + d) % PLANES
        blk = self.plane(k, self.c * HALF + self.z * SIDE, SIDE)
        return remote(blk, blk, self.zs.at[4, k, d - 1], self.zr.at[4, k, d - 1], z * 2 + self.c, self.m)

    def late_c(self, k):
        blk = self.plane(k, self.c * HALF, HALF)
        return remote(blk, blk, self.cs.at[4, k, 0], self.cr.at[4, k, 0], self.z * 2 + 1 - self.c, self.m)

    def late_start(self):
        for k in range(2):
            self.late_x(k).start()
            self.late_y(k, 0).start()
            self.own_copy(4, k).start()

    def late_relay(self):
        for k in range(2):
            self.late_x(k).wait_recv()
            self.late_y(k, 1).start()

    def late_planes(self):
        for k in range(2):
            self.own_copy(4, k).wait()
            self.late_y(k, 0).wait_recv()
            self.late_y(k, 1).wait_recv()
            for d in range(1, PLANES):
                self.late_z(k, d).start()

    def late_cross(self):
        for k in range(2):
            for d in range(1, PLANES):
                self.late_z(k, d).wait_recv()
            self.late_c(k).start()

    def drain(self):
        for k in range(2):
            for t in range(4):
                for d in range(1, PLANES):
                    self.z_copy(t, k, d).wait_send()
                self.x_copy(t, k).wait_send()
                self.y_copy(t, k, 0).wait_send()
                self.y_copy(t, k, 1).wait_send()
                for off in range(4):
                    self.c_copy(t, k, off).wait_send()
            self.late_x(k).wait_send()
            self.late_y(k, 0).wait_send()
            self.late_y(k, 1).wait_send()
            for d in range(1, PLANES):
                self.late_z(k, d).wait_send()
            self.late_c(k).wait_send()


def spread_sems():
    dma = pltpu.SemaphoreType.DMA
    return [
        dma((5, 2, 3)), dma((5, 2, 3)), dma((5, 2)), dma((5, 2)), dma((5, 2, 2)), dma((5, 2, 2)),
        dma((5, 2, 4)), dma((5, 2, 4)), dma((5, 2)),
    ]


def swap_vectors(src, dst, send, recv, chunked):
    z, c, m = place()
    f = z * 2 + c
    me = f * 4 + m

    def copy(d):
        other = (me + d) % 32
        fo, mo = other // 4, other % 4
        piece = src.at[mo * 8 + fo] if chunked else src
        return remote(piece, dst.at[m * 8 + f], send.at[d], recv.at[d], fo, mo)

    return copy


def share_vectors(src, dst, send, recv):
    z, c, m = place()
    f = z * 2 + c

    def copy(d):
        return remote(src, dst.at[f], send.at[d], recv.at[d], (f + d) % 8, m)

    return copy


def run_31(fn):
    def step(d, carry):
        fn(d)
        return carry

    lax.fori_loop(1, 32, step, 0)


WHOLE = ((2, 4, 1024, 384), (2, 4, 128, 1024), (2, 4, 1024, 512), (2, 4, 512, 1024))


def add_into(dst, src, step=64):
    rows = dst.shape[0]
    step = min(step, rows)

    def body(i, carry):
        r = pl.ds(pl.multiple_of(i * step, step), step)
        dst[r, :] = (dst[r, :].astype(F32) + src[r, :].astype(F32)).astype(BF16)
        return carry

    lax.fori_loop(0, rows // step, body, 0)


def fold_shapes():
    halves, blocks = [], []
    for (_, _, r, c), kind in zip(WHOLE, KINDS):
        halves.append((HALF, c) if kind == "rows" else (r, HALF))
        blocks.append((SIDE, c) if kind == "rows" else (r, SIDE))
    return halves, blocks


def fold_scratch():
    dma = pltpu.SemaphoreType.DMA
    halves, blocks = fold_shapes()
    return (
        [pltpu.VMEM((2, 4) + h, BF16) for h in halves]
        + [pltpu.VMEM((2, 2) + h, BF16) for h in halves]
        + [pltpu.VMEM((2,) + h, BF16) for h in halves]
        + [pltpu.VMEM((2, 3) + b, BF16) for b in blocks],
        [dma((4, 2, 4)), dma((4, 2, 4)), dma((4, 2, 2)), dma((4, 2, 2)), dma((4, 2)), dma((4, 2)),
         dma((4, 2, 3)), dma((4, 2, 3))],
    )


LOG2E = 1.4426950408889634
ERFC_P = 0.4
ERFC = (
    0.11596272084822187, 0.08090171204448858, 0.23416118618048126, -0.18548266222668147, 0.3545906580628177,
    -0.10013362874972173,
)
NT = (((1,), (1,)), ((), ()))
TN = (((0,), (0,)), ((), ()))


def mm(a, b):
    return jnp.dot(a, b, preferred_element_type=F32)


def mm_nt(a, b):
    return lax.dot_general(a, b, NT, preferred_element_type=F32)


def mm_tn(a, b):
    return lax.dot_general(a, b, TN, preferred_element_type=F32)


def aligned(start, size):
    return pl.ds(pl.multiple_of(start, size), size)


def gelu_pair(u):
    e = jnp.exp2(u * u * (-0.5 * LOG2E))
    d = 1.0 + (ERFC_P * 0.7071067811865476) * jnp.abs(u)
    t = pl.reciprocal(d, approx=True)
    t = t * (2.0 - d * t)
    p = ERFC[-1]
    for coef in ERFC[-2::-1]:
        p = p * t + coef
    tail = p * t * e
    phi = jnp.where(u >= 0.0, 1.0 - tail, tail)
    return u * phi, phi + u * (e * 0.3989422804014327)


def column_copies(hbm, vmem, sems, store):
    copies = []
    for s in range(2):
        for p in range(8):
            f = (p % 4) * 2 + p // 4
            outside = hbm.at[s, :, pl.ds(f * SIDE, SIDE)]
            inside = vmem.at[pl.ds(s * L, L), pl.ds(p * SIDE, SIDE)]
            pair = (inside, outside) if store else (outside, inside)
            copies.append(pltpu.make_async_copy(pair[0], pair[1], sems.at[s, p]))
    return copies


def lane_half(value, e):
    lane = lax.broadcasted_iota(jnp.int32, (1, value.shape[1]), 1)
    return jnp.where((lane < 64) if e == 0 else (lane >= 64), value, jnp.zeros_like(value))


def row_mean(v):
    return jnp.sum(v, axis=1, keepdims=True) * (1.0 / D)


def turn_out(m, idx):
    k, p = idx % 2, idx // 2
    off = jnp.where(p == 0, 0, jnp.where(p == 1, 1 + k, jnp.where(p == 2, 2 - k, 3)))
    return k, off, m ^ off


def forward_kernel(
    lens, x_hbm, cot_hbm, sqr, sor, sur, sdr, ob, g1, b1, db, g2, b2, ub, qb,
    y_hbm, wq_hbm, wo_hbm, wu_hbm, wd_hbm, qkv_hbm, p_hbm, mixed_hbm, lowh_hbm, n1_hbm, rs_hbm, act_hbm, gp_hbm,
    dpre_hbm, vec_out, gain_out,
    wq, wo, wu, wd, vec, x, sqp, sv, qst, pst, mixed, hid, lowh, act, gst, cot, yst, nst, rst, dst, dv, ubs, qvb, ust, sq,
    vecq,
    *sems,
):
    (vs, vr, us, ur, xsem, csem, ysem, wsem, qsem, psem, msem, gsem, nsem, dsem, asem) = sems[9:]
    z, c, m = place()
    zero = jnp.zeros((1, 128), F32)

    def prepare():
        for e in range(6):
            pair, part = e // 3, e % 3
            halves = [
                sqr[:, (pair * 2 + h) * 192 + part * 64:(pair * 2 + h) * 192 + part * 64 + 64].astype(F32)
                for h in range(2)
            ]
            sqp[pair, :, part * 128:part * 128 + 128] = jnp.concatenate(halves, axis=1).astype(BF16)
        q1 = qb[...].astype(F32)
        sv[...] = jnp.concatenate(
            [r[...].astype(F32) for r in (ob, g1, b1, db, g2, b2)] + [zero, zero, ub[...].astype(F32)]
            + [zero, zero, zero, zero], axis=0
        ).astype(BF16)
        sq[...] = jnp.concatenate([q1, q1], axis=1)

    greet_start()
    prepare()
    greet_end()
    shards = (
        [sqp.at[k] for k in range(2)],
        [sor.at[pl.ds(k * 128, 128), :] for k in range(2)],
        [sur.at[:, pl.ds(k * HALF, HALF)] for k in range(2)],
        [sdr.at[pl.ds(k * HALF, ROWS_A), :] for k in range(2)],
        [sdr.at[pl.ds(k * HALF + ROWS_A, ROWS_B), :] for k in range(2)],
    )
    spread = Spread(shards, (wq, wo, wu, wd), sems[:9])
    spread.start(0, 0)
    spread.late_start()
    vcopy = share_vectors(sv, vec, us, ur)
    for d in range(1, 8):
        vcopy(d).start()
    qcopy = swap_vectors(sq, vecq, vs, vr, False)
    run_31(lambda d: qcopy(d).start())
    vec[z * 2 + c] = sv[...]
    vecq[m * 8 + z * 2 + c] = sq[...]
    x_copies = column_copies(x_hbm, x, xsem, False)
    c_copies = column_copies(cot_hbm, cot, csem, False)
    for cp in x_copies:
        cp.start()
    spread.late_relay()
    spread.enter(0, 0)
    spread.second(0, 0)
    spread.start(0, 1)
    spread.start(1, 0)
    for d in range(1, 8):
        vcopy(d).wait()
    run_31(lambda d: qcopy(d).wait())
    for p in range(8):
        dv[:, p * SIDE:(p + 1) * SIDE] = vec[(p % 4) * 2 + p // 4].astype(F32)[0:8]
    lane = lax.broadcasted_iota(jnp.int32, (1, 128), 1)
    for j in range(8):
        k, mo = j // 4, j % 4
        t = vec[mo * 2 + k].astype(F32)
        ubs[j] = jnp.concatenate([t[8:9], t[9:10], t[10:11], t[11:12]], axis=1)
        rows = [vecq[mo * 8 + 4 * k + i] for i in range(4)]
        qvb[j] = jnp.concatenate(
            [jnp.where(lane < 64, rows[0], rows[2]), zero, jnp.where(lane < 64, rows[1], rows[3])], axis=1
        )
    for cp in x_copies:
        cp.wait()
    for cp in c_copies:
        cp.start()

    def w_copy(t, idx):
        k, _, mo = turn_out(m, idx)
        src, dst = ((wq, wq_hbm), (wo, wo_hbm), (wu, wu_hbm), (wd, wd_hbm))[t]
        return pltpu.make_async_copy(src.at[k, mo], dst.at[k, mo], wsem.at[t, idx])

    def q_copy(it):
        k, _, mo = turn_out(m, it // 2)
        s = it % 2
        return pltpu.make_async_copy(qst.at[s], qkv_hbm.at[k * 4 + mo, aligned(s * L, L), :], qsem.at[s])

    def p_copy(it):
        k, _, mo = turn_out(m, it // 2)
        s = it % 2
        return pltpu.make_async_copy(pst.at[s], p_hbm.at[k * 4 + mo, s], psem.at[s])

    def attend(it, carry):
        idx, s = it // 2, it % 2
        k, off, mo = turn_out(m, idx)
        j = k * 4 + mo
        rows = aligned(s * L, L)

        @pl.when(it == 2)
        def _():
            spread.enter(0, 1)
            spread.second(0, 1)
            spread.start(1, 1)
            spread.start(2, 0)
            spread.relay(0, 0)
            spread.cross(0, 0, 0)

        @pl.when(it == 4)
        def _():
            spread.enter(1, 0)
            spread.second(1, 0)

        @pl.when(it == 6)
        def _():
            spread.enter(1, 1)
            spread.second(1, 1)
            spread.relay(0, 1)
            spread.cross(0, 1, 0)
            spread.start(2, 1)

        @pl.when(it == 8)
        def _():
            spread.cross(0, 0, 1)

        @pl.when(it == 10)
        def _():
            spread.cross(0, 1, 1)
            spread.enter(2, 0)
            spread.second(2, 0)
            spread.start(3, 0)
            spread.relay(1, 0)
            spread.relay(1, 1)

        @pl.when(it == 12)
        def _():
            spread.cross(1, 0, 0)
            spread.cross(1, 1, 0)

        @pl.when(it == 14)
        def _():
            spread.cross(1, 0, 1)
            spread.cross(1, 1, 1)
            spread.enter(2, 1)
            spread.second(2, 1)
            spread.start(3, 1)

        @pl.when(s == 0)
        def _():
            spread.c_copy(0, k, off).wait_recv()
            w_copy(0, idx).start()

        @pl.when(it >= 2)
        def _():
            q_copy(it - 2).wait()
            p_copy(it - 2).wait()

        qst[s] = (mm(x[rows, :], wq[k, mo]) + qvb[j]).astype(BF16)
        q_copy(it).start()
        keys, values = qst[s, :, 128:256], qst[s, :, 256:384]
        length = lens[s, m]
        bias = jnp.where(lax.broadcasted_iota(jnp.int32, (1, L), 1) < length, 0.0, -1e30)
        out = [None, None]
        for e in range(2):
            k_e, v_e = lane_half(keys, e), lane_half(values, e)
            for h in range(2):
                half = slice(h * 256, h * 256 + 256)
                scores = mm_nt(qst[s, half, 0:128], k_e) + bias
                top = jnp.max(scores, axis=1, keepdims=True)
                ex = jnp.exp2((scores - top) * (LOG2E * DH ** (-0.5)))
                probs = (ex * (1.0 / jnp.sum(ex, axis=1, keepdims=True))).astype(BF16)
                pst[s, e, half, :] = probs
                part = mm(probs, v_e)
                out[h] = part if out[h] is None else out[h] + part
        p_copy(it).start()
        mixed[rows, aligned(j * 128, 128)] = jnp.concatenate(out, axis=0).astype(BF16)
        return carry

    lax.fori_loop(0, 16, attend, 0)
    for it in (14, 15):
        q_copy(it).wait()
        p_copy(it).wait()
    m_copy = pltpu.make_async_copy(mixed, mixed_hbm, msem.at[0])
    m_copy.start()
    spread.late_planes()
    for k in range(2):
        for off in range(4):
            spread.c_copy(1, k, off).wait_recv()
    for idx in range(8):
        w_copy(1, idx).start()

    def n_copy(i):
        return pltpu.make_async_copy(nst.at[i % 2], n1_hbm.at[aligned(i * 256, 256), :], nsem.at[i % 2])

    def r_copy(i):
        return pltpu.make_async_copy(rst.at[i % 2], rs_hbm.at[aligned(i * 256, 256), :], nsem.at[2 + i % 2])

    def first_norm(i, carry):
        rows = aligned(i * 256, 256)

        @pl.when(i >= 2)
        def _():
            n_copy(i - 2).wait()
            r_copy(i - 2).wait()

        pre = mm(mixed[rows, :], wo[...].reshape(D, D)) + dv[0:1] + x[rows, :].astype(F32)
        cen = pre - row_mean(pre)
        inv = lax.rsqrt(row_mean(cen * cen) + EPSILON)
        n = cen * inv
        nst[i % 2] = n
        rst[i % 2] = jnp.broadcast_to(inv, (256, 128))
        n_copy(i).start()
        r_copy(i).start()
        h = n * dv[1:2] + dv[2:3]
        hid[rows, :] = h
        lowh[rows, :] = h.astype(BF16)
        return carry

    lax.fori_loop(0, 4, first_norm, 0)
    for i in (2, 3):
        n_copy(i).wait()
        r_copy(i).wait()
    h_copy = pltpu.make_async_copy(lowh, lowh_hbm, msem.at[1])
    h_copy.start()

    def g_copy(i):
        k, _, mo = turn_out(m, i)
        return pltpu.make_async_copy(gst.at[i % 2], gp_hbm.at[k * 4 + mo], gsem.at[i % 2])

    def a_copy(i):
        k, _, mo = turn_out(m, i)
        j = k * 4 + mo
        return pltpu.make_async_copy(act.at[:, aligned(j * HALF, HALF)], act_hbm.at[j], asem.at[i])

    def up(idx, carry):
        k, off, mo = turn_out(m, idx)
        j = k * 4 + mo
        cols = aligned(j * HALF, HALF)

        @pl.when(idx == 0)
        def _():
            spread.relay(2, 0)
            spread.cross(2, 0, 0)

        @pl.when(idx == 1)
        def _():
            spread.relay(2, 1)
            spread.cross(2, 1, 0)
            spread.enter(3, 0)
            spread.second(3, 0)

        @pl.when(idx == 3)
        def _():
            spread.enter(3, 1)
            spread.second(3, 1)

        @pl.when(idx == 6)
        def _():
            spread.cross(2, 0, 1)
            spread.cross(2, 1, 1)

        spread.c_copy(2, k, off).wait_recv()
        w_copy(2, idx).start()

        @pl.when(idx >= 2)
        def _():
            g_copy(idx - 2).wait()

        w = wu[k, mo]
        ust[0] = mm(lowh[0:256, :], w)
        for h in range(4):
            if h < 3:
                ust[(h + 1) % 2] = mm(lowh[h * 256 + 256:h * 256 + 512, :], w)
            bias = ubs[j]
            for r in range(0, 256, 16):
                sub = slice(h * 256 + r, h * 256 + r + 16)
                a, g = gelu_pair(ust[h % 2, r:r + 16, :] + bias)
                act[sub, cols] = a.astype(BF16)
                gst[idx % 2, sub, :] = g.astype(BF16)
        g_copy(idx).start()
        a_copy(idx).start()
        return carry

    lax.fori_loop(0, 8, up, 0)
    gain_out[...] = jnp.zeros((8, D), F32)
    vec_out[...] = dv[...]
    spread.relay(3, 0)
    spread.cross(3, 0, 0)
    spread.relay(3, 1)
    spread.cross(3, 1, 0)
    spread.late_cross()
    for k in range(2):
        spread.late_c(k).wait_recv()

    def down(idx, carry):
        k, off, mo = turn_out(m, idx)
        cols = aligned((k * 4 + mo) * HALF, HALF)

        @pl.when(idx == 4)
        def _():
            spread.cross(3, 0, 1)
            spread.cross(3, 1, 1)

        spread.c_copy(3, k, off).wait_recv()
        w_copy(3, idx).start()
        for r in range(2):
            for h in range(2):
                rows, side = slice(r * L, r * L + L), slice(h * HALF, h * HALF + HALF)
                hid[rows, side] += mm(act[rows, cols], wd[k, mo, :, side])
        return carry

    lax.fori_loop(0, 8, down, 0)

    def d_copy(i):
        return pltpu.make_async_copy(dst.at[i % 2], dpre_hbm.at[aligned(i * 256, 256), :], dsem.at[i % 2])

    def second_norm(i, carry):
        rows = aligned(i * 256, 256)

        @pl.when(i >= 2)
        def _():
            d_copy(i - 2).wait()

        pre = hid[rows, :] + dv[3:4]
        cen = pre - row_mean(pre)
        inv = lax.rsqrt(row_mean(cen * cen) + EPSILON)
        n = cen * inv
        yst[rows, :] = (n * dv[4:5] + dv[5:6]).astype(BF16)
        pos = (i % 2) * 256 + lax.broadcasted_iota(jnp.int32, (256, 1), 0)
        grad = jnp.where(pos < lens[i // 2, m], cot[rows, :].astype(F32), 0.0)
        g = grad * dv[4:5]
        back = inv * (g - row_mean(g) - n * row_mean(g * n))
        dst[i % 2] = back
        d_copy(i).start()
        gain_out[3:4, :] += jnp.sum(back, axis=0, keepdims=True)
        gain_out[4:5, :] += jnp.sum(grad * n, axis=0, keepdims=True)
        gain_out[5:6, :] += jnp.sum(grad, axis=0, keepdims=True)
        return carry

    for cp in c_copies:
        cp.wait()
    lax.fori_loop(0, 4, second_norm, 0)
    y_copies = column_copies(y_hbm, yst, ysem, True)
    for cp in y_copies:
        cp.start()
    for i in (2, 3):
        d_copy(i).wait()
    for i in (6, 7):
        g_copy(i).wait()

    def finish(i, carry):
        a_copy(i).wait()
        for t in range(4):
            w_copy(t, i).wait()
        return carry

    lax.fori_loop(0, 8, finish, 0)
    m_copy.wait()
    h_copy.wait()
    for cp in y_copies:
        cp.wait()
    spread.drain()


SAVED = (
    ((8, 1024, 384), BF16), ((8, 2, 2, L, L), BF16), ((1024, D), BF16), ((1024, D), BF16), ((1024, D), F32),
    ((1024, 128), F32), ((8, 1024, HALF), BF16), ((8, 1024, HALF), BF16), ((1024, D), F32),
)


def forward(lengths, inputs, cotangent, weights, vectors):
    vm = pl.BlockSpec(memory_space=pltpu.VMEM)
    anywhere = pl.BlockSpec(memory_space=pl.ANY)
    shape = jax.ShapeDtypeStruct
    dma = pltpu.SemaphoreType.DMA
    v = pltpu.VMEM
    scratch = [v(s, BF16) for s in WHOLE] + [
        v((8, 16, 128), BF16), v((1024, D), BF16), v((2, 128, 384), BF16), v((16, 128), BF16), v((2, L, 384), BF16),
        v((2, 2, L, L), BF16), v((1024, D), BF16), v((1024, D), F32), v((1024, D), BF16), v((1024, FF), BF16),
        v((2, 1024, HALF), BF16), v((1024, D), BF16), v((1024, D), BF16), v((2, 256, D), F32), v((2, 256, 128), F32),
        v((2, 256, D), F32), v((8, D), F32), v((8, 1, HALF), F32), v((8, 1, 384), F32), v((2, 256, HALF), F32), v((1, 128), F32),
        v((32, 1, 128), F32),
    ] + spread_sems() + [
        dma((32,)), dma((32,)), dma((8,)), dma((8,)), dma((2, 8)), dma((2, 8)), dma((2, 8)), dma((4, 8)), dma((2,)), dma((2,)), dma((2,)),
        dma((2,)), dma((4,)), dma((2,)), dma((8,)),
    ]
    return pl.pallas_call(
        forward_kernel,
        out_shape=[shape((2, L, D), BF16)] + [shape(s, BF16) for s in WHOLE] + [shape(s, d) for s, d in SAVED]
        + [shape((8, D), F32), shape((8, D), F32)],
        in_specs=[pl.BlockSpec(memory_space=pltpu.SMEM), anywhere, anywhere] + [vm] * 12,
        out_specs=[anywhere] * 14 + [vm, vm],
        scratch_shapes=scratch,
        compiler_params=pltpu.CompilerParams(collective_id=0, has_side_effects=True, vmem_limit_bytes=67000000),
    )(lengths, inputs, cotangent, *weights, *vectors)

EARLY = 192


class Fold:
    def __init__(self, rc, rx, ry, rz, rl, sems, late):
        self.rc, self.rx, self.ry, self.rz, self.rl = rc, rx, ry, rz, rl
        self.cs, self.cr, self.xs, self.xr, self.ys, self.yr, self.zs, self.zr = sems
        self.ls, self.lr, self.lxs, self.lxr, self.lys, self.lyr = late
        self.z, self.c, self.m = place()

    def cut(self, t, ref):
        return ref.at[pl.ds(0, HALF - EARLY), :] if t == 3 else ref

    def patch(self, ref, z=None):
        start = pl.multiple_of((self.z if z is None else z) * SIDE, SIDE)
        return ref.at[pl.ds(HALF - EARLY, EARLY), pl.ds(start, SIDE)]

    def early_z(self, k, off, d):
        z, mo = (self.z + d) % PLANES, self.m ^ off
        return remote(
            self.patch(self.rc[3].at[k, mo], z), self.rl.at[k, mo, d - 1], self.ls.at[k, off, d - 1],
            self.lr.at[k, off, d - 1], z * 2 + self.c, self.m,
        )

    def early_x(self, k, i):
        src = self.patch(self.rc[3].at[k, self.m ^ (3 if i else 1 + k)])
        return remote(
            src, self.patch(self.rx[3].at[k, i]), self.lxs.at[k, i], self.lxr.at[k, i], self.z * 2 + self.c,
            self.m ^ (1 + k),
        )

    def early_y(self, k):
        m = self.m ^ (2 - k)
        return remote(
            self.patch(self.rc[3].at[k, m]), self.patch(self.ry[3].at[k]), self.lys.at[k], self.lyr.at[k],
            self.z * 2 + self.c, m,
        )

    def early_sum(self, k):
        for i, off in enumerate((3, 1 + k, 2 - k, 0)):
            mo = self.m ^ off
            for d in range(1, PLANES):
                self.early_z(k, off, d).wait_recv()
            own = self.patch(self.rc[3].at[k, mo])
            for r in range(0, EARLY, 64):
                rows = slice(r, r + 64)
                total = own[rows, :].astype(F32) + self.rl[k, mo, 0, rows, :].astype(F32)
                total = total + self.rl[k, mo, 1, rows, :].astype(F32) + self.rl[k, mo, 2, rows, :].astype(F32)
                own[rows, :] = total.astype(BF16)
            if i < 2:
                self.early_x(k, 1 - i).start()

    def early_to_y(self, k):
        self.early_x(k, 1).wait_recv()
        add_into(self.patch(self.rc[3].at[k, self.m ^ (2 - k)]), self.patch(self.rx[3].at[k, 1]))
        self.early_y(k).start()

    def early_total(self, k):
        self.early_x(k, 0).wait_recv()
        self.early_y(k).wait_recv()
        refs = (self.rc[3].at[k, self.m], self.rx[3].at[k, 0], self.ry[3].at[k])
        a, b, c = (self.patch(r)[...].astype(F32) for r in refs)
        return a + b + c

    def early_drain(self, k):
        for off in range(4):
            for d in range(1, PLANES):
                self.early_z(k, off, d).wait_send()
        self.early_x(k, 0).wait_send()
        self.early_x(k, 1).wait_send()
        self.early_y(k).wait_send()

    def c_copy(self, t, k, off, src):
        return remote(
            src, self.rc[t].at[k, self.m ^ off], self.cs.at[t, k, off], self.cr.at[t, k, off],
            self.z * 2 + 1 - self.c, self.m,
        )

    def x_copy(self, t, k, i):
        m = self.m ^ (3 if i else 1 + k)
        return remote(
            self.cut(t, self.rc[t].at[k, m]), self.cut(t, self.rx[t].at[k, i]), self.xs.at[t, k, i], self.xr.at[t, k, i],
            self.z * 2 + self.c, self.m ^ (1 + k),
        )

    def y_copy(self, t, k):
        m = self.m ^ (2 - k)
        return remote(
            self.cut(t, self.rc[t].at[k, m]), self.cut(t, self.ry[t].at[k]), self.ys.at[t, k], self.yr.at[t, k], self.z * 2 + self.c, m
        )

    def z_copy(self, t, k, d):
        z = (self.z + d) % PLANES
        src = span(self.cut(t, self.rc[t].at[k, self.m]), KINDS[t], z * SIDE, SIDE)
        return remote(
            src, self.cut(t, self.rz[t].at[k, d - 1]), self.zs.at[t, k, d - 1], self.zr.at[t, k, d - 1], z * 2 + self.c, self.m
        )

    def to_y(self, t, k):
        self.x_copy(t, k, 1).wait_recv()
        add_into(self.cut(t, self.rc[t].at[k, self.m ^ (2 - k)]), self.cut(t, self.rx[t].at[k, 1]))
        self.y_copy(t, k).start()

    def to_z(self, t, k):
        self.x_copy(t, k, 0).wait_recv()
        add_into(self.cut(t, self.rc[t].at[k, self.m]), self.cut(t, self.rx[t].at[k, 0]))
        self.y_copy(t, k).wait_recv()
        add_into(self.cut(t, self.rc[t].at[k, self.m]), self.cut(t, self.ry[t].at[k]))
        for d in range(1, PLANES):
            self.z_copy(t, k, d).start()

    def total(self, t, k):
        for d in range(1, PLANES):
            self.z_copy(t, k, d).wait_recv()
        own = span(self.cut(t, self.rc[t].at[k, self.m]), KINDS[t], self.z * SIDE, SIDE)[...].astype(F32)
        a, b, c = (self.cut(t, self.rz[t].at[k, i])[...].astype(F32) for i in range(3))
        return own + a + b + c

    def drain(self, t, k):
        self.x_copy(t, k, 0).wait_send()
        self.x_copy(t, k, 1).wait_send()
        self.y_copy(t, k).wait_send()
        for d in range(1, PLANES):
            self.z_copy(t, k, d).wait_send()


def backward_kernel(
    x_hbm, wq_hbm, wo_hbm, wu_hbm, wd_hbm, qkv_hbm, p_hbm, mixed_hbm, lowh_hbm, n1_hbm, rs_hbm, act_hbm, gp_hbm,
    dpre_hbm, dv, gains,
    ig_hbm, oq, oo, ou, od, ov,
    *rest,
):
    rc, rx, ry, rz = rest[0:4], rest[4:8], rest[8:12], rest[12:16]
    (dbr, dh, low, wdj, wuj, ag, gd, gu, dmix, qkvj, dproj, nst, rst, rv, gv, sums, ubg, qvg, rw, gw) = rest[16:36]
    fold = Fold(rc, rx, ry, rz, rest[44], rest[36:44], rest[45:51])
    vs, vr, us, ur, lsem, psem, ssem, nsem, isem, xsem = rest[51:]
    z, c, m = place()
    other = 1 - c
    mine, theirs = aligned(c * HALF, HALF), aligned(other * HALF, HALF)

    def turn(idx):
        k, p = idx % 2, idx // 2
        off = jnp.where(p == 0, 3, jnp.where(p == 1, 1 + k, jnp.where(p == 2, 2 - k, 0)))
        return k, p, off

    def down_loads(idx):
        k, _, off = turn(idx)
        mo, slot = m ^ off, idx % 2
        j = k * 4 + mo
        pairs = ((wd_hbm.at[k, mo], wdj.at[slot]), (act_hbm.at[j], ag.at[slot, 0]), (gp_hbm.at[j], ag.at[slot, 1]))
        return [pltpu.make_async_copy(a, b, lsem.at[slot, i]) for i, (a, b) in enumerate(pairs)]

    def up_load(idx):
        k, _, off = turn(idx)
        return pltpu.make_async_copy(wu_hbm.at[k, m ^ off], wuj.at[idx % 2], lsem.at[idx % 2, 3])

    greet_start()
    dp_copy = pltpu.make_async_copy(dpre_hbm, dh, ssem.at[0])
    dp_copy.start()
    for cp in down_loads(0):
        cp.start()
    lh_copy = pltpu.make_async_copy(lowh_hbm, low, ssem.at[1])
    mx_copies = [
        pltpu.make_async_copy(mixed_hbm.at[:, pl.ds(h * L, L)], ag.at[1, h], ssem.at[2 + h]) for h in range(2)
    ]
    sums[...] = gains[...]
    dp_copy.wait()

    def cast(i, carry):
        rows = aligned(i * 128, 128)
        dbr[rows, :] = dh[rows, :].astype(BF16)
        return carry

    lax.fori_loop(0, 8, cast, 0)

    def settle_ffn(t, idx, own):
        k, p, off = turn(idx)
        mo = m ^ off
        fold.c_copy(t, k, off, gd.at[idx % 2]).wait()
        add_into(rc[t].at[k, mo], own.at[idx % 2])
        if t == 3:
            for d in range(1, PLANES):
                fold.early_z(k, off, d).start()

        @pl.when(p == 0)
        def _():
            fold.x_copy(t, k, 1).start()

        @pl.when(p == 1)
        def _():
            fold.x_copy(t, k, 0).start()

    def down_step(idx, carry):
        k, p, off = turn(idx)
        mo, slot = m ^ off, idx % 2
        for cp in down_loads(idx):
            cp.wait()

        @pl.when(idx < 7)
        def _():
            for cp in down_loads(idx + 1):
                cp.start()

        @pl.when(idx == 3)
        def _():
            lh_copy.start()
            up_load(0).start()
            up_load(1).start()

        total = jnp.zeros((1, HALF), F32)
        for r in range(2):
            rows = slice(r * L, r * L + L)
            d = (mm_nt(dbr[rows, :], wdj[slot]) * ag[slot, 1, rows, :].astype(F32)).astype(BF16)
            dproj[idx, rows, :] = d
            total = total + jnp.sum(d.astype(F32), axis=0, keepdims=True)
        ubg[k * 4 + mo] = total
        gd[slot] = mm_tn(ag[slot, 0], dbr[:, theirs]).astype(BF16)

        @pl.when(idx == 0)
        def _():
            greet_end()

        fold.c_copy(3, k, off, gd.at[slot]).start()
        gu[slot] = mm_tn(ag[slot, 0], dbr[:, mine]).astype(BF16)

        @pl.when(idx >= 1)
        def _():
            settle_ffn(3, idx - 1, gu)

        return carry

    lax.fori_loop(0, 8, down_step, 0)
    for cp in mx_copies:
        cp.start()
    lh_copy.wait()
    for k in range(2):
        fold.to_y(3, k)

    def up_step(idx, carry):
        k, p, off = turn(idx)
        slot = idx % 2
        gd[slot] = mm_tn(low[:, theirs], dproj[idx]).astype(BF16)
        fold.c_copy(2, k, off, gd.at[slot]).start()
        gu[slot] = mm_tn(low[:, mine], dproj[idx]).astype(BF16)
        up_load(idx).wait()
        for r in range(2):
            for h in range(2):
                rows, cols = slice(r * L, r * L + L), slice(h * HALF, h * HALF + HALF)
                dh[rows, cols] += mm_nt(dproj[idx, rows, :], wuj[slot, cols, :])

        @pl.when(idx < 6)
        def _():
            up_load(idx + 2).start()

        @pl.when(idx == 0)
        def _():
            settle_ffn(3, 7, gu)

        @pl.when(idx == 5)
        def _():
            fold.to_z(3, 1)

        @pl.when(idx == 6)
        def _():
            fold.to_z(3, 0)

        @pl.when(idx == 7)
        def _():
            fold.early_sum(0)
            fold.early_sum(1)

        @pl.when(idx >= 1)
        def _():
            settle_ffn(2, idx - 1, gu)

        return carry

    lax.fori_loop(0, 8, up_step, 0)
    fold.to_y(2, 0)
    fold.to_y(2, 1)

    def norm_loads(i):
        rows, slot = aligned(i * 256, 256), i % 2
        return (
            pltpu.make_async_copy(n1_hbm.at[rows, :], nst.at[slot], nsem.at[slot, 0]),
            pltpu.make_async_copy(rs_hbm.at[rows, :], rst.at[slot], nsem.at[slot, 1]),
        )

    for cp in norm_loads(0):
        cp.start()
    wo_copies = [
        pltpu.make_async_copy(
            wo_hbm.at[j // 4, j % 4], wdj.at[j // 4, pl.ds((j % 4) * 128, 128), :], lsem.at[j // 4, j % 4]
        )
        for j in range(8)
    ]
    for cp in wo_copies:
        cp.start()
    x_copies = column_copies(x_hbm, low, xsem, False)
    for cp in x_copies:
        cp.start()

    def head_turn(idx):
        k = jnp.where(idx == 1, 1, jnp.where(idx == 4, 1, jnp.where(idx >= 6, 1, 0)))
        p = jnp.where(idx < 2, 0, jnp.where(idx == 2, 1, jnp.where(idx == 4, 1, jnp.where(idx == 3, 2, jnp.where(idx == 6, 2, 3)))))
        return k, p, jnp.where(p == 0, 3, jnp.where(p == 1, 1 + k, jnp.where(p == 2, 2 - k, 0)))

    def attn_loads(idx):
        k, _, off = head_turn(idx)
        j, slot = k * 4 + (m ^ off), idx % 2
        copies = [pltpu.make_async_copy(qkv_hbm.at[j], qkvj.at[slot], psem.at[slot, 4])]
        for s in range(2):
            for e in range(2):
                copies.append(
                    pltpu.make_async_copy(
                        p_hbm.at[j, s, e], ag.at[slot, s, pl.ds(e * L, L), :], psem.at[slot, 2 * s + e]
                    )
                )
        return copies

    for cp in attn_loads(0):
        cp.start()

    def first_back(i, carry):
        rows, slot = aligned(i * 256, 256), i % 2

        @pl.when(i < 3)
        def _():
            for cp in norm_loads(i + 1):
                cp.start()

        for cp in norm_loads(i):
            cp.wait()
        grad, n = dh[rows, :], nst[slot]
        g = grad * dv[1:2]
        inv = rst[slot][:, 0:1]
        back = inv * (g - row_mean(g) - n * row_mean(g * n))
        dh[rows, :] = back
        dbr[rows, :] = back.astype(BF16)
        sums[0:1, :] += jnp.sum(back, axis=0, keepdims=True)
        sums[1:2, :] += jnp.sum(grad * n, axis=0, keepdims=True)
        sums[2:3, :] += jnp.sum(grad, axis=0, keepdims=True)
        return carry

    lax.fori_loop(0, 4, first_back, 0)
    settle_ffn(2, 7, gu)
    fold.early_to_y(0)
    fold.early_to_y(1)
    for cp in mx_copies:
        cp.wait()
    for h in range(2):
        rows = slice(h * L, h * L + L)
        wuj[0, rows, :] = mm_tn(ag[1, h], dbr[:, theirs]).astype(BF16)
    for k in range(2):
        for off in range(4):
            src = wuj.at[0, aligned((k * 4 + (m ^ off)) * 128, 128), :]
            fold.c_copy(1, k, off, src).start()
    for cp in wo_copies:
        cp.wait()
    for h in range(2):
        rows = slice(h * L, h * L + L)
        for q in range(2):
            dmix[rows, q * L:q * L + L] = mm_nt(dbr[rows, :], wdj[q]).astype(BF16)
    for h in range(2):
        rows = slice(h * L, h * L + L)
        wuj[1, rows, :] = mm_tn(ag[1, h], dbr[:, mine]).astype(BF16)
    for k in range(2):
        for off in (3, 1 + k, 2 - k, 0):
            src = wuj.at[0, aligned((k * 4 + (m ^ off)) * 128, 128), :]
            fold.c_copy(1, k, off, src).wait()
            add_into(rc[1].at[k, m ^ off], wuj.at[1, aligned((k * 4 + (m ^ off)) * 128, 128), :])
            if off == 3:
                fold.x_copy(1, k, 1).start()
            elif off == 1 + k:
                fold.x_copy(1, k, 0).start()
    for cp in x_copies:
        cp.wait()

    def piece(idx):
        return gu.at[idx % 2, :, pl.ds(0, 384)]

    def attend(idx, s):
        k, _, off = head_turn(idx)
        mo, slot = m ^ off, idx % 2
        j = k * 4 + mo
        rows = slice(s * L, s * L + L)
        dout = dmix[rows, aligned(j * 128, 128)]
        queries, keys, values = (qkvj[slot, rows, i * 128:i * 128 + 128] for i in range(3))
        dq = dk = dval = None
        for e in range(2):
            probs = ag[slot, s, e * L:e * L + L, :]
            p32 = probs.astype(F32)
            t = p32 * mm_nt(dout, lane_half(values, e))
            ds = (t - p32 * jnp.sum(t, axis=1, keepdims=True)).astype(BF16)
            parts = (mm(ds, lane_half(keys, e)), mm_tn(ds, lane_half(queries, e)), mm_tn(probs, lane_half(dout, e)))
            dq, dk, dval = parts if e == 0 else (dq + parts[0], dk + parts[1], dval + parts[2])
        scale = DH ** (-0.5)
        out = jnp.concatenate([dq * scale, dk * scale, dval], axis=1).astype(BF16)
        dproj[idx, rows, 0:384] = out
        return jnp.sum(out.astype(F32), axis=0, keepdims=True)

    def settle(idx, hold=False):
        k, p, off = head_turn(idx)
        mo = m ^ off
        fold.c_copy(0, k, off, piece(idx)).wait()
        rc[0][k, mo] = (mm_tn(low[:, mine], dproj[idx, :, 0:384]) + rc[0][k, mo].astype(F32)).astype(BF16)

        @pl.when(p == 0)
        def _():
            fold.x_copy(0, k, 1).start()

        @pl.when(p == 1)
        def _():
            fold.x_copy(0, k, 0).start()

        @pl.when(p == 2)
        def _():
            fold.to_y(0, k)

        if not hold:

            @pl.when(p == 3)
            def _():
                fold.to_z(0, k)

    def heads(idx, carry):
        k, p, off = head_turn(idx)
        j = k * 4 + (m ^ off)
        for cp in attn_loads(idx):
            cp.wait()

        @pl.when(idx < 7)
        def _():
            for cp in attn_loads(idx + 1):
                cp.start()

        qvg[j] = attend(idx, 0) + attend(idx, 1)

        @pl.when(idx >= 1)
        def _():
            settle(idx - 1)

        gu[idx % 2, :, 0:384] = mm_tn(low[:, theirs], dproj[idx, :, 0:384]).astype(BF16)
        fold.c_copy(0, k, off, piece(idx)).start()

        @pl.when(idx == 1)
        def _():
            fold.to_z(2, 1)
            fold.to_y(1, 0)
            fold.to_y(1, 1)

        @pl.when(idx == 2)
        def _():
            fold.to_z(2, 0)

        @pl.when(idx == 4)
        def _():
            fold.to_z(1, 0)
            fold.to_z(1, 1)

        return carry

    for f in range(8):
        p = (f % 2) * 4 + f // 2
        ub = ubg[p]
        pad = jnp.zeros((4, 128), F32)
        tile = jnp.concatenate(
            [sums[:, p * SIDE:(p + 1) * SIDE]] + [ub[:, i * 128:i * 128 + 128] for i in range(4)] + [pad], axis=0
        ).astype(BF16)
        for mo in range(4):
            gv[mo * 8 + f] = tile
    vcopy = swap_vectors(gv, rv, us, ur, True)
    run_31(lambda d: vcopy(d).start())
    me = m * 8 + z * 2 + c
    rv[me] = gv[me]
    lax.fori_loop(0, 8, heads, 0)

    def wq_load(idx):
        k, _, off = head_turn(idx)
        return pltpu.make_async_copy(wq_hbm.at[k, m ^ off], qkvj.at[idx % 2], psem.at[idx % 2, 4])

    wq_load(0).start()
    wq_load(1).start()
    settle(7, True)
    for f in range(8):
        for mo in range(4):
            kk, e, part = f // 4, (f // 2) % 2, f % 2
            qv = qvg[kk * 4 + mo][:, part * 256 + e * 64:part * 256 + e * 64 + 64]
            gw[mo * 8 + f] = jnp.concatenate([qv, qv], axis=1)
    wcopy = swap_vectors(gw, rw, vs, vr, True)
    run_31(lambda d: wcopy(d).start())
    rw[me] = gw[me]

    def pull(idx, carry):
        slot = idx % 2
        wq_load(idx).wait()
        for r in range(2):
            for h in range(2):
                rows, cols = slice(r * L, r * L + L), slice(h * HALF, h * HALF + HALF)
                dh[rows, cols] += mm_nt(dproj[idx, rows, 0:384], qkvj[slot, cols, :])

        @pl.when(idx < 6)
        def _():
            wq_load(idx + 2).start()

        return carry

    lax.fori_loop(0, 3, pull, 0)
    fold.to_z(0, 1)
    lax.fori_loop(3, 8, pull, 0)
    i_copies = column_copies(ig_hbm, dh, isem, True)
    for cp in i_copies:
        cp.start()
    run_31(lambda d: vcopy(d).wait())
    run_31(lambda d: wcopy(d).wait())

    def gather_sum(i, acc):
        return acc[0] + rv[i].astype(F32), acc[1] + rw[i]

    wide, narrow = lax.fori_loop(0, 32, gather_sum, (jnp.zeros((16, 128), F32), jnp.zeros((1, 128), F32)))
    ov[...] = wide
    ov[12:13, :] = narrow
    for k in range(2):
        od[k * HALF:k * HALF + HALF - EARLY, :] = fold.total(3, k)
        od[k * HALF + HALF - EARLY:k * HALF + HALF, :] = fold.early_total(k)
        ou[:, k * HALF:k * HALF + HALF] = fold.total(2, k)
        oo[k * 128:k * 128 + 128, :] = fold.total(1, k)
    for k in range(2):
        t = fold.total(0, k)
        parts = [t[:, i * 128 + e * 64:i * 128 + e * 64 + 64] for e in range(2) for i in range(3)]
        oq[:, k * 384:k * 384 + 384] = jnp.concatenate(parts, axis=1)
    for cp in i_copies:
        cp.wait()
    for k in range(2):
        for t in range(4):
            fold.drain(t, k)
        fold.early_drain(k)


def export_kernel(y, ig, oq, oo, ou, od, ov, *rest):
    outs, bufs, sems = rest[:14], rest[14:20], rest[20]
    pairs = list(zip((y, ig, oq, oo, ou, od), bufs, (outs[0], outs[1], outs[2], outs[4], outs[8], outs[10])))
    pieces = []
    for n, (src, buf, dst) in enumerate(pairs):
        for h in range(2):
            at = (pl.ds(h, 1),) if n < 2 else (pl.ds(h * (src.shape[0] // 2), src.shape[0] // 2),)
            pieces.append((
                pltpu.make_async_copy(src.at[at], buf.at[at], sems.at[0, n, h]),
                pltpu.make_async_copy(buf.at[at], dst.at[at], sems.at[1, n, h]),
            ))
    for inward, _ in pieces:
        inward.start()
    for n, r in ((5, 0), (6, 1), (7, 2), (11, 3), (12, 4), (13, 5)):
        outs[n][...] = ov[r]
    outs[3][...] = ov[12, :64]
    for r in range(4):
        outs[9][r * 128:r * 128 + 128] = ov[8 + r]
    for inward, outward in pieces:
        inward.wait()
        outward.start()
    for _, outward in pieces:
        outward.wait()


def export(y, results):
    vm = pl.BlockSpec(memory_space=pltpu.VMEM)
    anywhere = pl.BlockSpec(memory_space=pl.ANY)
    shape = jax.ShapeDtypeStruct
    big = [shape(v.shape, v.dtype) for v in (y,) + tuple(results[:5])]
    vec = lambda n: shape((n,), F32)
    return pl.pallas_call(
        export_kernel,
        out_shape=[
            big[0], big[1], big[2], vec(64), big[3], vec(128), vec(128), vec(128), big[4], vec(512), big[5], vec(128),
            vec(128), vec(128),
        ],
        in_specs=[anywhere] * 6 + [vm],
        out_specs=[anywhere if i in (0, 1, 2, 4, 8, 10) else vm for i in range(14)],
        scratch_shapes=[pltpu.VMEM(b.shape, b.dtype) for b in big] + [pltpu.SemaphoreType.DMA((2, 6, 2))],
        compiler_params=pltpu.CompilerParams(vmem_limit_bytes=67000000),
    )(y, *results)


def backward(inputs, weights, saved, dv, gains):
    vm = pl.BlockSpec(memory_space=pltpu.VMEM)
    anywhere = pl.BlockSpec(memory_space=pl.ANY)
    shape = jax.ShapeDtypeStruct
    dma = pltpu.SemaphoreType.DMA
    v = pltpu.VMEM
    bufs, sems = fold_scratch()
    scratch = bufs + [
        v((1024, D), BF16), v((1024, D), F32), v((1024, D), BF16), v((2, HALF, D), BF16), v((2, D, HALF), BF16),
        v((2, 2, 1024, HALF), BF16), v((2, HALF, HALF), BF16), v((2, HALF, HALF), BF16),
        v((1024, D), BF16), v((2, 1024, 384), BF16), v((8, 1024, HALF), BF16),
        v((2, 256, D), F32), v((2, 256, 128), F32), v((32, 16, 128), BF16), v((32, 16, 128), BF16), v((8, D), F32),
        v((8, 1, HALF), F32), v((8, 1, 384), F32), v((32, 1, 128), F32), v((32, 1, 128), F32),
    ] + sems + [
        v((2, 4, 3, EARLY, SIDE), BF16), dma((2, 4, 3)), dma((2, 4, 3)), dma((2, 2)), dma((2, 2)), dma((2,)), dma((2,)),
        dma((32,)), dma((32,)), dma((32,)), dma((32,)), dma((2, 4)), dma((2, 5)), dma((4,)), dma((2, 2)), dma((2, 8)), dma((2, 8)),
    ]
    return pl.pallas_call(
        backward_kernel,
        out_shape=[
            shape((2, L, D), F32), shape((128, 768), F32), shape((256, 128), F32), shape((128, 1024), F32),
            shape((1024, 128), F32), shape((16, 128), F32),
        ],
        in_specs=[anywhere] * 14 + [vm, vm],
        out_specs=[anywhere] + [vm] * 5,
        scratch_shapes=scratch,
        compiler_params=pltpu.CompilerParams(collective_id=1, has_side_effects=True, vmem_limit_bytes=67000000),
    )(inputs, *weights, *saved, dv, gains)

def fast_body(
    inputs, lengths, qkv_weight, qv_bias, out_weight, out_bias, norm1_gain, norm1_bias, up_weight, up_bias,
    down_weight, down_bias, norm2_gain, norm2_bias, cotangent,
):
    row = lambda v: v.reshape(1, 128)
    results = forward(
        lengths, inputs, cotangent, (qkv_weight, out_weight, up_weight, down_weight),
        (row(out_bias), row(norm1_gain), row(norm1_bias), row(down_bias), row(norm2_gain), row(norm2_bias),
         up_bias.reshape(4, 128), qv_bias.reshape(1, 64)),
    )
    return tuple(export(results[0], backward(inputs, results[1:5], results[5:14], results[14], results[15])))


def solution(mesh):
    placed = (
        P(None, ("fsdp", "mp"), None),
        P(None, "fsdp"),
        P("fsdp", "mp"),
        P(("mp", "fsdp")),
        P("mp", "fsdp"),
        P("fsdp"),
        P("fsdp"),
        P("fsdp"),
        P("fsdp", "mp"),
        P("fsdp"),
        P("mp", "fsdp"),
        P("fsdp"),
        P("fsdp"),
        P("fsdp"),
        P(None, ("fsdp", "mp"), None),
    )
    blocks_fit = mesh.shape["fsdp"] == 8 and mesh.shape["mp"] == 4
    return jax.shard_map(
        fast_body if blocks_fit else generic_body,
        mesh=mesh,
        in_specs=placed,
        out_specs=(
            P(None, ("fsdp", "mp"), None),
            P(None, ("fsdp", "mp"), None),
            P("fsdp", "mp"),
            P(("mp", "fsdp")),
            P("mp", "fsdp"),
            P("fsdp"),
            P("fsdp"),
            P("fsdp"),
            P("fsdp", "mp"),
            P("fsdp"),
            P("mp", "fsdp"),
            P("fsdp"),
            P("fsdp"),
            P("fsdp"),
        ),
        check_vma=False,
    )
```
